32 devices in a mesh: grp: 4 (over z), gx: 4 (over y, x), gy: 2 (over core).
Axes of the slice: x: 2, y: 2, z: 4, core: 2. Of those that a mesh axis runs over, the one named last changes fastest.
Arguments:
- fluid_temp: float32 [64, 256, 1024], P('gx', 'gy', 'grp'), may hold values from -6 to 6
- active: int32 [64, 256, 1024], P('gx', 'gy', 'grp'), may hold values 0 or 1
- fin_temp: float32 [256, 128, 512], P('grp', 'gx', 'gy'), may hold values from -6 to 6
- fin_source: float32 [256, 128, 512], P('grp', 'gx', 'gy'), may hold values from -6 to 6
- wall_owner: int32 [4, 2, 2048, 1], P('gx', 'gy'), may hold values from 0 to 3, as said below
- wall_target: int32 [4, 2, 2048], P('gx', 'gy'), may hold values from 0 to 8191, as said below
Outputs:
- fluid_new: float32 [64, 256, 1024], P('gx', 'gy', 'grp')
- fin_new: float32 [256, 128, 512], P('grp', 'gx', 'gy')
The draws below stay inside these ranges and needn't reach their ends.
Inputs may be any that keep to these rules, and one draw needn't show every extreme that they name: `wall_owner`: among the 2048 wall cells of one column block (a, b), exactly 1024 name the owner a and at most 1024 name any one owner; in every draw one owner is named by exactly 1024 wall cells of every column block. `wall_target`: wall cell w = i * 128 + j names a root cell (2 * i + di) * 256 + 2 * j + dj of the 2 x 2 patch beneath it, di and dj being 0 or 1; the first wall cell of a block names its patch's first root cell, the last one its patch's last.
All inputs are finite; a program needn't handle non-finite values. No bound on the sum of `active` on one device may be relied on, other than what follows from the above.
Results may differ from the reference program's by a relative error of at most 0.00002.
Values sent between devices are 32-bit elements; how exact they have to be, the bound alone decides.
No kernel may reach another device: no remote copies, remote signals or barrier semaphores. Data moves between devices by JAX's collectives and lax.ppermute only.
A program may use at most 64 MiB of HBM per device.

```python
import jax
import jax.numpy as jnp
from jax import lax

CX = 16
CY = 128
FW = 32
FH = 256
NX = 64
NY = 256
NZ = 1024
FZG = 256
FWG = 128
FHG = 512
CAP = 1024
N_GX = 4
N_GY = 2


def owner_block(block_key, home, star):
    wall_cells = CX * CY
    away_count = (N_GX - 1) * CAP
    first_key, second_key = jax.random.split(block_key)
    order = jax.random.permutation(first_key, wall_cells)
    slot_scores = jax.random.permutation(second_key, away_count)
    slot_owner = (home + jnp.arange(away_count, dtype=jnp.int32) // CAP + 1) % N_GX
    priority = jnp.where(slot_owner == star, 0, away_count) + slot_scores
    slot_order = jnp.argsort(priority, stable=True)
    ranks = jnp.arange(wall_cells, dtype=jnp.int32)
    picked = slot_order[jnp.clip(ranks - CAP, 0, away_count - 1)]
    by_rank = jnp.where(ranks < CAP, home, slot_owner[picked]).astype(jnp.int32)
    return jnp.zeros((wall_cells,), jnp.int32).at[order].set(by_rank)


def draw_wall_owner(key, part):
    base = jax.random.fold_in(key, 11)
    star = jax.random.randint(jax.random.fold_in(base, 7), (), 0, N_GX).astype(jnp.int32)
    block_ids = jnp.arange(N_GX * N_GY, dtype=jnp.int32)
    homes = block_ids // N_GY
    keys = jax.vmap(lambda ident: jax.random.fold_in(base, ident))(block_ids)
    owners = jax.vmap(lambda block_key, home: owner_block(block_key, home, star))(keys, homes)
    return owners.reshape(N_GX, N_GY, CX * CY, 1)


def draw_wall_target(key, part):
    base = jax.random.fold_in(key, 23)
    wall_cells = CX * CY
    shifts = jax.random.randint(base, (N_GX, N_GY, wall_cells, 2), 0, 2).astype(jnp.int32)
    cells = jnp.arange(wall_cells, dtype=jnp.int32)
    row_shift = jnp.where(cells == 0, 0, jnp.where(cells == wall_cells - 1, 1, shifts[..., 0]))
    col_shift = jnp.where(cells == 0, 0, jnp.where(cells == wall_cells - 1, 1, shifts[..., 1]))
    rows = cells // CY
    columns = cells % CY
    return ((2 * rows + row_shift) * FH + 2 * columns + col_shift).astype(jnp.int32)


def plant(array, own_key, least, high):
    dims = array.shape
    index_at = [jax.random.randint(jax.random.fold_in(own_key, axis), (), 0, dims[axis]) for axis in range(len(dims))]
    array = array.at[tuple(index_at)].set(least)
    longest = dims.index(max(dims))
    index_at[longest] = (index_at[longest] + 1) % dims[longest]
    return array.at[tuple(index_at)].set(high)


def block_scale(stream_key, shape, cuts, smallest, largest):
    def one(axis_at, blocks):
        draws = jax.random.uniform(jax.random.fold_in(jax.random.fold_in(stream_key, 6), axis_at), (blocks,), jnp.float32, smallest / len(cuts), largest / len(cuts))
        return jnp.repeat(jnp.exp(draws), shape[axis_at] // blocks).reshape((-1,) + (1,) * (len(shape) - axis_at - 1))

    level = one(*cuts[0])
    for cut in cuts[1:]:
        level = level * one(*cut)
    return level


def centred(key, extent, deviation, most, cuts=(), kind=jnp.bfloat16):
    factor_of = block_scale(key, extent, cuts, -0.22, 0.18) if cuts else 1.0
    drawn = jax.random.normal(key, extent, jnp.float32) * deviation * factor_of
    return jnp.minimum(jnp.maximum(drawn, -most), most).astype(kind)


def setup_inputs(seed: int = 0) -> dict:
    streams_of = jax.random.split(jax.random.key(seed), 7)
    return {
        "fluid_temp": centred(streams_of[0], (NX, NY, NZ), 1.0, 6.0, ((0, 4), (1, 2), (2, 4)), jnp.float32),
        "active": plant((jax.random.randint(streams_of[1], (NX, NY, NZ), 0, 8) < 7).astype(jnp.int32), jax.random.fold_in(streams_of[1], 1), 0, 1),
        "fin_temp": centred(streams_of[2], (FZG, FWG, FHG), 1.0, 6.0, ((0, 4), (1, 4), (2, 2)), jnp.float32),
        "fin_source": centred(streams_of[3], (FZG, FWG, FHG), 1.0, 6.0, ((0, 4), (1, 4), (2, 2)), jnp.float32),
        "wall_owner": draw_wall_owner(jax.random.fold_in(streams_of[6], 71), 0),
        "wall_target": draw_wall_target(jax.random.fold_in(streams_of[6], 71), 0),
    }


FLUID_DIFFUSION = 1.0
FIN_CONDUCTION = 1.0
HEAT_COEF = 1.0


def six_sum(padded):
    return (padded[2:, 1:-1, 1:-1] + padded[:-2, 1:-1, 1:-1] + padded[1:-1, 2:, 1:-1]
            + padded[1:-1, :-2, 1:-1] + padded[1:-1, 1:-1, 2:] + padded[1:-1, 1:-1, :-2])


def fin_image(field):
    padded = jnp.pad(field, 1)
    return (1.0 + 6.0 * FIN_CONDUCTION) * field - FIN_CONDUCTION * six_sum(padded)


def reference(fluid_temp, active, fin_temp, fin_source, wall_owner, wall_target):
    owners = wall_owner[..., 0]
    column_b = lax.broadcasted_iota(jnp.int32, owners.shape, 1)
    surf_first = owners * FW + wall_target // FH
    surf_second = column_b * FH + wall_target % FH
    surface_index = (surf_first * FHG + surf_second).astype(jnp.int32)
    surface = fin_temp[0].reshape(-1)
    fin_wall = surface[surface_index]
    bottom = fluid_temp[:, :, 0].reshape(N_GX, CX, N_GY, CY).transpose(0, 2, 1, 3).reshape(N_GX, N_GY, CX * CY)
    heat_flux = HEAT_COEF * (bottom - fin_wall)
    deposit = jax.ops.segment_sum(heat_flux.reshape(-1), surface_index.reshape(-1), num_segments=FWG * FHG)
    fin_rhs = fin_temp + fin_source
    fin_rhs = fin_rhs.at[0].add(deposit.reshape(FWG, FHG))
    diag = 1.0 + 6.0 * FIN_CONDUCTION
    spectral = 6.0 * FIN_CONDUCTION / diag
    omega = 1.0 / (1.0 - spectral * spectral / 2.0)
    first_state = fin_temp + (fin_rhs - fin_image(fin_temp)) / diag
    fin_new = omega * (first_state + (fin_rhs - fin_image(first_state)) / diag - fin_temp) + fin_temp

    ghost = fin_wall.reshape(N_GX, N_GY, CX, CY).transpose(0, 2, 1, 3).reshape(NX, NY)
    shape = fluid_temp.shape
    colour = (lax.broadcasted_iota(jnp.int32, shape, 0) + lax.broadcasted_iota(jnp.int32, shape, 1)
              + lax.broadcasted_iota(jnp.int32, shape, 2)) % 2
    red_mask = (colour == 0) & (active == 1)
    black_mask = (colour == 1) & (active == 1)

    def half_sweep(field, update_mask):
        padded = jnp.pad(field, 1)
        padded = padded.at[1:-1, 1:-1, 0].set(ghost)
        updated = (fluid_temp + FLUID_DIFFUSION * six_sum(padded)) / (1.0 + 6.0 * FLUID_DIFFUSION)
        return jnp.where(update_mask, updated, field)

    red_temp = half_sweep(fluid_temp, red_mask)
    fluid_new = half_sweep(red_temp, black_mask)
    return fluid_new, fin_new
```

```python
import jax
import jax.numpy as jnp
from jax import lax
from jax.experimental import pallas as pl
from jax.experimental.pallas import tpu as pltpu
from jax.sharding import PartitionSpec as P

FLUID_DIFFUSION = 1.0
FIN_CONDUCTION = 1.0
HEAT_COEF = 1.0
DIAG = 1.0 + 6.0 * FIN_CONDUCTION
SPECTRAL = 6.0 * FIN_CONDUCTION / DIAG
OMEGA = 1.0 / (1.0 - SPECTRAL * SPECTRAL / 2.0)
FLUID_SCALE = 1.0 / (1.0 + 6.0 * FLUID_DIFFUSION)
LANES = 128
PAD = 8
ROWS = 32
HIGHEST = lax.Precision.HIGHEST


def iota(shape, axis):
    return lax.broadcasted_iota(jnp.int32, shape, axis)


def tiles(value):
    return [value[:, k : k + LANES] for k in range(0, value.shape[1], LANES)]


def lane_neighbours(block, low, high):
    parts = tiles(block)
    lane = iota(parts[0].shape, 1)
    down = [pltpu.roll(part, 1, axis=1) for part in parts]
    up = [pltpu.roll(part, LANES - 1, axis=1) for part in parts]
    below = [jnp.where(lane == 0, a, b) for a, b in zip([low] + down[:-1], down)]
    above = [jnp.where(lane == LANES - 1, a, b) for a, b in zip(up[1:] + [high], up)]
    return jnp.concatenate([a + b for a, b in zip(below, above)], axis=1)


def interleave_matrix(count):
    row = iota((count, count), 0)
    col = iota((count, count), 1)
    half = count // 2
    source = jnp.where(col < half, 2 * col, 2 * (col - half) + 1)
    return (row == source).astype(jnp.float32)


def dot(a, b, contract):
    return lax.dot_general(
        a, b, (contract, ((), ())), precision=HIGHEST, preferred_element_type=jnp.float32
    )


def checker_pack(plane, parity):
    rows = plane.shape[0] // 2
    top = plane[:rows]
    bottom = plane[rows:]
    colour = (iota(top.shape, 0) + iota(top.shape, 1)) & 1
    return jnp.where(colour == parity, top, pltpu.roll(bottom, 1, axis=1))


def lane_faces(fluid, cells, rows):
    width = fluid.shape[2]
    low = jnp.zeros((rows, LANES), jnp.float32)
    high = low
    lane = iota((rows, LANES), 1)
    for i in range(cells):
        here = lane == i
        low = jnp.where(here, fluid[i + 1, PAD : PAD + rows, 0:1], low)
        high = jnp.where(here, fluid[i + 1, PAD : PAD + rows, width - 1 : width], high)
    return low.T[:cells], high.T[:cells]


def pack_faces(fluid, fin, colour, gxf, gxb, grpf, grpb, gyx, gy, dims):
    cells, rows, width, depth, fin_rows, fin_width = dims
    half = rows // 2
    inner = pl.ds(PAD, rows)
    gxf[0:half, :] = checker_pack(fluid[cells, inner, :], (colour + cells - 1) % 2)
    gxb[0:half, :] = checker_pack(fluid[1, inner, :], colour)
    low, high = lane_faces(fluid, cells, rows)
    grpf[0:cells, 0:LANES] = high
    grpb[0:cells, 0:LANES] = low
    grpf[cells : cells + fin_rows, :] = fin[depth, PAD : PAD + fin_rows, :]
    grpb[cells : cells + fin_rows, :] = fin[1, PAD : PAD + fin_rows, :]
    edge = PAD + (1 - gy) * (rows - 1)
    for i in range(cells):
        gyx[i : i + 1, :] = fluid[i + 1, pl.ds(edge, 1), :]
    lane = iota((fin_rows, LANES), 1)

    def column(d, kept):
        gxf[pl.ds(half + d, 1), :] = fin[d + 1, PAD + fin_rows - 1 : PAD + fin_rows, :]
        gxb[pl.ds(half + d, 1), :] = fin[d + 1, PAD : PAD + 1, :]
        first = fin[d + 1, PAD : PAD + fin_rows, 0:LANES]
        last = fin[d + 1, PAD : PAD + fin_rows, fin_width - LANES : fin_width]
        edge_tile = jnp.where(gy == 0, pltpu.roll(last, 1, axis=1), first)
        return jnp.where(lane == d, pltpu.roll(edge_tile, d, axis=1), kept)

    gyx[cells : cells + fin_rows, 0:LANES] = lax.fori_loop(
        0, depth, column, jnp.zeros((fin_rows, LANES), jnp.float32)
    )
    return low


def unpack_halos(fluid, fin, zlow, zhigh, hlow, hhigh, prev, nxt, below, above, side,
                 low_face, gy, prev_on, next_on, dims):
    cells, rows, width, depth, fin_rows, fin_width = dims
    half = rows // 2
    for plane, ref, on in ((0, prev, prev_on), (cells + 1, nxt, next_on)):
        packed = ref[0:half, :] * on
        fluid[plane, PAD : PAD + half, :] = packed
        fluid[plane, PAD + half : PAD + rows, :] = pltpu.roll(packed, width - 1, axis=1)
    low_on = jnp.where(gy == 0, 0.0, 1.0)
    high_on = 1.0 - low_on
    for i in range(cells):
        line = side[i : i + 1, :]
        fluid[i + 1, PAD - 1 : PAD, :] = line * low_on
        fluid[i + 1, PAD + rows : PAD + rows + 1, :] = line * high_on
    blank = jnp.zeros((LANES - cells, rows), jnp.float32)
    zlow[...] = jnp.concatenate([low_face, blank], axis=0).T
    zhigh[...] = jnp.concatenate([above[0:cells, 0:LANES], blank], axis=0).T
    fin[0, PAD : PAD + fin_rows, :] = below[cells : cells + fin_rows, :]
    fin[depth + 1, PAD : PAD + fin_rows, :] = above[cells : cells + fin_rows, :]
    columns = side[cells : cells + fin_rows, 0:LANES]
    hlow[...] = columns * low_on
    hhigh[...] = columns * high_on

    def line_of(d, carry):
        fin[d + 1, PAD - 1 : PAD, :] = prev[pl.ds(half + d, 1), :] * prev_on
        fin[d + 1, PAD + fin_rows : PAD + fin_rows + 1, :] = nxt[pl.ds(half + d, 1), :] * next_on
        return carry

    lax.fori_loop(0, depth, line_of, 0)


def fluid_sweep(fluid, active, zlow, zhigh, colour, dims, done=None):
    cells, rows, width, depth, fin_rows, fin_width = dims
    parity = (iota((ROWS, width), 0) + iota((ROWS, width), 1)) & 1

    def plane(i, carry):
        off = parity ^ ((i + colour) & 1)
        for start in range(0, rows, ROWS):
            inner = slice(PAD + start, PAD + start + ROWS)
            here = fluid[i + 1, inner, :]
            low = pltpu.roll(zlow[start : start + ROWS, :], (LANES - i) % LANES, axis=1)
            high = pltpu.roll(zhigh[start : start + ROWS, :], LANES - 1 - i, axis=1)
            total = (
                fluid[i, inner, :]
                + fluid[i + 2, inner, :]
                + fluid[i + 1, PAD + start - 1 : PAD + start + ROWS - 1, :]
                + fluid[i + 1, PAD + start + 1 : PAD + start + ROWS + 1, :]
                + lane_neighbours(here, low, high)
            )
            updated = (here + FLUID_DIFFUSION * total) * FLUID_SCALE
            mask = active[i, start : start + ROWS, :] > off
            fluid[i + 1, inner, :] = jnp.where(mask, updated, here)
        if done is not None:
            done(i)
        return carry

    lax.fori_loop(0, cells, plane, 0)


def fin_neighbours(fin, d, hlow, hhigh, fin_rows):
    inner = slice(PAD, PAD + fin_rows)
    here = fin[d + 1, inner, :]
    low = pltpu.roll(hlow[...], (LANES - d) % LANES, axis=1)
    high = pltpu.roll(hhigh[...], LANES - 1 - d, axis=1)
    total = (
        fin[d, inner, :]
        + fin[d + 2, inner, :]
        + fin[d + 1, PAD - 1 : PAD + fin_rows - 1, :]
        + fin[d + 1, PAD + 1 : PAD + fin_rows + 1, :]
        + lane_neighbours(here, low, high)
    )
    return here, total


def solution(mesh):
    in_specs = (
        P("gx", "gy", "grp"),
        P("gx", "gy", "grp"),
        P("grp", "gx", "gy"),
        P("grp", "gx", "gy"),
        P("gx", "gy", None, None),
        P("gx", "gy", None),
    )
    out_specs = (P("gx", "gy", "grp"), P("grp", "gx", "gy"))
    count = mesh.shape["gx"]
    groups = mesh.shape["grp"]
    sides = mesh.shape["gy"]
    assert sides == 2
    ring = count == 4
    vmem = pl.BlockSpec(memory_space=pltpu.VMEM)
    hbm = pl.BlockSpec(memory_space=pl.ANY)

    def local(fluid_temp, active, fin_temp, fin_source, wall_owner, wall_target):
        cells, rows, width = fluid_temp.shape
        depth, fin_rows, fin_width = fin_temp.shape
        assert rows == LANES and width == fin_width == 2 * rows and fin_rows == 2 * cells
        assert depth <= LANES and cells % 2 == 0 and rows % ROWS == 0 and fin_rows == ROWS
        dims = (cells, rows, width, depth, fin_rows, fin_width)
        half = rows // 2
        face_rows = half + depth
        wall_rows = fin_rows + cells
        small_rows = cells + fin_rows
        gx_rows = face_rows + (wall_rows if ring else 0)
        owners = wall_owner.reshape(cells, rows)
        targets = wall_target.reshape(cells, rows)
        f32 = lambda *shape: jax.ShapeDtypeStruct(shape, jnp.float32)
        params = pltpu.CompilerParams(vmem_limit_bytes=32 * 1024 * 1024)
        fluid_pad = f32(cells + 2, rows + 2 * PAD, width)
        fin_pad = f32(depth + 2, fin_rows + 2 * PAD, fin_width)
        faces = (f32(small_rows, width), f32(small_rows, width), f32(small_rows, width))

        def start_kernel(fluid_hbm, fin_hbm, own, tgt, fluid, fin, gxf, gxb, grpf, grpb, gyx,
                         wall, sems):
            copies = (
                pltpu.make_async_copy(
                    fluid_hbm, fluid.at[pl.ds(1, cells), pl.ds(PAD, rows), :], sems.at[0]
                ),
                pltpu.make_async_copy(
                    fin_hbm, fin.at[pl.ds(1, depth), pl.ds(PAD, fin_rows), :], sems.at[1]
                ),
            )
            for copy in copies:
                copy.start()
            gy = lax.axis_index("gy")
            shape = (cells, rows)
            shift = tgt[...] - 2 * (iota(shape, 0) * fin_width + iota(shape, 1))
            row_shift = (shift >= fin_width).astype(jnp.int32)
            code = own[...] * 4 + row_shift * 2 + (shift - row_shift * fin_width)
            wall[fin_rows:, LANES:] = code.astype(jnp.float32)
            for copy in copies:
                copy.wait()
            bottom = pack_faces(fluid, fin, 1, gxf, gxb, grpf, grpb, gyx, gy, dims)
            wall[fin_rows:, 0:LANES] = bottom
            surface = fin[1, PAD : PAD + fin_rows, :]
            even_rows = dot(interleave_matrix(fin_rows), surface, ((0,), (0,)))
            wall[0:fin_rows, :] = dot(even_rows, interleave_matrix(fin_width), ((1,), (0,)))
            if ring:
                gxf[face_rows:, :] = wall[...]
                gxb[face_rows:, :] = wall[...]

        fluid0, fin0, gxf, gxb, grpf, grpb, gyx, wall = pl.pallas_call(
            start_kernel,
            out_shape=(fluid_pad, fin_pad, f32(gx_rows, width), f32(gx_rows, width)) + faces
            + (f32(wall_rows, width),),
            in_specs=[hbm, hbm, vmem, vmem],
            out_specs=(vmem,) * 8,
            scratch_shapes=[pltpu.SemaphoreType.DMA((2,))],
            compiler_params=params,
            name="start",
        )(fluid_temp, fin_temp, owners, targets)

        def chain(size, step):
            return [(i, i + step) for i in range(size) if 0 <= i + step < size]

        def around(size, step):
            return [(i, (i + step) % size) for i in range(size)]

        swap = [(0, 1), (1, 0)]
        if ring:
            prev = lax.ppermute(gxf, "gx", around(count, 1))
            nxt = lax.ppermute(gxb, "gx", around(count, -1))
            walls = [wall] + [lax.ppermute(wall, "gx", around(count, k)) for k in range(2, count - 1)]
        else:
            prev = lax.ppermute(gxf, "gx", chain(count, 1))
            nxt = lax.ppermute(gxb, "gx", chain(count, -1))
            walls = [wall, lax.all_gather(wall, "gx")]
        below = lax.ppermute(grpf, "grp", chain(groups, 1))
        above = lax.ppermute(grpb, "grp", chain(groups, -1))
        side = lax.ppermute(gyx, "gy", swap)

        def middle_kernel(*refs):
            (act, prev, nxt, below, above, side), refs = (refs[2],) + refs[4:9], refs[9:]
            wall_refs, refs = refs[: len(walls)], refs[len(walls) :]
            fluid, fin, first, src, ghost_out, gxf, gxb, grpf, grpb, gyx = refs[:10]
            zlow, zhigh, hlow, hhigh = refs[10:]
            gx = lax.axis_index("gx")
            gy = lax.axis_index("gy")
            on_wall = lax.axis_index("grp") == 0
            own = wall_refs[0]
            own_code = own[fin_rows:, LANES:]
            if ring:
                slots = [(gx, own, 0), ((gx + count - 1) % count, prev, face_rows),
                         ((gx + 1) % count, nxt, face_rows)]
                slots += [((gx + count - k) % count, ref, 0) for k, ref in
                          zip(range(2, count - 1), wall_refs[1:])]
                slots = [(o, ref.at[pl.ds(base, wall_rows), :]) for o, ref, base in slots]
            else:
                slots = [(s, wall_refs[1].at[s]) for s in range(count)]
            quadrants = [(a * cells, b * LANES) for a in range(2) for b in range(2)]
            ghost = jnp.zeros((cells, rows), jnp.float32)
            deposits = [jnp.zeros((cells, rows), jnp.float32) for _ in quadrants]
            mine = (4 * gx).astype(jnp.float32)
            for owner, ref in slots:
                theirs = own_code - (4 * jnp.asarray(owner, jnp.int32)).astype(jnp.float32)
                temps = ref[fin_rows:, 0:LANES]
                wanted = ref[fin_rows:, LANES:] - mine
                for q, (r, c) in enumerate(quadrants):
                    ghost = jnp.where(theirs == q, ref[r : r + cells, c : c + LANES], ghost)
                    flux = HEAT_COEF * (temps - own[r : r + cells, c : c + LANES])
                    deposits[q] = deposits[q] + jnp.where(wanted == q, flux, 0.0)
            ghost_out[...] = ghost

            @pl.when(on_wall)
            def _():
                split = jnp.concatenate(
                    [jnp.concatenate(deposits[0:2], axis=1), jnp.concatenate(deposits[2:4], axis=1)],
                    axis=0,
                )
                mixed = dot(split, interleave_matrix(fin_width), ((1,), (1,)))
                src[0] = src[0] + dot(interleave_matrix(fin_rows), mixed, ((1,), (0,)))

            low_face = jnp.where(on_wall, ghost, below[0:cells, 0:LANES])
            prev_on = jnp.where(gx == 0, 0.0, 1.0)
            next_on = jnp.where(gx == count - 1, 0.0, 1.0)
            unpack_halos(fluid, fin, zlow, zhigh, hlow, hhigh, prev, nxt, below, above, side,
                         low_face, gy, prev_on, next_on, dims)
            fluid_sweep(fluid, act, zlow, zhigh, 0, dims)

            def layer(d, carry):
                here, total = fin_neighbours(fin, d, hlow, hhigh, fin_rows)
                rhs = here + src[d]
                first[d + 1, PAD : PAD + fin_rows, :] = (rhs + FIN_CONDUCTION * total) * (1.0 / DIAG)
                src[d] = rhs * (OMEGA / DIAG) + here * (1.0 - OMEGA)
                return carry

            lax.fori_loop(0, depth, layer, 0)
            pack_faces(fluid, first, 0, gxf, gxb, grpf, grpb, gyx, gy, dims)

        received = (prev, nxt, below, above, side)
        scratch = [
            pltpu.VMEM((rows, LANES), jnp.float32),
            pltpu.VMEM((rows, LANES), jnp.float32),
            pltpu.VMEM((fin_rows, LANES), jnp.float32),
            pltpu.VMEM((fin_rows, LANES), jnp.float32),
        ]
        outs = pl.pallas_call(
            middle_kernel,
            out_shape=(fluid_pad, fin_pad, fin_pad, f32(depth, fin_rows, fin_width),
                       f32(cells, rows), f32(face_rows, width), f32(face_rows, width)) + faces,
            in_specs=[vmem] * (9 + len(walls)),
            out_specs=(vmem,) * 10,
            scratch_shapes=scratch,
            input_output_aliases={0: 0, 1: 1, 3: 3},
            compiler_params=params,
            name="middle",
        )(fluid0, fin0, active, fin_source, *received, *walls)
        fluid1, _, first, rest, ghost, gxf, gxb, grpf, grpb, gyx = outs

        prev = lax.ppermute(gxf, "gx", chain(count, 1))
        nxt = lax.ppermute(gxb, "gx", chain(count, -1))
        below = lax.ppermute(grpf, "grp", chain(groups, 1))
        above = lax.ppermute(grpb, "grp", chain(groups, -1))
        side = lax.ppermute(gyx, "gy", swap)

        def end_kernel(_0, _1, _2, act, ghost, prev, nxt, below, above, side,
                       fluid, first, rest, fluid_new, fin_new,
                       zlow, zhigh, hlow, hhigh, fluid_sems, fin_sems):
            gy = lax.axis_index("gy")
            on_wall = lax.axis_index("grp") == 0
            low_face = jnp.where(on_wall, ghost[...], below[0:cells, 0:LANES])
            unpack_halos(fluid, first, zlow, zhigh, hlow, hhigh, prev, nxt, below, above, side,
                         low_face, gy, 1.0, 1.0, dims)

            def fluid_copy(i):
                return pltpu.make_async_copy(
                    fluid.at[i + 1, pl.ds(PAD, rows), :], fluid_new.at[i], fluid_sems.at[i]
                )

            def fin_copy(d):
                return pltpu.make_async_copy(rest.at[d], fin_new.at[d], fin_sems.at[d])

            fluid_sweep(fluid, act, zlow, zhigh, 1, dims, lambda i: fluid_copy(i).start())

            def layer(d, carry):
                _, total = fin_neighbours(first, d, hlow, hhigh, fin_rows)
                rest[d] = rest[d] + (OMEGA * FIN_CONDUCTION / DIAG) * total
                fin_copy(d).start()
                return carry

            lax.fori_loop(0, depth, layer, 0)

            def finish_fluid(i, carry):
                fluid_copy(i).wait()
                return carry

            def finish_fin(d, carry):
                fin_copy(d).wait()
                return carry

            lax.fori_loop(0, cells, finish_fluid, 0)
            lax.fori_loop(0, depth, finish_fin, 0)

        results = pl.pallas_call(
            end_kernel,
            out_shape=(fluid_pad, fin_pad, f32(depth, fin_rows, fin_width),
                       f32(cells, rows, width), f32(depth, fin_rows, fin_width)),
            in_specs=[vmem] * 10,
            out_specs=(vmem, vmem, vmem, hbm, hbm),
            scratch_shapes=scratch + [pltpu.SemaphoreType.DMA((cells,)),
                                      pltpu.SemaphoreType.DMA((depth,))],
            input_output_aliases={0: 0, 1: 1, 2: 2},
            compiler_params=params,
            name="end",
        )(fluid1, first, rest, active, ghost, prev, nxt, below, above, side)
        return results[3], results[4]

    return jax.shard_map(local, mesh=mesh, in_specs=in_specs, out_specs=out_specs, check_vma=False)
```

```python
import jax
import jax.numpy as jnp
from jax import lax
from jax.experimental import pallas as pl
from jax.experimental.pallas import tpu as pltpu
from jax.sharding import PartitionSpec as P

FLUID_DIFFUSION = 1.0
FIN_CONDUCTION = 1.0
HEAT_COEF = 1.0
DIAG = 1.0 + 6.0 * FIN_CONDUCTION
SPECTRAL = 6.0 * FIN_CONDUCTION / DIAG
OMEGA = 1.0 / (1.0 - SPECTRAL * SPECTRAL / 2.0)
FLUID_SCALE = 1.0 / (1.0 + 6.0 * FLUID_DIFFUSION)
LANES = 128
PAD = 8
ROWS = 32
HIGHEST = lax.Precision.HIGHEST


def iota(shape, axis):
    return lax.broadcasted_iota(jnp.int32, shape, axis)


def repeat(count, body, step=8):
    def trip(k, carry):
        for j in range(step):
            body(k * step + j)
        return carry

    lax.fori_loop(0, count // step, trip, 0)


def tiles(value):
    return [value[:, k : k + LANES] for k in range(0, value.shape[1], LANES)]


def lane_neighbours(block, low, high):
    parts = tiles(block)
    lane = iota(parts[0].shape, 1)
    down = [pltpu.roll(part, 1, axis=1) for part in parts]
    up = [pltpu.roll(part, LANES - 1, axis=1) for part in parts]
    below = [jnp.where(lane == 0, a, b) for a, b in zip([low] + down[:-1], down)]
    above = [jnp.where(lane == LANES - 1, a, b) for a, b in zip(up[1:] + [high], up)]
    return jnp.concatenate([a + b for a, b in zip(below, above)], axis=1)


def interleave_matrix(count):
    row = iota((count, count), 0)
    col = iota((count, count), 1)
    half = count // 2
    source = jnp.where(col < half, 2 * col, 2 * (col - half) + 1)
    return (row == source).astype(jnp.float32)


def dot(a, b, contract):
    return lax.dot_general(
        a, b, (contract, ((), ())), precision=HIGHEST, preferred_element_type=jnp.float32
    )


def checker_pack(plane, parity):
    rows = plane.shape[0] // 2
    top = plane[:rows]
    bottom = plane[rows:]
    colour = (iota(top.shape, 0) + iota(top.shape, 1)) & 1
    return jnp.where(colour == parity, top, pltpu.roll(bottom, 1, axis=1))


def lane_faces(fluid, cells, rows):
    width = fluid.shape[2]
    low = jnp.zeros((rows, LANES), jnp.float32)
    high = low
    lane = iota((rows, LANES), 1)
    for i in range(cells):
        here = lane == i
        low = jnp.where(here, fluid[i + 1, PAD : PAD + rows, 0:1], low)
        high = jnp.where(here, fluid[i + 1, PAD : PAD + rows, width - 1 : width], high)
    return low.T[:cells], high.T[:cells]


def pack_faces(fluid, fin, colour, gxf, gxb, grpf, grpb, gyx, gy, dims):
    cells, rows, width, depth, fin_rows, fin_width = dims
    half = rows // 2
    inner = pl.ds(PAD, rows)
    gxf[0:half, :] = checker_pack(fluid[cells, inner, :], (colour + cells - 1) % 2)
    gxb[0:half, :] = checker_pack(fluid[1, inner, :], colour)
    low, high = lane_faces(fluid, cells, rows)
    grpf[0:cells, 0:LANES] = high
    grpb[0:cells, 0:LANES] = low
    grpf[cells : cells + fin_rows, :] = fin[depth, PAD : PAD + fin_rows, :]
    grpb[cells : cells + fin_rows, :] = fin[1, PAD : PAD + fin_rows, :]
    edge = PAD + (1 - gy) * (rows - 1)
    for i in range(cells):
        gyx[i : i + 1, :] = fluid[i + 1, pl.ds(edge, 1), :]
    lane = iota((fin_rows, LANES), 1)

    def columns(at):
        kept = jnp.zeros((fin_rows, LANES), jnp.float32)
        for d in range(depth):
            kept = jnp.where(lane == d, fin[d + 1, PAD : PAD + fin_rows, at : at + 1], kept)
        gyx[cells : cells + fin_rows, 0:LANES] = kept

    @pl.when(gy == 0)
    def _():
        columns(fin_width - 1)

    @pl.when(gy != 0)
    def _():
        columns(0)

    def lines(d):
        gxf[pl.ds(half + d, 1), :] = fin[d + 1, PAD + fin_rows - 1 : PAD + fin_rows, :]
        gxb[pl.ds(half + d, 1), :] = fin[d + 1, PAD : PAD + 1, :]

    repeat(depth, lines)
    return low


def unpack_halos(fluid, fin, zlow, zhigh, hlow, hhigh, prev, nxt, below, above, side,
                 low_face, gy, prev_on, next_on, dims):
    cells, rows, width, depth, fin_rows, fin_width = dims
    half = rows // 2
    for plane, ref, on in ((0, prev, prev_on), (cells + 1, nxt, next_on)):
        packed = ref[0:half, :] * on
        fluid[plane, PAD : PAD + half, :] = packed
        fluid[plane, PAD + half : PAD + rows, :] = pltpu.roll(packed, width - 1, axis=1)
    low_on = jnp.where(gy == 0, 0.0, 1.0)
    high_on = 1.0 - low_on
    for i in range(cells):
        line = side[i : i + 1, :]
        fluid[i + 1, PAD - 1 : PAD, :] = line * low_on
        fluid[i + 1, PAD + rows : PAD + rows + 1, :] = line * high_on
    blank = jnp.zeros((LANES - cells, rows), jnp.float32)
    zlow[...] = jnp.concatenate([low_face, blank], axis=0).T
    zhigh[...] = jnp.concatenate([above[0:cells, 0:LANES], blank], axis=0).T
    fin[0, PAD : PAD + fin_rows, :] = below[cells : cells + fin_rows, :]
    fin[depth + 1, PAD : PAD + fin_rows, :] = above[cells : cells + fin_rows, :]
    columns = side[cells : cells + fin_rows, 0:LANES]
    hlow[...] = columns * low_on
    hhigh[...] = columns * high_on

    def line_of(d):
        fin[d + 1, PAD - 1 : PAD, :] = prev[pl.ds(half + d, 1), :] * prev_on
        fin[d + 1, PAD + fin_rows : PAD + fin_rows + 1, :] = nxt[pl.ds(half + d, 1), :] * next_on

    repeat(depth, line_of)


def fluid_sweep(fluid, active, zlow, zhigh, colour, dims, done=None):
    cells, rows, width, depth, fin_rows, fin_width = dims
    parity = (iota((ROWS, width), 0) + iota((ROWS, width), 1)) & 1

    def plane(i, carry):
        off = parity ^ ((i + colour) & 1)
        for start in range(0, rows, ROWS):
            inner = slice(PAD + start, PAD + start + ROWS)
            here = fluid[i + 1, inner, :]
            low = pltpu.roll(zlow[start : start + ROWS, :], (LANES - i) % LANES, axis=1)
            high = pltpu.roll(zhigh[start : start + ROWS, :], LANES - 1 - i, axis=1)
            total = (
                fluid[i, inner, :]
                + fluid[i + 2, inner, :]
                + fluid[i + 1, PAD + start - 1 : PAD + start + ROWS - 1, :]
                + fluid[i + 1, PAD + start + 1 : PAD + start + ROWS + 1, :]
                + lane_neighbours(here, low, high)
            )
            updated = (here + FLUID_DIFFUSION * total) * FLUID_SCALE
            mask = active[i, start : start + ROWS, :] > off
            fluid[i + 1, inner, :] = jnp.where(mask, updated, here)
        if done is not None:
            done(i)
        return carry

    lax.fori_loop(0, cells, plane, 0)


def fin_neighbours(fin, d, hlow, hhigh, fin_rows):
    inner = slice(PAD, PAD + fin_rows)
    here = fin[d + 1, inner, :]
    low = pltpu.roll(hlow[...], (LANES - d) % LANES, axis=1)
    high = pltpu.roll(hhigh[...], LANES - 1 - d, axis=1)
    total = (
        fin[d, inner, :]
        + fin[d + 2, inner, :]
        + fin[d + 1, PAD - 1 : PAD + fin_rows - 1, :]
        + fin[d + 1, PAD + 1 : PAD + fin_rows + 1, :]
        + lane_neighbours(here, low, high)
    )
    return here, total


def solution(mesh):
    in_specs = (
        P("gx", "gy", "grp"),
        P("gx", "gy", "grp"),
        P("grp", "gx", "gy"),
        P("grp", "gx", "gy"),
        P("gx", "gy", None, None),
        P("gx", "gy", None),
    )
    out_specs = (P("gx", "gy", "grp"), P("grp", "gx", "gy"))
    count = mesh.shape["gx"]
    groups = mesh.shape["grp"]
    sides = mesh.shape["gy"]
    assert sides == 2
    ring = count == 4
    vmem = pl.BlockSpec(memory_space=pltpu.VMEM)
    hbm = pl.BlockSpec(memory_space=pl.ANY)

    def local(fluid_temp, active, fin_temp, fin_source, wall_owner, wall_target):
        cells, rows, width = fluid_temp.shape
        depth, fin_rows, fin_width = fin_temp.shape
        assert rows == LANES and width == fin_width == 2 * rows and fin_rows == 2 * cells
        assert depth <= LANES and depth % 8 == 0 and cells % 2 == 0 and rows % ROWS == 0 and fin_rows == ROWS
        dims = (cells, rows, width, depth, fin_rows, fin_width)
        half = rows // 2
        face_rows = half + depth
        wall_rows = fin_rows + cells
        small_rows = cells + fin_rows
        gx_rows = face_rows + (wall_rows if ring else 0)
        owners = wall_owner.reshape(cells, rows)
        targets = wall_target.reshape(cells, rows)
        f32 = lambda *shape: jax.ShapeDtypeStruct(shape, jnp.float32)
        params = pltpu.CompilerParams(vmem_limit_bytes=32 * 1024 * 1024)
        fluid_pad = f32(cells + 2, rows + 2 * PAD, width)
        fin_pad = f32(depth + 2, fin_rows + 2 * PAD, fin_width)
        faces = (f32(small_rows, width), f32(small_rows, width), f32(small_rows, width))

        def start_kernel(fluid_hbm, fin_hbm, own, tgt, fluid, fin, gxf, gxb, grpf, grpb, gyx,
                         wall, sems):
            copies = (
                pltpu.make_async_copy(
                    fluid_hbm, fluid.at[pl.ds(1, cells), pl.ds(PAD, rows), :], sems.at[0]
                ),
                pltpu.make_async_copy(
                    fin_hbm, fin.at[pl.ds(1, depth), pl.ds(PAD, fin_rows), :], sems.at[1]
                ),
            )
            for copy in copies:
                copy.start()
            gy = lax.axis_index("gy")
            shape = (cells, rows)
            shift = tgt[...] - 2 * (iota(shape, 0) * fin_width + iota(shape, 1))
            row_shift = (shift >= fin_width).astype(jnp.int32)
            code = own[...] * 4 + row_shift * 2 + (shift - row_shift * fin_width)
            wall[fin_rows:, LANES:] = code.astype(jnp.float32)
            for copy in copies:
                copy.wait()
            bottom = pack_faces(fluid, fin, 1, gxf, gxb, grpf, grpb, gyx, gy, dims)
            wall[fin_rows:, 0:LANES] = bottom
            surface = fin[1, PAD : PAD + fin_rows, :]
            even_rows = dot(interleave_matrix(fin_rows), surface, ((0,), (0,)))
            wall[0:fin_rows, :] = dot(even_rows, interleave_matrix(fin_width), ((1,), (0,)))
            if ring:
                gxf[face_rows:, :] = wall[...]
                gxb[face_rows:, :] = wall[...]

        fluid0, fin0, gxf, gxb, grpf, grpb, gyx, wall = pl.pallas_call(
            start_kernel,
            out_shape=(fluid_pad, fin_pad, f32(gx_rows, width), f32(gx_rows, width)) + faces
            + (f32(wall_rows, width),),
            in_specs=[hbm, hbm, vmem, vmem],
            out_specs=(vmem,) * 8,
            scratch_shapes=[pltpu.SemaphoreType.DMA((2,))],
            compiler_params=params,
            name="start",
        )(fluid_temp, fin_temp, owners, targets)

        def chain(size, step):
            return [(i, i + step) for i in range(size) if 0 <= i + step < size]

        def around(size, step):
            return [(i, (i + step) % size) for i in range(size)]

        swap = [(0, 1), (1, 0)]
        if ring:
            prev = lax.ppermute(gxf, "gx", around(count, 1))
            nxt = lax.ppermute(gxb, "gx", around(count, -1))
            walls = [wall] + [lax.ppermute(wall, "gx", around(count, k)) for k in range(2, count - 1)]
        else:
            prev = lax.ppermute(gxf, "gx", chain(count, 1))
            nxt = lax.ppermute(gxb, "gx", chain(count, -1))
            walls = [wall, lax.all_gather(wall, "gx")]
        below = lax.ppermute(grpf, "grp", chain(groups, 1))
        above = lax.ppermute(grpb, "grp", chain(groups, -1))
        side = lax.ppermute(gyx, "gy", swap)

        def middle_kernel(*refs):
            (act, prev, nxt, below, above, side), refs = (refs[2],) + refs[4:9], refs[9:]
            wall_refs, refs = refs[: len(walls)], refs[len(walls) :]
            fluid, fin, first, src, ghost_out, gxf, gxb, grpf, grpb, gyx = refs[:10]
            zlow, zhigh, hlow, hhigh = refs[10:]
            gx = lax.axis_index("gx")
            gy = lax.axis_index("gy")
            on_wall = lax.axis_index("grp") == 0
            own = wall_refs[0]
            own_code = own[fin_rows:, LANES:]
            if ring:
                slots = [(gx, own, 0), ((gx + count - 1) % count, prev, face_rows),
                         ((gx + 1) % count, nxt, face_rows)]
                slots += [((gx + count - k) % count, ref, 0) for k, ref in
                          zip(range(2, count - 1), wall_refs[1:])]
                slots = [(o, ref.at[pl.ds(base, wall_rows), :]) for o, ref, base in slots]
            else:
                slots = [(s, wall_refs[1].at[s]) for s in range(count)]
            quadrants = [(a * cells, b * LANES) for a in range(2) for b in range(2)]
            ghost = jnp.zeros((cells, rows), jnp.float32)
            deposits = [jnp.zeros((cells, rows), jnp.float32) for _ in quadrants]
            mine = (4 * gx).astype(jnp.float32)
            for owner, ref in slots:
                theirs = own_code - (4 * jnp.asarray(owner, jnp.int32)).astype(jnp.float32)
                temps = ref[fin_rows:, 0:LANES]
                wanted = ref[fin_rows:, LANES:] - mine
                for q, (r, c) in enumerate(quadrants):
                    ghost = jnp.where(theirs == q, ref[r : r + cells, c : c + LANES], ghost)
                    flux = HEAT_COEF * (temps - own[r : r + cells, c : c + LANES])
                    deposits[q] = deposits[q] + jnp.where(wanted == q, flux, 0.0)
            ghost_out[...] = ghost

            @pl.when(on_wall)
            def _():
                split = jnp.concatenate(
                    [jnp.concatenate(deposits[0:2], axis=1), jnp.concatenate(deposits[2:4], axis=1)],
                    axis=0,
                )
                mixed = dot(split, interleave_matrix(fin_width), ((1,), (1,)))
                src[0] = src[0] + dot(interleave_matrix(fin_rows), mixed, ((1,), (0,)))

            low_face = jnp.where(on_wall, ghost, below[0:cells, 0:LANES])
            prev_on = jnp.where(gx == 0, 0.0, 1.0)
            next_on = jnp.where(gx == count - 1, 0.0, 1.0)
            unpack_halos(fluid, fin, zlow, zhigh, hlow, hhigh, prev, nxt, below, above, side,
                         low_face, gy, prev_on, next_on, dims)
            fluid_sweep(fluid, act, zlow, zhigh, 0, dims)

            def layer(d):
                here, total = fin_neighbours(fin, d, hlow, hhigh, fin_rows)
                rhs = here + src[d]
                first[d + 1, PAD : PAD + fin_rows, :] = (rhs + FIN_CONDUCTION * total) * (1.0 / DIAG)
                src[d] = rhs * (OMEGA / DIAG) + here * (1.0 - OMEGA)

            repeat(depth, layer)
            pack_faces(fluid, first, 0, gxf, gxb, grpf, grpb, gyx, gy, dims)

        received = (prev, nxt, below, above, side)
        scratch = [
            pltpu.VMEM((rows, LANES), jnp.float32),
            pltpu.VMEM((rows, LANES), jnp.float32),
            pltpu.VMEM((fin_rows, LANES), jnp.float32),
            pltpu.VMEM((fin_rows, LANES), jnp.float32),
        ]
        outs = pl.pallas_call(
            middle_kernel,
            out_shape=(fluid_pad, fin_pad, fin_pad, f32(depth, fin_rows, fin_width),
                       f32(cells, rows), f32(face_rows, width), f32(face_rows, width)) + faces,
            in_specs=[vmem] * (9 + len(walls)),
            out_specs=(vmem,) * 10,
            scratch_shapes=scratch,
            input_output_aliases={0: 0, 1: 1, 3: 3},
            compiler_params=params,
            name="middle",
        )(fluid0, fin0, active, fin_source, *received, *walls)
        fluid1, _, first, rest, ghost, gxf, gxb, grpf, grpb, gyx = outs

        prev = lax.ppermute(gxf, "gx", chain(count, 1))
        nxt = lax.ppermute(gxb, "gx", chain(count, -1))
        below = lax.ppermute(grpf, "grp", chain(groups, 1))
        above = lax.ppermute(grpb, "grp", chain(groups, -1))
        side = lax.ppermute(gyx, "gy", swap)

        def end_kernel(_0, _1, _2, act, ghost, prev, nxt, below, above, side,
                       fluid, first, rest, fluid_new, fin_new,
                       zlow, zhigh, hlow, hhigh, fluid_sems, fin_sems):
            gy = lax.axis_index("gy")
            on_wall = lax.axis_index("grp") == 0
            low_face = jnp.where(on_wall, ghost[...], below[0:cells, 0:LANES])
            unpack_halos(fluid, first, zlow, zhigh, hlow, hhigh, prev, nxt, below, above, side,
                         low_face, gy, 1.0, 1.0, dims)

            def fluid_copy(i):
                return pltpu.make_async_copy(
                    fluid.at[i + 1, pl.ds(PAD, rows), :], fluid_new.at[i], fluid_sems.at[i]
                )

            def fin_copy(k):
                part = pl.ds(k * 8, 8)
                return pltpu.make_async_copy(rest.at[part], fin_new.at[part], fin_sems.at[k])

            fluid_sweep(fluid, act, zlow, zhigh, 1, dims, lambda i: fluid_copy(i).start())

            def layers(k, carry):
                for j in range(8):
                    d = k * 8 + j
                    _, total = fin_neighbours(first, d, hlow, hhigh, fin_rows)
                    rest[d] = rest[d] + (OMEGA * FIN_CONDUCTION / DIAG) * total
                fin_copy(k).start()
                return carry

            lax.fori_loop(0, depth // 8, layers, 0)

            def finish_fluid(i, carry):
                fluid_copy(i).wait()
                return carry

            def finish_fin(d, carry):
                fin_copy(d).wait()
                return carry

            lax.fori_loop(0, cells, finish_fluid, 0)
            lax.fori_loop(0, depth // 8, finish_fin, 0)

        results = pl.pallas_call(
            end_kernel,
            out_shape=(fluid_pad, fin_pad, f32(depth, fin_rows, fin_width),
                       f32(cells, rows, width), f32(depth, fin_rows, fin_width)),
            in_specs=[vmem] * 10,
            out_specs=(vmem, vmem, vmem, hbm, hbm),
            scratch_shapes=scratch + [pltpu.SemaphoreType.DMA((cells,)),
                                      pltpu.SemaphoreType.DMA((depth // 8,))],
            input_output_aliases={0: 0, 1: 1, 2: 2},
            compiler_params=params,
            name="end",
        )(fluid1, first, rest, active, ghost, prev, nxt, below, above, side)
        return results[3], results[4]

    return jax.shard_map(local, mesh=mesh, in_specs=in_specs, out_specs=out_specs, check_vma=False)
```

```python
import jax
import jax.numpy as jnp
from jax import lax
from jax.experimental import pallas as pl
from jax.experimental.pallas import tpu as pltpu
from jax.sharding import PartitionSpec as P

FLUID_DIFFUSION = 1.0
FIN_CONDUCTION = 1.0
HEAT_COEF = 1.0
DIAG = 1.0 + 6.0 * FIN_CONDUCTION
SPECTRAL = 6.0 * FIN_CONDUCTION / DIAG
OMEGA = 1.0 / (1.0 - SPECTRAL * SPECTRAL / 2.0)
FLUID_SCALE = 1.0 / (1.0 + 6.0 * FLUID_DIFFUSION)
LANES = 128
PAD = 8
ROWS = 32
HIGHEST = lax.Precision.HIGHEST


def iota(shape, axis):
    return lax.broadcasted_iota(jnp.int32, shape, axis)


def repeat(count, body, step=8):
    def trip(k, carry):
        for j in range(step):
            body(k * step + j)
        return carry

    lax.fori_loop(0, count // step, trip, 0)


def tiles(value):
    return [value[:, k : k + LANES] for k in range(0, value.shape[1], LANES)]


def lane_neighbours(block, low, high):
    parts = tiles(block)
    lane = iota(parts[0].shape, 1)
    down = [pltpu.roll(part, 1, axis=1) for part in parts]
    up = [pltpu.roll(part, LANES - 1, axis=1) for part in parts]
    below = [jnp.where(lane == 0, a, b) for a, b in zip([low] + down[:-1], down)]
    above = [jnp.where(lane == LANES - 1, a, b) for a, b in zip(up[1:] + [high], up)]
    return jnp.concatenate([a + b for a, b in zip(below, above)], axis=1)


def interleave_matrix(count):
    row = iota((count, count), 0)
    col = iota((count, count), 1)
    half = count // 2
    source = jnp.where(col < half, 2 * col, 2 * (col - half) + 1)
    return (row == source).astype(jnp.float32)


def dot(a, b, contract):
    return lax.dot_general(
        a, b, (contract, ((), ())), precision=HIGHEST, preferred_element_type=jnp.float32
    )


def checker_pack(plane, parity):
    rows = plane.shape[0] // 2
    top = plane[:rows]
    bottom = plane[rows:]
    colour = (iota(top.shape, 0) + iota(top.shape, 1)) & 1
    return jnp.where(colour == parity, top, pltpu.roll(bottom, 1, axis=1))


def lane_faces(fluid, cells, rows):
    width = fluid.shape[2]
    low = jnp.zeros((rows, LANES), jnp.float32)
    high = low
    lane = iota((rows, LANES), 1)
    for i in range(cells):
        here = lane == i
        low = jnp.where(here, fluid[i + 1, PAD : PAD + rows, 0:1], low)
        high = jnp.where(here, fluid[i + 1, PAD : PAD + rows, width - 1 : width], high)
    return low.T[:cells], high.T[:cells]


def pack_faces(fluid, fin, colour, gxf, gxb, grpf, grpb, gyx, gy, dims):
    cells, rows, width, depth, fin_rows, fin_width = dims
    half = rows // 2
    inner = pl.ds(PAD, rows)
    gxf[0:half, :] = checker_pack(fluid[cells, inner, :], (colour + cells - 1) % 2)
    gxb[0:half, :] = checker_pack(fluid[1, inner, :], colour)
    low, high = lane_faces(fluid, cells, rows)
    grpf[0:cells, 0:LANES] = high
    grpb[0:cells, 0:LANES] = low
    grpf[cells : cells + fin_rows, :] = fin[depth, PAD : PAD + fin_rows, :]
    grpb[cells : cells + fin_rows, :] = fin[1, PAD : PAD + fin_rows, :]
    edge = PAD + (1 - gy) * (rows - 1)
    for i in range(cells):
        gyx[i : i + 1, :] = fluid[i + 1, pl.ds(edge, 1), :]
    lane = iota((fin_rows, LANES), 1)

    def columns(at):
        kept = jnp.zeros((fin_rows, LANES), jnp.float32)
        for d in range(depth):
            kept = jnp.where(lane == d, fin[d + 1, PAD : PAD + fin_rows, at : at + 1], kept)
        gyx[cells : cells + fin_rows, 0:LANES] = kept

    @pl.when(gy == 0)
    def _():
        columns(fin_width - 1)

    @pl.when(gy != 0)
    def _():
        columns(0)

    def lines(d):
        gxf[pl.ds(half + d, 1), :] = fin[d + 1, PAD + fin_rows - 1 : PAD + fin_rows, :]
        gxb[pl.ds(half + d, 1), :] = fin[d + 1, PAD : PAD + 1, :]

    repeat(depth, lines)
    return low


def unpack_halos(fluid, fin, zlow, zhigh, hlow, hhigh, prev, nxt, below, above, side,
                 low_face, place, sizes, dims):
    cells, rows, width, depth, fin_rows, fin_width = dims
    half = rows // 2
    grp, gx, gy = place
    groups, count = sizes
    below_on = jnp.where(grp == 0, 0.0, 1.0)
    above_on = jnp.where(grp == groups - 1, 0.0, 1.0)
    prev_on = jnp.where(gx == 0, 0.0, 1.0)
    next_on = jnp.where(gx == count - 1, 0.0, 1.0)
    for plane, ref, on in ((0, prev, prev_on), (cells + 1, nxt, next_on)):
        packed = ref[0:half, :] * on
        fluid[plane, PAD : PAD + half, :] = packed
        fluid[plane, PAD + half : PAD + rows, :] = pltpu.roll(packed, width - 1, axis=1)
    low_on = jnp.where(gy == 0, 0.0, 1.0)
    high_on = 1.0 - low_on
    for i in range(cells):
        line = side[i : i + 1, :]
        fluid[i + 1, PAD - 1 : PAD, :] = line * low_on
        fluid[i + 1, PAD + rows : PAD + rows + 1, :] = line * high_on
    blank = jnp.zeros((LANES - cells, rows), jnp.float32)
    zlow[...] = jnp.concatenate([low_face, blank], axis=0).T
    zhigh[...] = jnp.concatenate([above[0:cells, 0:LANES] * above_on, blank], axis=0).T
    fin[0, PAD : PAD + fin_rows, :] = below[cells : cells + fin_rows, :] * below_on
    fin[depth + 1, PAD : PAD + fin_rows, :] = above[cells : cells + fin_rows, :] * above_on
    columns = side[cells : cells + fin_rows, 0:LANES]
    hlow[...] = columns * low_on
    hhigh[...] = columns * high_on

    def line_of(d):
        fin[d + 1, PAD - 1 : PAD, :] = prev[pl.ds(half + d, 1), :] * prev_on
        fin[d + 1, PAD + fin_rows : PAD + fin_rows + 1, :] = nxt[pl.ds(half + d, 1), :] * next_on

    repeat(depth, line_of)


def fluid_sweep(fluid, active, zlow, zhigh, colour, dims, done=None):
    cells, rows, width, depth, fin_rows, fin_width = dims
    parity = (iota((ROWS, width), 0) + iota((ROWS, width), 1)) & 1

    def plane(i, carry):
        off = parity ^ ((i + colour) & 1)
        for start in range(0, rows, ROWS):
            inner = slice(PAD + start, PAD + start + ROWS)
            here = fluid[i + 1, inner, :]
            low = pltpu.roll(zlow[start : start + ROWS, :], (LANES - i) % LANES, axis=1)
            high = pltpu.roll(zhigh[start : start + ROWS, :], LANES - 1 - i, axis=1)
            total = (
                fluid[i, inner, :]
                + fluid[i + 2, inner, :]
                + fluid[i + 1, PAD + start - 1 : PAD + start + ROWS - 1, :]
                + fluid[i + 1, PAD + start + 1 : PAD + start + ROWS + 1, :]
                + lane_neighbours(here, low, high)
            )
            updated = (here + FLUID_DIFFUSION * total) * FLUID_SCALE
            mask = active[i, start : start + ROWS, :] > off
            fluid[i + 1, inner, :] = jnp.where(mask, updated, here)
        if done is not None:
            done(i)
        return carry

    lax.fori_loop(0, cells, plane, 0)


def fin_neighbours(fin, d, hlow, hhigh, fin_rows):
    inner = slice(PAD, PAD + fin_rows)
    here = fin[d + 1, inner, :]
    low = pltpu.roll(hlow[...], (LANES - d) % LANES, axis=1)
    high = pltpu.roll(hhigh[...], LANES - 1 - d, axis=1)
    total = (
        fin[d, inner, :]
        + fin[d + 2, inner, :]
        + fin[d + 1, PAD - 1 : PAD + fin_rows - 1, :]
        + fin[d + 1, PAD + 1 : PAD + fin_rows + 1, :]
        + lane_neighbours(here, low, high)
    )
    return here, total


def solution(mesh):
    in_specs = (
        P("gx", "gy", "grp"),
        P("gx", "gy", "grp"),
        P("grp", "gx", "gy"),
        P("grp", "gx", "gy"),
        P("gx", "gy", None, None),
        P("gx", "gy", None),
    )
    out_specs = (P("gx", "gy", "grp"), P("grp", "gx", "gy"))
    count = mesh.shape["gx"]
    groups = mesh.shape["grp"]
    sides = mesh.shape["gy"]
    assert sides == 2
    ring = count == 4
    vmem = pl.BlockSpec(memory_space=pltpu.VMEM)
    hbm = pl.BlockSpec(memory_space=pl.ANY)

    def local(fluid_temp, active, fin_temp, fin_source, wall_owner, wall_target):
        cells, rows, width = fluid_temp.shape
        depth, fin_rows, fin_width = fin_temp.shape
        assert rows == LANES and width == fin_width == 2 * rows and fin_rows == 2 * cells
        assert depth <= LANES and depth % 8 == 0 and cells % 2 == 0 and rows % ROWS == 0 and fin_rows == ROWS
        dims = (cells, rows, width, depth, fin_rows, fin_width)
        sizes = (groups, count)
        half = rows // 2
        face_rows = half + depth
        wall_rows = fin_rows + cells
        small_rows = cells + fin_rows
        gx_rows = face_rows + (wall_rows if ring else 0)
        owners = wall_owner.reshape(cells, rows)
        targets = wall_target.reshape(cells, rows)
        f32 = lambda *shape: jax.ShapeDtypeStruct(shape, jnp.float32)
        params = pltpu.CompilerParams(vmem_limit_bytes=32 * 1024 * 1024)
        fluid_pad = f32(cells + 2, rows + 2 * PAD, width)
        fin_pad = f32(depth + 2, fin_rows + 2 * PAD, fin_width)
        faces = (f32(small_rows, width), f32(small_rows, width), f32(small_rows, width))

        def start_kernel(fluid_hbm, fin_hbm, own_hbm, tgt_hbm, fluid, fin, gxf, gxb, grpf, grpb,
                         gyx, wall, own, tgt, sems):
            copies = (
                pltpu.make_async_copy(own_hbm, own, sems.at[2]),
                pltpu.make_async_copy(tgt_hbm, tgt, sems.at[3]),
                pltpu.make_async_copy(
                    fluid_hbm, fluid.at[pl.ds(1, cells), pl.ds(PAD, rows), :], sems.at[0]
                ),
                pltpu.make_async_copy(
                    fin_hbm, fin.at[pl.ds(1, depth), pl.ds(PAD, fin_rows), :], sems.at[1]
                ),
            )
            for copy in copies:
                copy.start()
            gy = lax.axis_index("gy")
            shape = (cells, rows)
            for copy in copies:
                copy.wait()
            shift = tgt[...] - 2 * (iota(shape, 0) * fin_width + iota(shape, 1))
            row_shift = (shift >= fin_width).astype(jnp.int32)
            code = own[...] * 4 + row_shift * 2 + (shift - row_shift * fin_width)
            wall[fin_rows:, LANES:] = code.astype(jnp.float32)
            bottom = pack_faces(fluid, fin, 1, gxf, gxb, grpf, grpb, gyx, gy, dims)
            wall[fin_rows:, 0:LANES] = bottom
            surface = fin[1, PAD : PAD + fin_rows, :]
            even_rows = dot(interleave_matrix(fin_rows), surface, ((0,), (0,)))
            wall[0:fin_rows, :] = dot(even_rows, interleave_matrix(fin_width), ((1,), (0,)))
            if ring:
                gxf[face_rows:, :] = wall[...]
                gxb[face_rows:, :] = wall[...]

        fluid0, fin0, gxf, gxb, grpf, grpb, gyx, wall = pl.pallas_call(
            start_kernel,
            out_shape=(fluid_pad, fin_pad, f32(gx_rows, width), f32(gx_rows, width)) + faces
            + (f32(wall_rows, width),),
            in_specs=[pl.BlockSpec(memory_space=pltpu.HBM)] * 4,
            out_specs=(vmem,) * 8,
            scratch_shapes=[pltpu.VMEM((cells, rows), jnp.int32), pltpu.VMEM((cells, rows), jnp.int32),
                            pltpu.SemaphoreType.DMA((4,))],
            compiler_params=params,
            name="start",
        )(*(pltpu.with_memory_space_constraint(v, pltpu.HBM)
            for v in (fluid_temp, fin_temp, owners, targets)))

        def around(size, step):
            return [(i, (i + step) % size) for i in range(size)]

        swap = [(0, 1), (1, 0)]
        prev = lax.ppermute(gxf, "gx", around(count, 1))
        nxt = lax.ppermute(gxb, "gx", around(count, -1))
        if ring:
            walls = [wall] + [lax.ppermute(wall, "gx", around(count, k)) for k in range(2, count - 1)]
        else:
            walls = [wall, lax.all_gather(wall, "gx")]
        below = lax.ppermute(grpf, "grp", around(groups, 1))
        above = lax.ppermute(grpb, "grp", around(groups, -1))
        side = lax.ppermute(gyx, "gy", swap)

        def middle_kernel(*refs):
            (act, src, prev, nxt, below, above, side), refs = refs[2:9], refs[9:]
            wall_refs, refs = refs[: len(walls)], refs[len(walls) :]
            fluid, fin, first, rest, ghost_out, gxf, gxb, grpf, grpb, gyx = refs[:10]
            zlow, zhigh, hlow, hhigh, deposit = refs[10:]
            place = [lax.axis_index(name) for name in ("grp", "gx", "gy")]
            grp, gx, gy = place
            on_wall = grp == 0
            own = wall_refs[0]
            own_code = own[fin_rows:, LANES:]
            if ring:
                slots = [(gx, own, 0), ((gx + count - 1) % count, prev, face_rows),
                         ((gx + 1) % count, nxt, face_rows)]
                slots += [((gx + count - k) % count, ref, 0) for k, ref in
                          zip(range(2, count - 1), wall_refs[1:])]
                slots = [(o, ref.at[pl.ds(base, wall_rows), :]) for o, ref, base in slots]
            else:
                slots = [(s, wall_refs[1].at[s]) for s in range(count)]
            quadrants = [(a * cells, b * LANES) for a in range(2) for b in range(2)]
            ghost = jnp.zeros((cells, rows), jnp.float32)
            deposits = [jnp.zeros((cells, rows), jnp.float32) for _ in quadrants]
            mine = (4 * gx).astype(jnp.float32)
            for owner, ref in slots:
                theirs = own_code - (4 * jnp.asarray(owner, jnp.int32)).astype(jnp.float32)
                temps = ref[fin_rows:, 0:LANES]
                wanted = ref[fin_rows:, LANES:] - mine
                for q, (r, c) in enumerate(quadrants):
                    ghost = jnp.where(theirs == q, ref[r : r + cells, c : c + LANES], ghost)
                    flux = HEAT_COEF * (temps - own[r : r + cells, c : c + LANES])
                    deposits[q] = deposits[q] + jnp.where(wanted == q, flux, 0.0)
            ghost_out[...] = ghost

            @pl.when(on_wall)
            def _():
                split = jnp.concatenate(
                    [jnp.concatenate(deposits[0:2], axis=1), jnp.concatenate(deposits[2:4], axis=1)],
                    axis=0,
                )
                mixed = dot(split, interleave_matrix(fin_width), ((1,), (1,)))
                deposit[...] = dot(interleave_matrix(fin_rows), mixed, ((1,), (0,)))

            @pl.when(jnp.logical_not(on_wall))
            def _():
                deposit[...] = jnp.zeros((fin_rows, fin_width), jnp.float32)

            low_face = jnp.where(on_wall, ghost, below[0:cells, 0:LANES])
            unpack_halos(fluid, fin, zlow, zhigh, hlow, hhigh, prev, nxt, below, above, side,
                         low_face, place, sizes, dims)
            fluid_sweep(fluid, act, zlow, zhigh, 0, dims)

            def layer(d):
                here, total = fin_neighbours(fin, d, hlow, hhigh, fin_rows)
                rhs = here + src[d]
                first[d + 1, PAD : PAD + fin_rows, :] = (rhs + FIN_CONDUCTION * total) * (1.0 / DIAG)
                rest[d] = rhs * (OMEGA / DIAG) + here * (1.0 - OMEGA)

            repeat(depth, layer)
            first[1, PAD : PAD + fin_rows, :] += deposit[...] * (1.0 / DIAG)
            rest[0] += deposit[...] * (OMEGA / DIAG)
            pack_faces(fluid, first, 0, gxf, gxb, grpf, grpb, gyx, gy, dims)

        received = (prev, nxt, below, above, side)
        scratch = [
            pltpu.VMEM((rows, LANES), jnp.float32),
            pltpu.VMEM((rows, LANES), jnp.float32),
            pltpu.VMEM((fin_rows, LANES), jnp.float32),
            pltpu.VMEM((fin_rows, LANES), jnp.float32),
        ]
        outs = pl.pallas_call(
            middle_kernel,
            out_shape=(fluid_pad, fin_pad, fin_pad, f32(depth, fin_rows, fin_width),
                       f32(cells, rows), f32(face_rows, width), f32(face_rows, width)) + faces,
            in_specs=[vmem] * (9 + len(walls)),
            out_specs=(vmem,) * 10,
            scratch_shapes=scratch + [pltpu.VMEM((fin_rows, fin_width), jnp.float32)],
            input_output_aliases={0: 0, 1: 1},
            compiler_params=params,
            name="middle",
        )(fluid0, fin0, active, fin_source, *received, *walls)
        fluid1, _, first, rest, ghost, gxf, gxb, grpf, grpb, gyx = outs

        prev = lax.ppermute(gxf, "gx", around(count, 1))
        nxt = lax.ppermute(gxb, "gx", around(count, -1))
        below = lax.ppermute(grpf, "grp", around(groups, 1))
        above = lax.ppermute(grpb, "grp", around(groups, -1))
        side = lax.ppermute(gyx, "gy", swap)

        def end_kernel(_0, _1, _2, act, ghost, prev, nxt, below, above, side,
                       fluid, first, rest, fluid_new, fin_new,
                       zlow, zhigh, hlow, hhigh, fluid_sems, fin_sems):
            place = [lax.axis_index(name) for name in ("grp", "gx", "gy")]
            on_wall = place[0] == 0
            low_face = jnp.where(on_wall, ghost[...], below[0:cells, 0:LANES])
            unpack_halos(fluid, first, zlow, zhigh, hlow, hhigh, prev, nxt, below, above, side,
                         low_face, place, sizes, dims)

            def fluid_copy(i):
                return pltpu.make_async_copy(
                    fluid.at[i + 1, pl.ds(PAD, rows), :], fluid_new.at[i], fluid_sems.at[i]
                )

            def fin_copy(k):
                part = pl.ds(k * 8, 8)
                return pltpu.make_async_copy(rest.at[part], fin_new.at[part], fin_sems.at[k])

            fluid_sweep(fluid, act, zlow, zhigh, 1, dims, lambda i: fluid_copy(i).start())

            def layers(k, carry):
                for j in range(8):
                    d = k * 8 + j
                    _, total = fin_neighbours(first, d, hlow, hhigh, fin_rows)
                    rest[d] = rest[d] + (OMEGA * FIN_CONDUCTION / DIAG) * total
                fin_copy(k).start()
                return carry

            lax.fori_loop(0, depth // 8, layers, 0)

            def finish_fluid(i, carry):
                fluid_copy(i).wait()
                return carry

            def finish_fin(d, carry):
                fin_copy(d).wait()
                return carry

            lax.fori_loop(0, cells, finish_fluid, 0)
            lax.fori_loop(0, depth // 8, finish_fin, 0)

        results = pl.pallas_call(
            end_kernel,
            out_shape=(fluid_pad, fin_pad, f32(depth, fin_rows, fin_width),
                       f32(cells, rows, width), f32(depth, fin_rows, fin_width)),
            in_specs=[vmem] * 10,
            out_specs=(vmem, vmem, vmem, hbm, hbm),
            scratch_shapes=scratch + [pltpu.SemaphoreType.DMA((cells,)),
                                      pltpu.SemaphoreType.DMA((depth // 8,))],
            input_output_aliases={0: 0, 1: 1, 2: 2},
            compiler_params=params,
            name="end",
        )(fluid1, first, rest, active, ghost, prev, nxt, below, above, side)
        return results[3], results[4]

    return jax.shard_map(local, mesh=mesh, in_specs=in_specs, out_specs=out_specs, check_vma=False)
```

```python
import jax
import jax.numpy as jnp
from jax import lax
from jax.experimental import pallas as pl
from jax.experimental.pallas import tpu as pltpu
from jax.sharding import PartitionSpec as P

FLUID_DIFFUSION = 1.0
FIN_CONDUCTION = 1.0
HEAT_COEF = 1.0
DIAG = 1.0 + 6.0 * FIN_CONDUCTION
SPECTRAL = 6.0 * FIN_CONDUCTION / DIAG
OMEGA = 1.0 / (1.0 - SPECTRAL * SPECTRAL / 2.0)
FLUID_SCALE = 1.0 / (1.0 + 6.0 * FLUID_DIFFUSION)
LANES = 128
PAD = 8
ROWS = 32
HIGHEST = lax.Precision.HIGHEST


def iota(shape, axis):
    return lax.broadcasted_iota(jnp.int32, shape, axis)


def repeat(count, body, step=8):
    def trip(k, carry):
        for j in range(step):
            body(k * step + j)
        return carry

    lax.fori_loop(0, count // step, trip, 0)


def tiles(value):
    return [value[:, k : k + LANES] for k in range(0, value.shape[1], LANES)]


def lane_neighbours(block, low, high):
    parts = tiles(block)
    lane = iota(parts[0].shape, 1)
    down = [pltpu.roll(part, 1, axis=1) for part in parts]
    up = [pltpu.roll(part, LANES - 1, axis=1) for part in parts]
    below = [jnp.where(lane == 0, a, b) for a, b in zip([low] + down[:-1], down)]
    above = [jnp.where(lane == LANES - 1, a, b) for a, b in zip(up[1:] + [high], up)]
    return jnp.concatenate([a + b for a, b in zip(below, above)], axis=1)


def interleave_matrix(count):
    row = iota((count, count), 0)
    col = iota((count, count), 1)
    half = count // 2
    source = jnp.where(col < half, 2 * col, 2 * (col - half) + 1)
    return (row == source).astype(jnp.float32)


def dot(a, b, contract):
    return lax.dot_general(
        a, b, (contract, ((), ())), precision=HIGHEST, preferred_element_type=jnp.float32
    )


def checker_pack(plane, parity):
    rows = plane.shape[0] // 2
    top = plane[:rows]
    bottom = plane[rows:]
    colour = (iota(top.shape, 0) + iota(top.shape, 1)) & 1
    return jnp.where(colour == parity, top, pltpu.roll(bottom, 1, axis=1))


def lane_faces(fluid, cells, rows):
    width = fluid.shape[2]
    low = jnp.zeros((rows, LANES), jnp.float32)
    high = low
    lane = iota((rows, LANES), 1)
    for i in range(cells):
        here = lane == i
        low = jnp.where(here, fluid[i + 1, PAD : PAD + rows, 0:1], low)
        high = jnp.where(here, fluid[i + 1, PAD : PAD + rows, width - 1 : width], high)
    return low.T[:cells], high.T[:cells]


def pack_faces(fluid, fin, colour, gxf, gxb, grpf, grpb, gyx, gy, dims):
    cells, rows, width, depth, fin_rows, fin_width = dims
    half = rows // 2
    inner = pl.ds(PAD, rows)
    gxf[0:half, :] = checker_pack(fluid[cells, inner, :], (colour + cells - 1) % 2)
    gxb[0:half, :] = checker_pack(fluid[1, inner, :], colour)
    low, high = lane_faces(fluid, cells, rows)
    grpf[0:cells, 0:LANES] = high
    grpb[0:cells, 0:LANES] = low
    grpf[cells : cells + fin_rows, :] = fin[depth, PAD : PAD + fin_rows, :]
    grpb[cells : cells + fin_rows, :] = fin[1, PAD : PAD + fin_rows, :]
    edge = PAD + (1 - gy) * (rows - 1)
    for i in range(cells):
        gyx[i : i + 1, :] = fluid[i + 1, pl.ds(edge, 1), :]
    lane = iota((fin_rows, LANES), 1)

    def columns(at, side):
        kept = jnp.zeros((fin_rows, LANES), jnp.float32)
        for d in range(depth):
            column = fin[d + 1, PAD : PAD + fin_rows, at : at + 1]
            kept = jnp.where(lane == 2 * d + side, column, kept)
        gyx[cells : cells + fin_rows, 0:LANES] = kept

    @pl.when(gy == 0)
    def _():
        columns(fin_width - 1, 1)

    @pl.when(gy != 0)
    def _():
        columns(0, 0)

    def lines(d):
        gxf[pl.ds(half + d, 1), :] = fin[d + 1, PAD + fin_rows - 1 : PAD + fin_rows, :]
        gxb[pl.ds(half + d, 1), :] = fin[d + 1, PAD : PAD + 1, :]

    repeat(depth, lines)
    return low


def unpack_halos(fluid, fin, zrows, zedge, prev, nxt, below, above, side, low_face, colour,
                 place, sizes, dims):
    cells, rows, width, depth, fin_rows, fin_width = dims
    half = rows // 2
    grp, gx, gy = place
    groups, count = sizes
    below_on = jnp.where(grp == 0, 0.0, 1.0)
    above_on = jnp.where(grp == groups - 1, 0.0, 1.0)
    prev_on = jnp.where(gx == 0, 0.0, 1.0)
    next_on = jnp.where(gx == count - 1, 0.0, 1.0)
    for plane, ref, on in ((0, prev, prev_on), (cells + 1, nxt, next_on)):
        packed = ref[0:half, :] * on
        fluid[plane, PAD : PAD + half, :] = packed
        fluid[plane, PAD + half : PAD + rows, :] = pltpu.roll(packed, width - 1, axis=1)
    low_on = jnp.where(gy == 0, 0.0, 1.0)
    high_on = 1.0 - low_on
    for i in range(cells):
        line = side[i : i + 1, :]
        fluid[i + 1, PAD - 1 : PAD, :] = line * low_on
        fluid[i + 1, PAD + rows : PAD + rows + 1, :] = line * high_on
    high_face = above[0:cells, 0:LANES] * above_on
    odd_row = (iota((1, rows), 1) & 1) == 1
    for k in range(cells // 2):
        for lane, face, swap in ((2 * k, high_face, colour == 1), (2 * k + 1, low_face, colour == 0)):
            first, second = face[2 * k : 2 * k + 1, :], face[2 * k + 1 : 2 * k + 2, :]
            zrows[lane : lane + 1, :] = jnp.where(odd_row == swap, second, first)
    zrows[cells:, :] = jnp.zeros((LANES - cells, rows), jnp.float32)
    zedge[...] = zrows[...].T
    fin[0, PAD : PAD + fin_rows, :] = below[cells : cells + fin_rows, :] * below_on
    fin[depth + 1, PAD : PAD + fin_rows, :] = above[cells : cells + fin_rows, :] * above_on

    def line_of(d):
        fin[d + 1, PAD - 1 : PAD, :] = prev[pl.ds(half + d, 1), :] * prev_on
        fin[d + 1, PAD + fin_rows : PAD + fin_rows + 1, :] = nxt[pl.ds(half + d, 1), :] * next_on

    repeat(depth, line_of)


def fluid_sweep(fluid, active, zedge, other, colour, dims, done=None):
    cells, rows, width, depth, fin_rows, fin_width = dims
    parity = (iota((ROWS, width), 0) + iota((ROWS, width), 1)) & 1
    updating = parity == colour
    off = parity ^ colour
    end_parity = iota((1, width), 1) & 1

    def pair(k, carry):
        a, b = 2 * k + 1, 2 * k + 2
        for at, swap in ((PAD - 1, 1 - colour), (PAD + rows, colour)):
            line = slice(at, at + 1)
            other[line, :] = jnp.where(end_parity == swap, fluid[b, line, :], fluid[a, line, :])
        for start in range(0, rows, ROWS):
            inner = slice(PAD + start, PAD + start + ROWS)
            other[inner, :] = jnp.where(updating, fluid[b, inner, :], fluid[a, inner, :])
        for start in range(0, rows, ROWS):
            inner = slice(PAD + start, PAD + start + ROWS)
            edge = pltpu.roll(zedge[start : start + ROWS, :], LANES - 1 - 2 * k, axis=1)
            shared = (
                other[PAD + start - 1 : PAD + start + ROWS - 1, :]
                + other[PAD + start + 1 : PAD + start + ROWS + 1, :]
                + lane_neighbours(other[inner, :], edge, edge)
            )
            here_a = fluid[a, inner, :]
            here_b = fluid[b, inner, :]
            total_a = shared + fluid[a - 1, inner, :] + here_b
            total_b = shared + fluid[b + 1, inner, :] + here_a
            new_a = (here_a + FLUID_DIFFUSION * total_a) * FLUID_SCALE
            new_b = (here_b + FLUID_DIFFUSION * total_b) * FLUID_SCALE
            mask_a = active[a - 1, start : start + ROWS, :] > off
            mask_b = active[b - 1, start : start + ROWS, :] > 1 - off
            fluid[a, inner, :] = jnp.where(mask_a, new_a, here_a)
            fluid[b, inner, :] = jnp.where(mask_b, new_b, here_b)
        if done is not None:
            done(k)
        return carry

    lax.fori_loop(0, cells // 2, pair, 0)


def fin_neighbours(fin, d, hedge, fin_rows):
    inner = slice(PAD, PAD + fin_rows)
    here = fin[d + 1, inner, :]
    edge = pltpu.roll(hedge, LANES - 1 - 2 * d, axis=1)
    total = (
        fin[d, inner, :]
        + fin[d + 2, inner, :]
        + fin[d + 1, PAD - 1 : PAD + fin_rows - 1, :]
        + fin[d + 1, PAD + 1 : PAD + fin_rows + 1, :]
        + lane_neighbours(here, edge, edge)
    )
    return here, total


def solution(mesh):
    in_specs = (
        P("gx", "gy", "grp"),
        P("gx", "gy", "grp"),
        P("grp", "gx", "gy"),
        P("grp", "gx", "gy"),
        P("gx", "gy", None, None),
        P("gx", "gy", None),
    )
    out_specs = (P("gx", "gy", "grp"), P("grp", "gx", "gy"))
    count = mesh.shape["gx"]
    groups = mesh.shape["grp"]
    sides = mesh.shape["gy"]
    assert sides == 2
    ring = count == 4
    vmem = pl.BlockSpec(memory_space=pltpu.VMEM)
    hbm = pl.BlockSpec(memory_space=pl.ANY)

    def local(fluid_temp, active, fin_temp, fin_source, wall_owner, wall_target):
        cells, rows, width = fluid_temp.shape
        depth, fin_rows, fin_width = fin_temp.shape
        assert rows == LANES and width == fin_width == 2 * rows and fin_rows == 2 * cells
        assert 2 * depth <= LANES and depth % 8 == 0 and cells % 2 == 0 and rows % ROWS == 0 and fin_rows == ROWS
        dims = (cells, rows, width, depth, fin_rows, fin_width)
        sizes = (groups, count)
        half = rows // 2
        face_rows = half + depth
        wall_rows = fin_rows + cells
        small_rows = cells + fin_rows
        gx_rows = face_rows + (wall_rows if ring else 0)
        owners = wall_owner.reshape(cells, rows)
        targets = wall_target.reshape(cells, rows)
        f32 = lambda *shape: jax.ShapeDtypeStruct(shape, jnp.float32)
        params = pltpu.CompilerParams(vmem_limit_bytes=32 * 1024 * 1024)
        fluid_pad = f32(cells + 2, rows + 2 * PAD, width)
        fin_pad = f32(depth + 2, fin_rows + 2 * PAD, fin_width)
        faces = (f32(small_rows, width), f32(small_rows, width), f32(small_rows, width))

        def start_kernel(fluid_hbm, fin_hbm, own_hbm, tgt_hbm, fluid, fin, gxf, gxb, grpf, grpb,
                         gyx, wall, own, tgt, sems):
            copies = (
                pltpu.make_async_copy(own_hbm, own, sems.at[2]),
                pltpu.make_async_copy(tgt_hbm, tgt, sems.at[3]),
                pltpu.make_async_copy(
                    fluid_hbm, fluid.at[pl.ds(1, cells), pl.ds(PAD, rows), :], sems.at[0]
                ),
                pltpu.make_async_copy(
                    fin_hbm, fin.at[pl.ds(1, depth), pl.ds(PAD, fin_rows), :], sems.at[1]
                ),
            )
            for copy in copies:
                copy.start()
            gy = lax.axis_index("gy")
            shape = (cells, rows)
            for copy in copies:
                copy.wait()
            shift = tgt[...] - 2 * (iota(shape, 0) * fin_width + iota(shape, 1))
            row_shift = (shift >= fin_width).astype(jnp.int32)
            code = own[...] * 4 + row_shift * 2 + (shift - row_shift * fin_width)
            wall[fin_rows:, LANES:] = code.astype(jnp.float32)
            bottom = pack_faces(fluid, fin, 1, gxf, gxb, grpf, grpb, gyx, gy, dims)
            wall[fin_rows:, 0:LANES] = bottom
            surface = fin[1, PAD : PAD + fin_rows, :]
            even_rows = dot(interleave_matrix(fin_rows), surface, ((0,), (0,)))
            wall[0:fin_rows, :] = dot(even_rows, interleave_matrix(fin_width), ((1,), (0,)))
            if ring:
                gxf[face_rows:, :] = wall[...]
                gxb[face_rows:, :] = wall[...]

        fluid0, fin0, gxf, gxb, grpf, grpb, gyx, wall = pl.pallas_call(
            start_kernel,
            out_shape=(fluid_pad, fin_pad, f32(gx_rows, width), f32(gx_rows, width)) + faces
            + (f32(wall_rows, width),),
            in_specs=[pl.BlockSpec(memory_space=pltpu.HBM)] * 4,
            out_specs=(vmem,) * 8,
            scratch_shapes=[pltpu.VMEM((cells, rows), jnp.int32), pltpu.VMEM((cells, rows), jnp.int32),
                            pltpu.SemaphoreType.DMA((4,))],
            compiler_params=params,
            name="start",
        )(*(pltpu.with_memory_space_constraint(v, pltpu.HBM)
            for v in (fluid_temp, fin_temp, owners, targets)))

        def around(size, step):
            return [(i, (i + step) % size) for i in range(size)]

        swap = [(0, 1), (1, 0)]
        prev = lax.ppermute(gxf, "gx", around(count, 1))
        nxt = lax.ppermute(gxb, "gx", around(count, -1))
        if ring:
            walls = [wall] + [lax.ppermute(wall, "gx", around(count, k)) for k in range(2, count - 1)]
        else:
            walls = [wall, lax.all_gather(wall, "gx")]
        below = lax.ppermute(grpf, "grp", around(groups, 1))
        above = lax.ppermute(grpb, "grp", around(groups, -1))
        side = lax.ppermute(gyx, "gy", swap)

        def middle_kernel(*refs):
            (act, src, prev, nxt, below, above, side), refs = refs[2:9], refs[9:]
            wall_refs, refs = refs[: len(walls)], refs[len(walls) :]
            fluid, fin, first, rest, ghost_out, gxf, gxb, grpf, grpb, gyx = refs[:10]
            zrows, zedge, other, deposit = refs[10:]
            place = [lax.axis_index(name) for name in ("grp", "gx", "gy")]
            grp, gx, gy = place
            on_wall = grp == 0
            own = wall_refs[0]
            own_code = own[fin_rows:, LANES:]
            if ring:
                slots = [(gx, own, 0), ((gx + count - 1) % count, prev, face_rows),
                         ((gx + 1) % count, nxt, face_rows)]
                slots += [((gx + count - k) % count, ref, 0) for k, ref in
                          zip(range(2, count - 1), wall_refs[1:])]
                slots = [(o, ref.at[pl.ds(base, wall_rows), :]) for o, ref, base in slots]
            else:
                slots = [(s, wall_refs[1].at[s]) for s in range(count)]
            quadrants = [(a * cells, b * LANES) for a in range(2) for b in range(2)]
            ghost = jnp.zeros((cells, rows), jnp.float32)
            deposits = [jnp.zeros((cells, rows), jnp.float32) for _ in quadrants]
            mine = (4 * gx).astype(jnp.float32)
            for owner, ref in slots:
                theirs = own_code - (4 * jnp.asarray(owner, jnp.int32)).astype(jnp.float32)
                temps = ref[fin_rows:, 0:LANES]
                wanted = ref[fin_rows:, LANES:] - mine
                for q, (r, c) in enumerate(quadrants):
                    ghost = jnp.where(theirs == q, ref[r : r + cells, c : c + LANES], ghost)
                    flux = HEAT_COEF * (temps - own[r : r + cells, c : c + LANES])
                    deposits[q] = deposits[q] + jnp.where(wanted == q, flux, 0.0)
            ghost_out[...] = ghost

            @pl.when(on_wall)
            def _():
                split = jnp.concatenate(
                    [jnp.concatenate(deposits[0:2], axis=1), jnp.concatenate(deposits[2:4], axis=1)],
                    axis=0,
                )
                mixed = dot(split, interleave_matrix(fin_width), ((1,), (1,)))
                deposit[...] = dot(interleave_matrix(fin_rows), mixed, ((1,), (0,)))

            @pl.when(jnp.logical_not(on_wall))
            def _():
                deposit[...] = jnp.zeros((fin_rows, fin_width), jnp.float32)

            low_face = jnp.where(on_wall, ghost, below[0:cells, 0:LANES])
            unpack_halos(fluid, fin, zrows, zedge, prev, nxt, below, above, side, low_face, 0,
                         place, sizes, dims)
            fluid_sweep(fluid, act, zedge, other, 0, dims)
            hedge = side[cells : cells + fin_rows, 0:LANES]

            def layer(d):
                here, total = fin_neighbours(fin, d, hedge, fin_rows)
                rhs = here + src[d]
                first[d + 1, PAD : PAD + fin_rows, :] = (rhs + FIN_CONDUCTION * total) * (1.0 / DIAG)
                rest[d] = rhs * (OMEGA / DIAG) + here * (1.0 - OMEGA)

            repeat(depth, layer)
            first[1, PAD : PAD + fin_rows, :] += deposit[...] * (1.0 / DIAG)
            rest[0] += deposit[...] * (OMEGA / DIAG)
            pack_faces(fluid, first, 0, gxf, gxb, grpf, grpb, gyx, gy, dims)

        received = (prev, nxt, below, above, side)
        scratch = [
            pltpu.VMEM((LANES, rows), jnp.float32),
            pltpu.VMEM((rows, LANES), jnp.float32),
            pltpu.VMEM((rows + 2 * PAD, width), jnp.float32),
        ]
        outs = pl.pallas_call(
            middle_kernel,
            out_shape=(fluid_pad, fin_pad, fin_pad, f32(depth, fin_rows, fin_width),
                       f32(cells, rows), f32(face_rows, width), f32(face_rows, width)) + faces,
            in_specs=[vmem] * (9 + len(walls)),
            out_specs=(vmem,) * 10,
            scratch_shapes=scratch + [pltpu.VMEM((fin_rows, fin_width), jnp.float32)],
            input_output_aliases={0: 0, 1: 1},
            compiler_params=params,
            name="middle",
        )(fluid0, fin0, active, fin_source, *received, *walls)
        fluid1, _, first, rest, ghost, gxf, gxb, grpf, grpb, gyx = outs

        prev = lax.ppermute(gxf, "gx", around(count, 1))
        nxt = lax.ppermute(gxb, "gx", around(count, -1))
        below = lax.ppermute(grpf, "grp", around(groups, 1))
        above = lax.ppermute(grpb, "grp", around(groups, -1))
        side = lax.ppermute(gyx, "gy", swap)

        def end_kernel(_0, _1, _2, act, ghost, prev, nxt, below, above, side,
                       fluid, first, rest, fluid_new, fin_new,
                       zrows, zedge, other, fluid_sems, fin_sems):
            place = [lax.axis_index(name) for name in ("grp", "gx", "gy")]
            on_wall = place[0] == 0
            low_face = jnp.where(on_wall, ghost[...], below[0:cells, 0:LANES])
            unpack_halos(fluid, first, zrows, zedge, prev, nxt, below, above, side, low_face, 1,
                         place, sizes, dims)
            hedge = side[cells : cells + fin_rows, 0:LANES]

            def fluid_copy(k):
                return pltpu.make_async_copy(
                    fluid.at[pl.ds(2 * k + 1, 2), pl.ds(PAD, rows), :],
                    fluid_new.at[pl.ds(2 * k, 2)], fluid_sems.at[k],
                )

            def fin_copy(k):
                part = pl.ds(k * 8, 8)
                return pltpu.make_async_copy(rest.at[part], fin_new.at[part], fin_sems.at[k])

            fluid_sweep(fluid, act, zedge, other, 1, dims, lambda k: fluid_copy(k).start())

            def layers(k, carry):
                for j in range(8):
                    d = k * 8 + j
                    _, total = fin_neighbours(first, d, hedge, fin_rows)
                    rest[d] = rest[d] + (OMEGA * FIN_CONDUCTION / DIAG) * total
                fin_copy(k).start()
                return carry

            lax.fori_loop(0, depth // 8, layers, 0)

            def finish_fluid(i, carry):
                fluid_copy(i).wait()
                return carry

            def finish_fin(d, carry):
                fin_copy(d).wait()
                return carry

            lax.fori_loop(0, cells // 2, finish_fluid, 0)
            lax.fori_loop(0, depth // 8, finish_fin, 0)

        results = pl.pallas_call(
            end_kernel,
            out_shape=(fluid_pad, fin_pad, f32(depth, fin_rows, fin_width),
                       f32(cells, rows, width), f32(depth, fin_rows, fin_width)),
            in_specs=[vmem] * 10,
            out_specs=(vmem, vmem, vmem, hbm, hbm),
            scratch_shapes=scratch + [pltpu.SemaphoreType.DMA((cells // 2,)),
                                      pltpu.SemaphoreType.DMA((depth // 8,))],
            input_output_aliases={0: 0, 1: 1, 2: 2},
            compiler_params=params,
            name="end",
        )(fluid1, first, rest, active, ghost, prev, nxt, below, above, side)
        return results[3], results[4]

    return jax.shard_map(local, mesh=mesh, in_specs=in_specs, out_specs=out_specs, check_vma=False)
```

```python
import jax
import jax.numpy as jnp
from jax import lax
from jax.experimental import pallas as pl
from jax.experimental.pallas import tpu as pltpu
from jax.sharding import PartitionSpec as P

FLUID_DIFFUSION = 1.0
FIN_CONDUCTION = 1.0
HEAT_COEF = 1.0
DIAG = 1.0 + 6.0 * FIN_CONDUCTION
SPECTRAL = 6.0 * FIN_CONDUCTION / DIAG
OMEGA = 1.0 / (1.0 - SPECTRAL * SPECTRAL / 2.0)
FLUID_SCALE = 1.0 / (1.0 + 6.0 * FLUID_DIFFUSION)
LANES = 128
PAD = 8
ROWS = 32
HIGHEST = lax.Precision.HIGHEST


def iota(shape, axis):
    return lax.broadcasted_iota(jnp.int32, shape, axis)


def repeat(count, body, step=8):
    def trip(k, carry):
        for j in range(step):
            body(k * step + j)
        return carry

    lax.fori_loop(0, count // step, trip, 0)


def tiles(value):
    return [value[:, k : k + LANES] for k in range(0, value.shape[1], LANES)]


def lane_neighbours(block, low, high):
    parts = tiles(block)
    lane = iota(parts[0].shape, 1)
    down = [pltpu.roll(part, 1, axis=1) for part in parts]
    up = [pltpu.roll(part, LANES - 1, axis=1) for part in parts]
    below = [jnp.where(lane == 0, a, b) for a, b in zip([low] + down[:-1], down)]
    above = [jnp.where(lane == LANES - 1, a, b) for a, b in zip(up[1:] + [high], up)]
    return jnp.concatenate([a + b for a, b in zip(below, above)], axis=1)


def interleave_matrix(count):
    row = iota((count, count), 0)
    col = iota((count, count), 1)
    half = count // 2
    source = jnp.where(col < half, 2 * col, 2 * (col - half) + 1)
    return (row == source).astype(jnp.float32)


def dot(a, b, contract):
    return lax.dot_general(
        a, b, (contract, ((), ())), precision=HIGHEST, preferred_element_type=jnp.float32
    )


def checker_pack(plane, parity):
    rows = plane.shape[0] // 2
    top = plane[:rows]
    bottom = plane[rows:]
    colour = (iota(top.shape, 0) + iota(top.shape, 1)) & 1
    return jnp.where(colour == parity, top, pltpu.roll(bottom, 1, axis=1))


def lane_column(column, cells, rows):
    kept = jnp.zeros((rows, LANES), jnp.float32)
    lane = iota((rows, LANES), 1)
    for i in range(cells):
        kept = jnp.where(lane == i, column(i), kept)
    return kept.T[:cells]


def pack_gx(low_plane, high_plane, low_row, high_row, colour, gxf, gxb, dims):
    cells, rows, width, depth, fin_rows, fin_width = dims
    half = rows // 2
    gxf[0:half, :] = checker_pack(high_plane, (colour + cells - 1) % 2)
    gxb[0:half, :] = checker_pack(low_plane, colour)

    def lines(d):
        gxf[pl.ds(half + d, 1), :] = high_row(d)
        gxb[pl.ds(half + d, 1), :] = low_row(d)

    repeat(depth, lines)


def pack_rest(fluid, fin, grpf, grpb, gyx, gy, dims):
    cells, rows, width, depth, fin_rows, fin_width = dims
    for send, lane, layer in ((grpf, width - 1, depth), (grpb, 0, 1)):
        send[0:cells, 0:LANES] = lane_column(
            lambda i: fluid[i + 1, PAD : PAD + rows, lane : lane + 1], cells, rows
        )
        send[cells : cells + fin_rows, :] = fin[layer, PAD : PAD + fin_rows, :]
    edge = PAD + (1 - gy) * (rows - 1)
    for i in range(cells):
        gyx[i : i + 1, :] = fluid[i + 1, pl.ds(edge, 1), :]
    lane = iota((fin_rows, LANES), 1)

    def columns(at, side):
        kept = jnp.zeros((fin_rows, LANES), jnp.float32)
        for d in range(depth):
            column = fin[d + 1, PAD : PAD + fin_rows, at : at + 1]
            kept = jnp.where(lane == 2 * d + side, column, kept)
        gyx[cells : cells + fin_rows, 0:LANES] = kept

    @pl.when(gy == 0)
    def _():
        columns(fin_width - 1, 1)

    @pl.when(gy != 0)
    def _():
        columns(0, 0)


def unpack_halos(fluid, fin, zrows, zedge, prev, nxt, below, above, side, low_face, colour,
                 place, sizes, dims):
    cells, rows, width, depth, fin_rows, fin_width = dims
    half = rows // 2
    grp, gx, gy = place
    groups, count = sizes
    below_on = jnp.where(grp == 0, 0.0, 1.0)
    above_on = jnp.where(grp == groups - 1, 0.0, 1.0)
    prev_on = jnp.where(gx == 0, 0.0, 1.0)
    next_on = jnp.where(gx == count - 1, 0.0, 1.0)
    for plane, ref, on in ((0, prev, prev_on), (cells + 1, nxt, next_on)):
        packed = ref[0:half, :] * on
        fluid[plane, PAD : PAD + half, :] = packed
        fluid[plane, PAD + half : PAD + rows, :] = pltpu.roll(packed, width - 1, axis=1)
    low_on = jnp.where(gy == 0, 0.0, 1.0)
    high_on = 1.0 - low_on
    for i in range(cells):
        line = side[i : i + 1, :]
        fluid[i + 1, PAD - 1 : PAD, :] = line * low_on
        fluid[i + 1, PAD + rows : PAD + rows + 1, :] = line * high_on
    high_face = above[0:cells, 0:LANES] * above_on
    odd_row = (iota((1, rows), 1) & 1) == 1
    for k in range(cells // 2):
        for lane, face, swap in ((2 * k, high_face, colour == 1), (2 * k + 1, low_face, colour == 0)):
            first, second = face[2 * k : 2 * k + 1, :], face[2 * k + 1 : 2 * k + 2, :]
            zrows[lane : lane + 1, :] = jnp.where(odd_row == swap, second, first)
    zrows[cells:, :] = jnp.zeros((LANES - cells, rows), jnp.float32)
    zedge[...] = zrows[...].T
    fin[0, PAD : PAD + fin_rows, :] = below[cells : cells + fin_rows, :] * below_on
    fin[depth + 1, PAD : PAD + fin_rows, :] = above[cells : cells + fin_rows, :] * above_on

    def line_of(d):
        fin[d + 1, PAD - 1 : PAD, :] = prev[pl.ds(half + d, 1), :] * prev_on
        fin[d + 1, PAD + fin_rows : PAD + fin_rows + 1, :] = nxt[pl.ds(half + d, 1), :] * next_on

    repeat(depth, line_of)


def fluid_sweep(fluid, active, zedge, other, colour, dims, pairs, done=None):
    cells, rows, width, depth, fin_rows, fin_width = dims
    parity = (iota((ROWS, width), 0) + iota((ROWS, width), 1)) & 1
    updating = parity == colour
    off = parity ^ colour
    end_parity = iota((1, width), 1) & 1

    first_pair, step, count = pairs

    def pair(j, carry):
        k = first_pair + step * j
        a, b = 2 * k + 1, 2 * k + 2
        for at, swap in ((PAD - 1, 1 - colour), (PAD + rows, colour)):
            line = slice(at, at + 1)
            other[line, :] = jnp.where(end_parity == swap, fluid[b, line, :], fluid[a, line, :])
        for start in range(0, rows, ROWS):
            inner = slice(PAD + start, PAD + start + ROWS)
            other[inner, :] = jnp.where(updating, fluid[b, inner, :], fluid[a, inner, :])
        for start in range(0, rows, ROWS):
            inner = slice(PAD + start, PAD + start + ROWS)
            edge = pltpu.roll(zedge[start : start + ROWS, :], LANES - 1 - 2 * k, axis=1)
            shared = (
                other[PAD + start - 1 : PAD + start + ROWS - 1, :]
                + other[PAD + start + 1 : PAD + start + ROWS + 1, :]
                + lane_neighbours(other[inner, :], edge, edge)
            )
            here_a = fluid[a, inner, :]
            here_b = fluid[b, inner, :]
            total_a = shared + fluid[a - 1, inner, :] + here_b
            total_b = shared + fluid[b + 1, inner, :] + here_a
            new_a = (here_a + FLUID_DIFFUSION * total_a) * FLUID_SCALE
            new_b = (here_b + FLUID_DIFFUSION * total_b) * FLUID_SCALE
            mask_a = active[a - 1, start : start + ROWS, :] > off
            mask_b = active[b - 1, start : start + ROWS, :] > 1 - off
            fluid[a, inner, :] = jnp.where(mask_a, new_a, here_a)
            fluid[b, inner, :] = jnp.where(mask_b, new_b, here_b)
        if done is not None:
            done(k)
        return carry

    lax.fori_loop(0, count, pair, 0)


def fin_neighbours(fin, d, hedge, fin_rows):
    inner = slice(PAD, PAD + fin_rows)
    here = fin[d + 1, inner, :]
    edge = pltpu.roll(hedge, LANES - 1 - 2 * d, axis=1)
    total = (
        fin[d, inner, :]
        + fin[d + 2, inner, :]
        + fin[d + 1, PAD - 1 : PAD + fin_rows - 1, :]
        + fin[d + 1, PAD + 1 : PAD + fin_rows + 1, :]
        + lane_neighbours(here, edge, edge)
    )
    return here, total


def solution(mesh):
    in_specs = (
        P("gx", "gy", "grp"),
        P("gx", "gy", "grp"),
        P("grp", "gx", "gy"),
        P("grp", "gx", "gy"),
        P("gx", "gy", None, None),
        P("gx", "gy", None),
    )
    out_specs = (P("gx", "gy", "grp"), P("grp", "gx", "gy"))
    count = mesh.shape["gx"]
    groups = mesh.shape["grp"]
    sides = mesh.shape["gy"]
    assert sides == 2
    ring = count == 4
    vmem = pl.BlockSpec(memory_space=pltpu.VMEM)
    hbm = pl.BlockSpec(memory_space=pl.ANY)

    def local(fluid_temp, active, fin_temp, fin_source, wall_owner, wall_target):
        cells, rows, width = fluid_temp.shape
        depth, fin_rows, fin_width = fin_temp.shape
        assert rows == LANES and width == fin_width == 2 * rows and fin_rows == 2 * cells
        assert 2 * depth <= LANES and depth % 8 == 0 and cells % 2 == 0 and cells >= 4 and rows % ROWS == 0 and fin_rows == ROWS
        dims = (cells, rows, width, depth, fin_rows, fin_width)
        sizes = (groups, count)
        half = rows // 2
        pairs = cells // 2
        face_rows = half + depth
        wall_rows = fin_rows + cells
        small_rows = cells + fin_rows
        gx_rows = face_rows + (wall_rows if ring else 0)
        owners = wall_owner.reshape(cells, rows)
        targets = wall_target.reshape(cells, rows)
        f32 = lambda *shape: jax.ShapeDtypeStruct(shape, jnp.float32)
        params = pltpu.CompilerParams(vmem_limit_bytes=32 * 1024 * 1024)
        fluid_pad = f32(cells + 2, rows + 2 * PAD, width)
        fin_pad = f32(depth + 2, fin_rows + 2 * PAD, fin_width)
        faces = (f32(small_rows, width), f32(small_rows, width), f32(small_rows, width))

        def start_gx_kernel(fluid_hbm, fin_hbm, own_hbm, tgt_hbm, gxf, gxb, wall,
                            planes, bottom, low_rows, high_rows, root, own, tgt, sems):
            last = cells - 1
            copies = [
                pltpu.make_async_copy(source, target, sems.at[k])
                for k, (source, target) in enumerate((
                    (own_hbm, own),
                    (tgt_hbm, tgt),
                    (fluid_hbm.at[:, :, pl.ds(0, LANES)], bottom),
                    (fin_hbm.at[0], root),
                    (fluid_hbm.at[0], planes.at[0]),
                    (fluid_hbm.at[last], planes.at[1]),
                    (fin_hbm.at[:, pl.ds(0, PAD), :], low_rows),
                    (fin_hbm.at[:, pl.ds(fin_rows - PAD, PAD), :], high_rows),
                ))
            ]
            for copy in copies:
                copy.start()
            for copy in copies:
                copy.wait()
            shape = (cells, rows)
            shift = tgt[...] - 2 * (iota(shape, 0) * fin_width + iota(shape, 1))
            row_shift = (shift >= fin_width).astype(jnp.int32)
            code = own[...] * 4 + row_shift * 2 + (shift - row_shift * fin_width)
            wall[fin_rows:, LANES:] = code.astype(jnp.float32)
            wall[fin_rows:, 0:LANES] = lane_column(lambda i: bottom[i, :, 0:1], cells, rows)
            even_rows = dot(interleave_matrix(fin_rows), root[...], ((0,), (0,)))
            wall[0:fin_rows, :] = dot(even_rows, interleave_matrix(fin_width), ((1,), (0,)))
            pack_gx(planes[0], planes[1], lambda d: low_rows[d, 0:1, :],
                    lambda d: high_rows[d, PAD - 1 : PAD, :], 1, gxf, gxb, dims)
            if ring:
                gxf[face_rows:, :] = wall[...]
                gxb[face_rows:, :] = wall[...]

        fluid_hbm, fin_hbm, owners, targets = (
            pltpu.with_memory_space_constraint(v, pltpu.HBM)
            for v in (fluid_temp, fin_temp, owners, targets)
        )
        in_hbm = pl.BlockSpec(memory_space=pltpu.HBM)
        buffer = lambda *shape: pltpu.VMEM(shape, jnp.float32)
        gxf, gxb, wall = pl.pallas_call(
            start_gx_kernel,
            out_shape=(f32(gx_rows, width), f32(gx_rows, width), f32(wall_rows, width)),
            in_specs=[in_hbm] * 4,
            out_specs=(vmem,) * 3,
            scratch_shapes=[buffer(2, rows, width), buffer(cells, rows, LANES),
                            buffer(depth, PAD, fin_width), buffer(depth, PAD, fin_width),
                            buffer(fin_rows, fin_width), pltpu.VMEM((cells, rows), jnp.int32),
                            pltpu.VMEM((cells, rows), jnp.int32), pltpu.SemaphoreType.DMA((8,))],
            compiler_params=params,
            name="start_gx",
        )(fluid_hbm, fin_hbm, owners, targets)

        def start_rest_kernel(fluid_hbm, fin_hbm, _, fluid, fin, grpf, grpb, gyx, sems):
            copies = (
                pltpu.make_async_copy(
                    fluid_hbm, fluid.at[pl.ds(1, cells), pl.ds(PAD, rows), :], sems.at[0]
                ),
                pltpu.make_async_copy(
                    fin_hbm, fin.at[pl.ds(1, depth), pl.ds(PAD, fin_rows), :], sems.at[1]
                ),
            )
            for copy in copies:
                copy.start()
            for copy in copies:
                copy.wait()
            pack_rest(fluid, fin, grpf, grpb, gyx, lax.axis_index("gy"), dims)

        fluid0, fin0, grpf, grpb, gyx = pl.pallas_call(
            start_rest_kernel,
            out_shape=(fluid_pad, fin_pad) + faces,
            in_specs=[in_hbm, in_hbm, vmem],
            out_specs=(vmem,) * 5,
            scratch_shapes=[pltpu.SemaphoreType.DMA((2,))],
            compiler_params=params,
            name="start_rest",
        )(fluid_hbm, fin_hbm, wall)

        def around(size, step):
            return [(i, (i + step) % size) for i in range(size)]

        swap = [(0, 1), (1, 0)]
        prev = lax.ppermute(gxf, "gx", around(count, 1))
        nxt = lax.ppermute(gxb, "gx", around(count, -1))
        if ring:
            walls = [wall] + [lax.ppermute(wall, "gx", around(count, k)) for k in range(2, count - 1)]
        else:
            walls = [wall, lax.all_gather(wall, "gx")]
        below = lax.ppermute(grpf, "grp", around(groups, 1))
        above = lax.ppermute(grpb, "grp", around(groups, -1))
        side = lax.ppermute(gyx, "gy", swap)

        def middle_kernel(*refs):
            (act, src, prev, nxt, below, above, side), refs = refs[2:9], refs[9:]
            wall_refs, refs = refs[: len(walls)], refs[len(walls) :]
            fluid, fin, first, rest, ghost_out, zedge, gxf, gxb = refs[:8]
            zrows, other, deposit = refs[8:]
            place = [lax.axis_index(name) for name in ("grp", "gx", "gy")]
            grp, gx, gy = place
            on_wall = grp == 0
            own = wall_refs[0]
            own_code = own[fin_rows:, LANES:]
            if ring:
                slots = [(gx, own, 0), ((gx + count - 1) % count, prev, face_rows),
                         ((gx + 1) % count, nxt, face_rows)]
                slots += [((gx + count - k) % count, ref, 0) for k, ref in
                          zip(range(2, count - 1), wall_refs[1:])]
                slots = [(o, ref.at[pl.ds(base, wall_rows), :]) for o, ref, base in slots]
            else:
                slots = [(s, wall_refs[1].at[s]) for s in range(count)]
            quadrants = [(a * cells, b * LANES) for a in range(2) for b in range(2)]
            ghost = jnp.zeros((cells, rows), jnp.float32)
            deposits = [jnp.zeros((cells, rows), jnp.float32) for _ in quadrants]
            mine = (4 * gx).astype(jnp.float32)
            for owner, ref in slots:
                theirs = own_code - (4 * jnp.asarray(owner, jnp.int32)).astype(jnp.float32)
                temps = ref[fin_rows:, 0:LANES]
                wanted = ref[fin_rows:, LANES:] - mine
                for q, (r, c) in enumerate(quadrants):
                    ghost = jnp.where(theirs == q, ref[r : r + cells, c : c + LANES], ghost)
                    flux = HEAT_COEF * (temps - own[r : r + cells, c : c + LANES])
                    deposits[q] = deposits[q] + jnp.where(wanted == q, flux, 0.0)
            ghost_out[...] = ghost

            @pl.when(on_wall)
            def _():
                split = jnp.concatenate(
                    [jnp.concatenate(deposits[0:2], axis=1), jnp.concatenate(deposits[2:4], axis=1)],
                    axis=0,
                )
                mixed = dot(split, interleave_matrix(fin_width), ((1,), (1,)))
                deposit[...] = dot(interleave_matrix(fin_rows), mixed, ((1,), (0,)))

            @pl.when(jnp.logical_not(on_wall))
            def _():
                deposit[...] = jnp.zeros((fin_rows, fin_width), jnp.float32)

            low_face = jnp.where(on_wall, ghost, below[0:cells, 0:LANES])
            unpack_halos(fluid, fin, zrows, zedge, prev, nxt, below, above, side, low_face, 0,
                         place, sizes, dims)
            fluid_sweep(fluid, act, zedge, other, 0, dims, (0, pairs - 1, 2))
            hedge = side[cells : cells + fin_rows, 0:LANES]

            def layer(d):
                here, total = fin_neighbours(fin, d, hedge, fin_rows)
                rhs = here + src[d]
                first[d + 1, PAD : PAD + fin_rows, :] = (rhs + FIN_CONDUCTION * total) * (1.0 / DIAG)
                rest[d] = rhs * (OMEGA / DIAG) + here * (1.0 - OMEGA)

            repeat(depth, layer)
            first[1, PAD : PAD + fin_rows, :] += deposit[...] * (1.0 / DIAG)
            rest[0] += deposit[...] * (OMEGA / DIAG)
            inner = slice(PAD, PAD + rows)
            top, bottom = slice(PAD, PAD + 1), slice(PAD + fin_rows - 1, PAD + fin_rows)
            pack_gx(fluid[1, inner, :], fluid[cells, inner, :], lambda d: first[d + 1, top, :],
                    lambda d: first[d + 1, bottom, :], 0, gxf, gxb, dims)

        received = (prev, nxt, below, above, side)
        zrows_buffer, zedge_buffer = buffer(LANES, rows), buffer(rows, LANES)
        other_buffer = buffer(rows + 2 * PAD, width)
        outs = pl.pallas_call(
            middle_kernel,
            out_shape=(fluid_pad, fin_pad, fin_pad, f32(depth, fin_rows, fin_width),
                       f32(cells, rows), f32(rows, LANES), f32(face_rows, width),
                       f32(face_rows, width)),
            in_specs=[vmem] * (9 + len(walls)),
            out_specs=(vmem,) * 8,
            scratch_shapes=[zrows_buffer, other_buffer, buffer(fin_rows, fin_width)],
            input_output_aliases={0: 0, 1: 1},
            compiler_params=params,
            name="middle_gx",
        )(fluid0, fin0, active, fin_source, *received, *walls)
        fluid1, _, first, rest, ghost, zedge, gxf, gxb = outs

        def middle_rest_kernel(_, act, zedge, first, fluid, grpf, grpb, gyx, other):
            fluid_sweep(fluid, act, zedge, other, 0, dims, (1, 1, pairs - 2))
            pack_rest(fluid, first, grpf, grpb, gyx, lax.axis_index("gy"), dims)

        fluid2, grpf, grpb, gyx = pl.pallas_call(
            middle_rest_kernel,
            out_shape=(fluid_pad,) + faces,
            in_specs=[vmem] * 4,
            out_specs=(vmem,) * 4,
            scratch_shapes=[other_buffer],
            input_output_aliases={0: 0},
            compiler_params=params,
            name="middle_rest",
        )(fluid1, active, zedge, first)

        prev = lax.ppermute(gxf, "gx", around(count, 1))
        nxt = lax.ppermute(gxb, "gx", around(count, -1))
        below = lax.ppermute(grpf, "grp", around(groups, 1))
        above = lax.ppermute(grpb, "grp", around(groups, -1))
        side = lax.ppermute(gyx, "gy", swap)

        def end_kernel(_0, _1, _2, act, ghost, prev, nxt, below, above, side,
                       fluid, first, rest, fluid_new, fin_new,
                       zrows, zedge, other, fluid_sems, fin_sems):
            place = [lax.axis_index(name) for name in ("grp", "gx", "gy")]
            on_wall = place[0] == 0
            low_face = jnp.where(on_wall, ghost[...], below[0:cells, 0:LANES])
            unpack_halos(fluid, first, zrows, zedge, prev, nxt, below, above, side, low_face, 1,
                         place, sizes, dims)
            hedge = side[cells : cells + fin_rows, 0:LANES]

            def fluid_copy(k):
                return pltpu.make_async_copy(
                    fluid.at[pl.ds(2 * k + 1, 2), pl.ds(PAD, rows), :],
                    fluid_new.at[pl.ds(2 * k, 2)], fluid_sems.at[k],
                )

            def fin_copy(k):
                part = pl.ds(k * 8, 8)
                return pltpu.make_async_copy(rest.at[part], fin_new.at[part], fin_sems.at[k])

            fluid_sweep(fluid, act, zedge, other, 1, dims, (0, 1, pairs),
                        lambda k: fluid_copy(k).start())

            def layers(k, carry):
                for j in range(8):
                    d = k * 8 + j
                    _, total = fin_neighbours(first, d, hedge, fin_rows)
                    rest[d] = rest[d] + (OMEGA * FIN_CONDUCTION / DIAG) * total
                fin_copy(k).start()
                return carry

            lax.fori_loop(0, depth // 8, layers, 0)

            def finish_fluid(i, carry):
                fluid_copy(i).wait()
                return carry

            def finish_fin(d, carry):
                fin_copy(d).wait()
                return carry

            lax.fori_loop(0, cells // 2, finish_fluid, 0)
            lax.fori_loop(0, depth // 8, finish_fin, 0)

        results = pl.pallas_call(
            end_kernel,
            out_shape=(fluid_pad, fin_pad, f32(depth, fin_rows, fin_width),
                       f32(cells, rows, width), f32(depth, fin_rows, fin_width)),
            in_specs=[vmem] * 10,
            out_specs=(vmem, vmem, vmem, hbm, hbm),
            scratch_shapes=[zrows_buffer, zedge_buffer, other_buffer,
                            pltpu.SemaphoreType.DMA((cells // 2,)),
                                      pltpu.SemaphoreType.DMA((depth // 8,))],
            input_output_aliases={0: 0, 1: 1, 2: 2},
            compiler_params=params,
            name="end",
        )(fluid2, first, rest, active, ghost, prev, nxt, below, above, side)
        return results[3], results[4]

    return jax.shard_map(local, mesh=mesh, in_specs=in_specs, out_specs=out_specs, check_vma=False)
```

```python
import jax
import jax.numpy as jnp
from jax import lax
from jax.experimental import pallas as pl
from jax.experimental.pallas import tpu as pltpu
from jax.sharding import PartitionSpec as P

FLUID_DIFFUSION = 1.0
FIN_CONDUCTION = 1.0
HEAT_COEF = 1.0
DIAG = 1.0 + 6.0 * FIN_CONDUCTION
SPECTRAL = 6.0 * FIN_CONDUCTION / DIAG
OMEGA = 1.0 / (1.0 - SPECTRAL * SPECTRAL / 2.0)
FLUID_SCALE = 1.0 / (1.0 + 6.0 * FLUID_DIFFUSION)
LANES = 128
PAD = 8
ROWS = 32
HIGHEST = lax.Precision.HIGHEST


def iota(shape, axis):
    return lax.broadcasted_iota(jnp.int32, shape, axis)


def repeat(count, body, step=8):
    def trip(k, carry):
        for j in range(step):
            body(k * step + j)
        return carry

    lax.fori_loop(0, count // step, trip, 0)


def tiles(value):
    return [value[:, k : k + LANES] for k in range(0, value.shape[1], LANES)]


def lane_neighbours(block, low, high):
    parts = tiles(block)
    lane = iota(parts[0].shape, 1)
    down = [pltpu.roll(part, 1, axis=1) for part in parts]
    up = [pltpu.roll(part, LANES - 1, axis=1) for part in parts]
    below = [jnp.where(lane == 0, a, b) for a, b in zip([low] + down[:-1], down)]
    above = [jnp.where(lane == LANES - 1, a, b) for a, b in zip(up[1:] + [high], up)]
    return jnp.concatenate([a + b for a, b in zip(below, above)], axis=1)


def interleave_matrix(count):
    row = iota((count, count), 0)
    col = iota((count, count), 1)
    half = count // 2
    source = jnp.where(col < half, 2 * col, 2 * (col - half) + 1)
    return (row == source).astype(jnp.float32)


def dot(a, b, contract):
    return lax.dot_general(
        a, b, (contract, ((), ())), precision=HIGHEST, preferred_element_type=jnp.float32
    )


def checker_pack(plane, parity):
    rows = plane.shape[0] // 2
    top = plane[:rows]
    bottom = plane[rows:]
    colour = (iota(top.shape, 0) + iota(top.shape, 1)) & 1
    return jnp.where(colour == parity, top, pltpu.roll(bottom, 1, axis=1))


def lane_column(column, cells, rows):
    kept = jnp.zeros((rows, LANES), jnp.float32)
    lane = iota((rows, LANES), 1)
    for i in range(cells):
        kept = jnp.where(lane == i, column(i), kept)
    return kept.T[:cells]


def pack_gx(low_plane, high_plane, low_row, high_row, colour, gxf, gxb, dims):
    cells, rows, width, depth, fin_rows, fin_width = dims
    half = rows // 2
    gxf[0:half, :] = checker_pack(high_plane, (colour + cells - 1) % 2)
    gxb[0:half, :] = checker_pack(low_plane, colour)

    def lines(d):
        gxf[pl.ds(half + d, 1), :] = high_row(d)
        gxb[pl.ds(half + d, 1), :] = low_row(d)

    repeat(depth, lines)


def pack_rest(fluid, fin, grpa, grpb, gyx, place, dims):
    cells, rows, width, depth, fin_rows, fin_width = dims
    grp, gx, gy = place
    even = grp % 2 == 0
    low, high = (
        lane_column(lambda i: fluid[i + 1, PAD : PAD + rows, k : k + 1], cells, rows)
        for k in (0, width - 1)
    )
    grpa[0:cells, 0:LANES] = jnp.where(even, high, low)
    grpb[0:cells, 0:LANES] = jnp.where(even, low, high)
    up = jnp.where(even, depth, 1)
    grpa[cells : cells + fin_rows, :] = fin[up, PAD : PAD + fin_rows, :]
    grpb[cells : cells + fin_rows, :] = fin[depth + 1 - up, PAD : PAD + fin_rows, :]
    edge = PAD + (1 - gy) * (rows - 1)
    for i in range(cells):
        gyx[i : i + 1, :] = fluid[i + 1, pl.ds(edge, 1), :]
    lane = iota((fin_rows, LANES), 1)

    def columns(at, side):
        kept = jnp.zeros((fin_rows, LANES), jnp.float32)
        for d in range(depth):
            column = fin[d + 1, PAD : PAD + fin_rows, at : at + 1]
            kept = jnp.where(lane == 2 * d + side, column, kept)
        gyx[cells : cells + fin_rows, 0:LANES] = kept

    @pl.when(gy == 0)
    def _():
        columns(fin_width - 1, 1)

    @pl.when(gy != 0)
    def _():
        columns(0, 0)


def my_place():
    return [lax.axis_index(name) for name in ("grp", "gx", "gy")]


def grp_halos(paira, pairb, grp):
    even = grp % 2 == 0
    a, b = paira[...], pairb[...]
    return jnp.where(even, b, a), jnp.where(even, a, b)


def unpack_halos(fluid, fin, zrows, zedge, prev, nxt, below, above, side, low_face, colour,
                 place, sizes, dims):
    cells, rows, width, depth, fin_rows, fin_width = dims
    half = rows // 2
    grp, gx, gy = place
    groups, count = sizes
    below_on = jnp.where(grp == 0, 0.0, 1.0)
    above_on = jnp.where(grp == groups - 1, 0.0, 1.0)
    prev_on = jnp.where(gx == 0, 0.0, 1.0)
    next_on = jnp.where(gx == count - 1, 0.0, 1.0)
    for plane, ref, on in ((0, prev, prev_on), (cells + 1, nxt, next_on)):
        packed = ref[0:half, :] * on
        fluid[plane, PAD : PAD + half, :] = packed
        fluid[plane, PAD + half : PAD + rows, :] = pltpu.roll(packed, width - 1, axis=1)
    low_on = jnp.where(gy == 0, 0.0, 1.0)
    high_on = 1.0 - low_on
    for i in range(cells):
        line = side[i : i + 1, :]
        fluid[i + 1, PAD - 1 : PAD, :] = line * low_on
        fluid[i + 1, PAD + rows : PAD + rows + 1, :] = line * high_on
    high_face = above[0:cells, 0:LANES] * above_on
    odd_row = (iota((1, rows), 1) & 1) == 1
    for k in range(cells // 2):
        for lane, face, swap in ((2 * k, high_face, colour == 1), (2 * k + 1, low_face, colour == 0)):
            first, second = face[2 * k : 2 * k + 1, :], face[2 * k + 1 : 2 * k + 2, :]
            zrows[lane : lane + 1, :] = jnp.where(odd_row == swap, second, first)
    zrows[cells:, :] = jnp.zeros((LANES - cells, rows), jnp.float32)
    zedge[...] = zrows[...].T
    fin[0, PAD : PAD + fin_rows, :] = below[cells : cells + fin_rows, :] * below_on
    fin[depth + 1, PAD : PAD + fin_rows, :] = above[cells : cells + fin_rows, :] * above_on

    def line_of(d):
        fin[d + 1, PAD - 1 : PAD, :] = prev[pl.ds(half + d, 1), :] * prev_on
        fin[d + 1, PAD + fin_rows : PAD + fin_rows + 1, :] = nxt[pl.ds(half + d, 1), :] * next_on

    repeat(depth, line_of)


def fluid_sweep(fluid, active, zedge, other, colour, dims, pairs, done=None):
    cells, rows, width, depth, fin_rows, fin_width = dims
    parity = (iota((ROWS, width), 0) + iota((ROWS, width), 1)) & 1
    updating = parity == colour
    off = parity ^ colour
    end_parity = iota((1, width), 1) & 1

    first_pair, step, count = pairs

    def pair(j, carry):
        k = first_pair + step * j
        a, b = 2 * k + 1, 2 * k + 2
        for at, swap in ((PAD - 1, 1 - colour), (PAD + rows, colour)):
            line = slice(at, at + 1)
            other[line, :] = jnp.where(end_parity == swap, fluid[b, line, :], fluid[a, line, :])
        for start in range(0, rows, ROWS):
            inner = slice(PAD + start, PAD + start + ROWS)
            other[inner, :] = jnp.where(updating, fluid[b, inner, :], fluid[a, inner, :])
        for start in range(0, rows, ROWS):
            inner = slice(PAD + start, PAD + start + ROWS)
            edge = pltpu.roll(zedge[start : start + ROWS, :], LANES - 1 - 2 * k, axis=1)
            shared = (
                other[PAD + start - 1 : PAD + start + ROWS - 1, :]
                + other[PAD + start + 1 : PAD + start + ROWS + 1, :]
                + lane_neighbours(other[inner, :], edge, edge)
            )
            here_a = fluid[a, inner, :]
            here_b = fluid[b, inner, :]
            total_a = shared + fluid[a - 1, inner, :] + here_b
            total_b = shared + fluid[b + 1, inner, :] + here_a
            new_a = (here_a + FLUID_DIFFUSION * total_a) * FLUID_SCALE
            new_b = (here_b + FLUID_DIFFUSION * total_b) * FLUID_SCALE
            mask_a = active[a - 1, start : start + ROWS, :] > off
            mask_b = active[b - 1, start : start + ROWS, :] > 1 - off
            fluid[a, inner, :] = jnp.where(mask_a, new_a, here_a)
            fluid[b, inner, :] = jnp.where(mask_b, new_b, here_b)
        if done is not None:
            done(k)
        return carry

    lax.fori_loop(0, count, pair, 0)


def fin_neighbours(fin, d, hedge, fin_rows):
    inner = slice(PAD, PAD + fin_rows)
    here = fin[d + 1, inner, :]
    edge = pltpu.roll(hedge, LANES - 1 - 2 * d, axis=1)
    total = (
        fin[d, inner, :]
        + fin[d + 2, inner, :]
        + fin[d + 1, PAD - 1 : PAD + fin_rows - 1, :]
        + fin[d + 1, PAD + 1 : PAD + fin_rows + 1, :]
        + lane_neighbours(here, edge, edge)
    )
    return here, total


def solution(mesh):
    in_specs = (
        P("gx", "gy", "grp"),
        P("gx", "gy", "grp"),
        P("grp", "gx", "gy"),
        P("grp", "gx", "gy"),
        P("gx", "gy", None, None),
        P("gx", "gy", None),
    )
    out_specs = (P("gx", "gy", "grp"), P("grp", "gx", "gy"))
    count = mesh.shape["gx"]
    groups = mesh.shape["grp"]
    sides = mesh.shape["gy"]
    assert sides == 2 and groups % 2 == 0
    ring = count == 4
    vmem = pl.BlockSpec(memory_space=pltpu.VMEM)
    hbm = pl.BlockSpec(memory_space=pl.ANY)

    def local(fluid_temp, active, fin_temp, fin_source, wall_owner, wall_target):
        cells, rows, width = fluid_temp.shape
        depth, fin_rows, fin_width = fin_temp.shape
        assert rows == LANES and width == fin_width == 2 * rows and fin_rows == 2 * cells
        assert 2 * depth <= LANES and depth % 8 == 0 and cells % 2 == 0 and cells >= 4 and rows % ROWS == 0 and fin_rows == ROWS
        dims = (cells, rows, width, depth, fin_rows, fin_width)
        sizes = (groups, count)
        half = rows // 2
        pairs = cells // 2
        face_rows = half + depth
        wall_rows = fin_rows + cells
        small_rows = cells + fin_rows
        gx_rows = face_rows + (wall_rows if ring else 0)
        owners = wall_owner.reshape(cells, rows)
        targets = wall_target.reshape(cells, rows)
        f32 = lambda *shape: jax.ShapeDtypeStruct(shape, jnp.float32)
        params = pltpu.CompilerParams(vmem_limit_bytes=32 * 1024 * 1024)
        fluid_pad = f32(cells + 2, rows + 2 * PAD, width)
        fin_pad = f32(depth + 2, fin_rows + 2 * PAD, fin_width)
        faces = (f32(small_rows, width), f32(small_rows, width), f32(small_rows, width))

        def start_gx_kernel(fluid_hbm, fin_hbm, own_hbm, tgt_hbm, gxf, gxb, wall,
                            planes, bottom, low_rows, high_rows, root, own, tgt, sems):
            last = cells - 1
            copies = [
                pltpu.make_async_copy(source, target, sems.at[k])
                for k, (source, target) in enumerate((
                    (own_hbm, own),
                    (tgt_hbm, tgt),
                    (fluid_hbm.at[:, :, pl.ds(0, LANES)], bottom),
                    (fin_hbm.at[0], root),
                    (fluid_hbm.at[0], planes.at[0]),
                    (fluid_hbm.at[last], planes.at[1]),
                    (fin_hbm.at[:, pl.ds(0, PAD), :], low_rows),
                    (fin_hbm.at[:, pl.ds(fin_rows - PAD, PAD), :], high_rows),
                ))
            ]
            for copy in copies:
                copy.start()
            for copy in copies:
                copy.wait()
            shape = (cells, rows)
            shift = tgt[...] - 2 * (iota(shape, 0) * fin_width + iota(shape, 1))
            row_shift = (shift >= fin_width).astype(jnp.int32)
            code = own[...] * 4 + row_shift * 2 + (shift - row_shift * fin_width)
            wall[fin_rows:, LANES:] = code.astype(jnp.float32)
            wall[fin_rows:, 0:LANES] = lane_column(lambda i: bottom[i, :, 0:1], cells, rows)
            even_rows = dot(interleave_matrix(fin_rows), root[...], ((0,), (0,)))
            wall[0:fin_rows, :] = dot(even_rows, interleave_matrix(fin_width), ((1,), (0,)))
            pack_gx(planes[0], planes[1], lambda d: low_rows[d, 0:1, :],
                    lambda d: high_rows[d, PAD - 1 : PAD, :], 1, gxf, gxb, dims)
            if ring:
                gxf[face_rows:, :] = wall[...]
                gxb[face_rows:, :] = wall[...]

        fluid_hbm, fin_hbm, owners, targets = (
            pltpu.with_memory_space_constraint(v, pltpu.HBM)
            for v in (fluid_temp, fin_temp, owners, targets)
        )
        in_hbm = pl.BlockSpec(memory_space=pltpu.HBM)
        buffer = lambda *shape: pltpu.VMEM(shape, jnp.float32)
        gxf, gxb, wall = pl.pallas_call(
            start_gx_kernel,
            out_shape=(f32(gx_rows, width), f32(gx_rows, width), f32(wall_rows, width)),
            in_specs=[in_hbm] * 4,
            out_specs=(vmem,) * 3,
            scratch_shapes=[buffer(2, rows, width), buffer(cells, rows, LANES),
                            buffer(depth, PAD, fin_width), buffer(depth, PAD, fin_width),
                            buffer(fin_rows, fin_width), pltpu.VMEM((cells, rows), jnp.int32),
                            pltpu.VMEM((cells, rows), jnp.int32), pltpu.SemaphoreType.DMA((8,))],
            compiler_params=params,
            name="start_gx",
        )(fluid_hbm, fin_hbm, owners, targets)

        def start_rest_kernel(fluid_hbm, fin_hbm, _, fluid, fin, grpa, grpb, gyx, sems):
            copies = (
                pltpu.make_async_copy(
                    fluid_hbm, fluid.at[pl.ds(1, cells), pl.ds(PAD, rows), :], sems.at[0]
                ),
                pltpu.make_async_copy(
                    fin_hbm, fin.at[pl.ds(1, depth), pl.ds(PAD, fin_rows), :], sems.at[1]
                ),
            )
            for copy in copies:
                copy.start()
            for copy in copies:
                copy.wait()
            pack_rest(fluid, fin, grpa, grpb, gyx, my_place(), dims)

        fluid0, fin0, grpa, grpb, gyx = pl.pallas_call(
            start_rest_kernel,
            out_shape=(fluid_pad, fin_pad) + faces,
            in_specs=[in_hbm, in_hbm, vmem],
            out_specs=(vmem,) * 5,
            scratch_shapes=[pltpu.SemaphoreType.DMA((2,))],
            compiler_params=params,
            name="start_rest",
        )(fluid_hbm, fin_hbm, wall)

        def around(size, step):
            return [(i, (i + step) % size) for i in range(size)]

        def exchange(paira, pairb, side):
            cores = [(g, c) for g in range(groups) for c in range(sides)]
            number = {core: k for k, core in enumerate(cores)}

            def partner(g, c):
                other = g - 1 if g % 2 == 0 else g + 1
                return (other, c) if 0 <= other < groups else (g, 1 - c)

            first = [(number[g, c], number[g ^ 1, c]) for g, c in cores]
            second = [(number[g, c], number[partner(g, c)]) for g, c in cores]
            return (
                lax.ppermute(paira, ("grp", "gy"), first),
                lax.ppermute(pairb, ("grp", "gy"), second),
                lax.ppermute(side, "gy", [(0, 1), (1, 0)]),
            )

        prev = lax.ppermute(gxf, "gx", around(count, 1))
        nxt = lax.ppermute(gxb, "gx", around(count, -1))
        if ring:
            walls = [wall] + [lax.ppermute(wall, "gx", around(count, k)) for k in range(2, count - 1)]
        else:
            walls = [wall, lax.all_gather(wall, "gx")]
        paira, pairb, side = exchange(grpa, grpb, gyx)

        def middle_kernel(*refs):
            (act, src, prev, nxt, paira, pairb, side), refs = refs[2:9], refs[9:]
            wall_refs, refs = refs[: len(walls)], refs[len(walls) :]
            fluid, fin, first, rest, ghost_out, zedge, gxf, gxb = refs[:8]
            zrows, other, deposit = refs[8:]
            place = my_place()
            grp, gx, gy = place
            on_wall = grp == 0
            own = wall_refs[0]
            own_code = own[fin_rows:, LANES:]
            if ring:
                slots = [(gx, own, 0), ((gx + count - 1) % count, prev, face_rows),
                         ((gx + 1) % count, nxt, face_rows)]
                slots += [((gx + count - k) % count, ref, 0) for k, ref in
                          zip(range(2, count - 1), wall_refs[1:])]
                slots = [(o, ref.at[pl.ds(base, wall_rows), :]) for o, ref, base in slots]
            else:
                slots = [(s, wall_refs[1].at[s]) for s in range(count)]
            quadrants = [(a * cells, b * LANES) for a in range(2) for b in range(2)]
            ghost = jnp.zeros((cells, rows), jnp.float32)
            deposits = [jnp.zeros((cells, rows), jnp.float32) for _ in quadrants]
            mine = (4 * gx).astype(jnp.float32)
            for owner, ref in slots:
                theirs = own_code - (4 * jnp.asarray(owner, jnp.int32)).astype(jnp.float32)
                temps = ref[fin_rows:, 0:LANES]
                wanted = ref[fin_rows:, LANES:] - mine
                for q, (r, c) in enumerate(quadrants):
                    ghost = jnp.where(theirs == q, ref[r : r + cells, c : c + LANES], ghost)
                    flux = HEAT_COEF * (temps - own[r : r + cells, c : c + LANES])
                    deposits[q] = deposits[q] + jnp.where(wanted == q, flux, 0.0)
            ghost_out[...] = ghost

            @pl.when(on_wall)
            def _():
                split = jnp.concatenate(
                    [jnp.concatenate(deposits[0:2], axis=1), jnp.concatenate(deposits[2:4], axis=1)],
                    axis=0,
                )
                mixed = dot(split, interleave_matrix(fin_width), ((1,), (1,)))
                deposit[...] = dot(interleave_matrix(fin_rows), mixed, ((1,), (0,)))

            @pl.when(jnp.logical_not(on_wall))
            def _():
                deposit[...] = jnp.zeros((fin_rows, fin_width), jnp.float32)

            below, above = grp_halos(paira, pairb, grp)
            low_face = jnp.where(on_wall, ghost, below[0:cells, 0:LANES])
            unpack_halos(fluid, fin, zrows, zedge, prev, nxt, below, above, side, low_face, 0,
                         place, sizes, dims)
            fluid_sweep(fluid, act, zedge, other, 0, dims, (0, pairs - 1, 2))
            hedge = side[cells : cells + fin_rows, 0:LANES]

            def layer(d):
                here, total = fin_neighbours(fin, d, hedge, fin_rows)
                rhs = here + src[d]
                first[d + 1, PAD : PAD + fin_rows, :] = (rhs + FIN_CONDUCTION * total) * (1.0 / DIAG)
                rest[d] = rhs * (OMEGA / DIAG) + here * (1.0 - OMEGA)

            repeat(depth, layer)
            first[1, PAD : PAD + fin_rows, :] += deposit[...] * (1.0 / DIAG)
            rest[0] += deposit[...] * (OMEGA / DIAG)
            inner = slice(PAD, PAD + rows)
            top, bottom = slice(PAD, PAD + 1), slice(PAD + fin_rows - 1, PAD + fin_rows)
            pack_gx(fluid[1, inner, :], fluid[cells, inner, :], lambda d: first[d + 1, top, :],
                    lambda d: first[d + 1, bottom, :], 0, gxf, gxb, dims)

        received = (prev, nxt, paira, pairb, side)
        zrows_buffer, zedge_buffer = buffer(LANES, rows), buffer(rows, LANES)
        other_buffer = buffer(rows + 2 * PAD, width)
        outs = pl.pallas_call(
            middle_kernel,
            out_shape=(fluid_pad, fin_pad, fin_pad, f32(depth, fin_rows, fin_width),
                       f32(cells, rows), f32(rows, LANES), f32(face_rows, width),
                       f32(face_rows, width)),
            in_specs=[vmem] * (9 + len(walls)),
            out_specs=(vmem,) * 8,
            scratch_shapes=[zrows_buffer, other_buffer, buffer(fin_rows, fin_width)],
            input_output_aliases={0: 0, 1: 1},
            compiler_params=params,
            name="middle_gx",
        )(fluid0, fin0, active, fin_source, *received, *walls)
        fluid1, _, first, rest, ghost, zedge, gxf, gxb = outs

        def middle_rest_kernel(_, act, zedge, first, fluid, grpa, grpb, gyx, other):
            fluid_sweep(fluid, act, zedge, other, 0, dims, (1, 1, pairs - 2))
            pack_rest(fluid, first, grpa, grpb, gyx, my_place(), dims)

        fluid2, grpa, grpb, gyx = pl.pallas_call(
            middle_rest_kernel,
            out_shape=(fluid_pad,) + faces,
            in_specs=[vmem] * 4,
            out_specs=(vmem,) * 4,
            scratch_shapes=[other_buffer],
            input_output_aliases={0: 0},
            compiler_params=params,
            name="middle_rest",
        )(fluid1, active, zedge, first)

        prev = lax.ppermute(gxf, "gx", around(count, 1))
        nxt = lax.ppermute(gxb, "gx", around(count, -1))
        paira, pairb, side = exchange(grpa, grpb, gyx)

        def end_kernel(_0, _1, _2, act, ghost, prev, nxt, paira, pairb, side,
                       fluid, first, rest, fluid_new, fin_new,
                       zrows, zedge, other, fluid_sems, fin_sems):
            place = my_place()
            on_wall = place[0] == 0
            below, above = grp_halos(paira, pairb, place[0])
            low_face = jnp.where(on_wall, ghost[...], below[0:cells, 0:LANES])
            unpack_halos(fluid, first, zrows, zedge, prev, nxt, below, above, side, low_face, 1,
                         place, sizes, dims)
            hedge = side[cells : cells + fin_rows, 0:LANES]

            def fluid_copy(k):
                return pltpu.make_async_copy(
                    fluid.at[pl.ds(2 * k + 1, 2), pl.ds(PAD, rows), :],
                    fluid_new.at[pl.ds(2 * k, 2)], fluid_sems.at[k],
                )

            def fin_copy(k):
                part = pl.ds(k * 8, 8)
                return pltpu.make_async_copy(rest.at[part], fin_new.at[part], fin_sems.at[k])

            fluid_sweep(fluid, act, zedge, other, 1, dims, (0, 1, pairs),
                        lambda k: fluid_copy(k).start())

            def layers(k, carry):
                for j in range(8):
                    d = k * 8 + j
                    _, total = fin_neighbours(first, d, hedge, fin_rows)
                    rest[d] = rest[d] + (OMEGA * FIN_CONDUCTION / DIAG) * total
                fin_copy(k).start()
                return carry

            lax.fori_loop(0, depth // 8, layers, 0)

            def finish_fluid(i, carry):
                fluid_copy(i).wait()
                return carry

            def finish_fin(d, carry):
                fin_copy(d).wait()
                return carry

            lax.fori_loop(0, cells // 2, finish_fluid, 0)
            lax.fori_loop(0, depth // 8, finish_fin, 0)

        results = pl.pallas_call(
            end_kernel,
            out_shape=(fluid_pad, fin_pad, f32(depth, fin_rows, fin_width),
                       f32(cells, rows, width), f32(depth, fin_rows, fin_width)),
            in_specs=[vmem] * 10,
            out_specs=(vmem, vmem, vmem, hbm, hbm),
            scratch_shapes=[zrows_buffer, zedge_buffer, other_buffer,
                            pltpu.SemaphoreType.DMA((cells // 2,)),
                                      pltpu.SemaphoreType.DMA((depth // 8,))],
            input_output_aliases={0: 0, 1: 1, 2: 2},
            compiler_params=params,
            name="end",
        )(fluid2, first, rest, active, ghost, prev, nxt, paira, pairb, side)
        return results[3], results[4]

    return jax.shard_map(local, mesh=mesh, in_specs=in_specs, out_specs=out_specs, check_vma=False)
```

```python
import jax
import jax.numpy as jnp
from jax import lax
from jax.experimental import pallas as pl
from jax.experimental.pallas import tpu as pltpu
from jax.sharding import PartitionSpec as P

FLUID_DIFFUSION = 1.0
FIN_CONDUCTION = 1.0
HEAT_COEF = 1.0
DIAG = 1.0 + 6.0 * FIN_CONDUCTION
SPECTRAL = 6.0 * FIN_CONDUCTION / DIAG
OMEGA = 1.0 / (1.0 - SPECTRAL * SPECTRAL / 2.0)
FLUID_SCALE = 1.0 / (1.0 + 6.0 * FLUID_DIFFUSION)
LANES = 128
PAD = 8
ROWS = 32
HIGHEST = lax.Precision.HIGHEST


def iota(shape, axis):
    return lax.broadcasted_iota(jnp.int32, shape, axis)


def repeat(count, body, step=8):
    def trip(k, carry):
        for j in range(step):
            body(k * step + j)
        return carry

    lax.fori_loop(0, count // step, trip, 0)


def tiles(value):
    return [value[:, k : k + LANES] for k in range(0, value.shape[1], LANES)]


def lane_neighbours(block, low, high):
    parts = tiles(block)
    lane = iota(parts[0].shape, 1)
    down = [pltpu.roll(part, 1, axis=1) for part in parts]
    up = [pltpu.roll(part, LANES - 1, axis=1) for part in parts]
    below = [jnp.where(lane == 0, a, b) for a, b in zip([low] + down[:-1], down)]
    above = [jnp.where(lane == LANES - 1, a, b) for a, b in zip(up[1:] + [high], up)]
    return jnp.concatenate([a + b for a, b in zip(below, above)], axis=1)


def interleave_matrix(count):
    row = iota((count, count), 0)
    col = iota((count, count), 1)
    half = count // 2
    source = jnp.where(col < half, 2 * col, 2 * (col - half) + 1)
    return (row == source).astype(jnp.float32)


def dot(a, b, contract):
    return lax.dot_general(
        a, b, (contract, ((), ())), precision=HIGHEST, preferred_element_type=jnp.float32
    )


def checker_pack(plane, parity):
    rows = plane.shape[0] // 2
    top = plane[:rows]
    bottom = plane[rows:]
    colour = (iota(top.shape, 0) + iota(top.shape, 1)) & 1
    return jnp.where(colour == parity, top, pltpu.roll(bottom, 1, axis=1))


def lane_column(column, cells, rows):
    kept = jnp.zeros((rows, LANES), jnp.float32)
    lane = iota((rows, LANES), 1)
    for i in range(cells):
        kept = jnp.where(lane == i, column(i), kept)
    return kept.T[:cells]


def pack_gx(plane, row, colour, gx, senda, sendb, dims):
    cells, rows, width, depth, fin_rows, fin_width = dims
    half = rows // 2
    even = gx % 2 == 0
    for send, high in ((senda, even), (sendb, jnp.logical_not(even))):
        parity = jnp.where(high, (colour + cells - 1) % 2, colour)
        send[0:half, :] = checker_pack(plane(high), parity)

    def lines(d):
        senda[pl.ds(half + d, 1), :] = row(d, even)
        sendb[pl.ds(half + d, 1), :] = row(d, jnp.logical_not(even))

    repeat(depth, lines)


def pack_rest(fluid, fin, grpa, grpb, gyx, place, dims):
    cells, rows, width, depth, fin_rows, fin_width = dims
    grp, gx, gy = place
    even = grp % 2 == 0
    low, high = (
        lane_column(lambda i: fluid[i + 1, PAD : PAD + rows, k : k + 1], cells, rows)
        for k in (0, width - 1)
    )
    grpa[0:cells, 0:LANES] = jnp.where(even, high, low)
    grpb[0:cells, 0:LANES] = jnp.where(even, low, high)
    up = jnp.where(even, depth, 1)
    grpa[cells : cells + fin_rows, :] = fin[up, PAD : PAD + fin_rows, :]
    grpb[cells : cells + fin_rows, :] = fin[depth + 1 - up, PAD : PAD + fin_rows, :]
    edge = PAD + (1 - gy) * (rows - 1)
    for i in range(cells):
        gyx[i : i + 1, :] = fluid[i + 1, pl.ds(edge, 1), :]
    lane = iota((fin_rows, LANES), 1)

    def columns(at, side):
        kept = jnp.zeros((fin_rows, LANES), jnp.float32)
        for d in range(depth):
            column = fin[d + 1, PAD : PAD + fin_rows, at : at + 1]
            kept = jnp.where(lane == 2 * d + side, column, kept)
        gyx[cells : cells + fin_rows, 0:LANES] = kept

    @pl.when(gy == 0)
    def _():
        columns(fin_width - 1, 1)

    @pl.when(gy != 0)
    def _():
        columns(0, 0)


def my_place():
    return [lax.axis_index(name) for name in ("grp", "gx", "gy")]


def sides_of(at, count):
    return at % 2 == 0, jnp.where((at == 0) | (at == count - 1), 0.0, 1.0)


def grp_halos(paira, pairb, grp, groups):
    even, inside = sides_of(grp, groups)
    a, b = paira[...], pairb[...] * inside
    return jnp.where(even, b, a), jnp.where(even, a, b)


def unpack_fluid(fluid, zrows, zedge, paira, pairb, low_face, high_face, side, colour, place,
                 count, dims):
    cells, rows, width, depth, fin_rows, fin_width = dims
    half = rows // 2
    grp, gx, gy = place
    even, inside = sides_of(gx, count)
    high_plane = jnp.where(even, cells + 1, 0)
    for plane, ref, on in ((high_plane, paira, 1.0), (cells + 1 - high_plane, pairb, inside)):
        packed = ref[0:half, :] * on
        fluid[plane, PAD : PAD + half, :] = packed
        fluid[plane, PAD + half : PAD + rows, :] = pltpu.roll(packed, width - 1, axis=1)
    low_on = jnp.where(gy == 0, 0.0, 1.0)
    high_on = 1.0 - low_on
    for i in range(cells):
        line = side[i : i + 1, :]
        fluid[i + 1, PAD - 1 : PAD, :] = line * low_on
        fluid[i + 1, PAD + rows : PAD + rows + 1, :] = line * high_on
    odd_row = (iota((1, rows), 1) & 1) == 1
    for k in range(cells // 2):
        for lane, face, swap in ((2 * k, high_face, colour == 1), (2 * k + 1, low_face, colour == 0)):
            first, second = face[2 * k : 2 * k + 1, :], face[2 * k + 1 : 2 * k + 2, :]
            zrows[lane : lane + 1, :] = jnp.where(odd_row == swap, second, first)
    zrows[cells:, :] = jnp.zeros((LANES - cells, rows), jnp.float32)
    zedge[...] = zrows[...].T


def fluid_sweep(fluid, active, zedge, other, colour, dims, pairs, done=None):
    cells, rows, width, depth, fin_rows, fin_width = dims
    parity = (iota((ROWS, width), 0) + iota((ROWS, width), 1)) & 1
    updating = parity == colour
    off = parity ^ colour
    end_parity = iota((1, width), 1) & 1

    first_pair, step, count = pairs

    def pair(j, carry):
        k = first_pair + step * j
        a, b = 2 * k + 1, 2 * k + 2
        for at, swap in ((PAD - 1, 1 - colour), (PAD + rows, colour)):
            line = slice(at, at + 1)
            other[line, :] = jnp.where(end_parity == swap, fluid[b, line, :], fluid[a, line, :])
        for start in range(0, rows, ROWS):
            inner = slice(PAD + start, PAD + start + ROWS)
            other[inner, :] = jnp.where(updating, fluid[b, inner, :], fluid[a, inner, :])
        for start in range(0, rows, ROWS):
            inner = slice(PAD + start, PAD + start + ROWS)
            edge = pltpu.roll(zedge[start : start + ROWS, :], LANES - 1 - 2 * k, axis=1)
            shared = (
                other[PAD + start - 1 : PAD + start + ROWS - 1, :]
                + other[PAD + start + 1 : PAD + start + ROWS + 1, :]
                + lane_neighbours(other[inner, :], edge, edge)
            )
            here_a = fluid[a, inner, :]
            here_b = fluid[b, inner, :]
            total_a = shared + fluid[a - 1, inner, :] + here_b
            total_b = shared + fluid[b + 1, inner, :] + here_a
            new_a = (here_a + FLUID_DIFFUSION * total_a) * FLUID_SCALE
            new_b = (here_b + FLUID_DIFFUSION * total_b) * FLUID_SCALE
            mask_a = active[a - 1, start : start + ROWS, :] > off
            mask_b = active[b - 1, start : start + ROWS, :] > 1 - off
            fluid[a, inner, :] = jnp.where(mask_a, new_a, here_a)
            fluid[b, inner, :] = jnp.where(mask_b, new_b, here_b)
        if done is not None:
            done(k)
        return carry

    lax.fori_loop(0, count, pair, 0)


def fin_neighbours(fin, d, hedge, fin_rows):
    inner = slice(PAD, PAD + fin_rows)
    here = fin[d + 1, inner, :]
    edge = pltpu.roll(hedge, LANES - 1 - 2 * d, axis=1)
    total = (
        fin[d, inner, :]
        + fin[d + 2, inner, :]
        + fin[d + 1, PAD - 1 : PAD + fin_rows - 1, :]
        + fin[d + 1, PAD + 1 : PAD + fin_rows + 1, :]
        + lane_neighbours(here, edge, edge)
    )
    return here, total


def solution(mesh):
    in_specs = (
        P("gx", "gy", "grp"),
        P("gx", "gy", "grp"),
        P("grp", "gx", "gy"),
        P("grp", "gx", "gy"),
        P("gx", "gy", None, None),
        P("gx", "gy", None),
    )
    out_specs = (P("gx", "gy", "grp"), P("grp", "gx", "gy"))
    count = mesh.shape["gx"]
    groups = mesh.shape["grp"]
    sides = mesh.shape["gy"]
    assert sides == 2 and groups % 2 == 0 and count % 2 == 0
    ring = count == 4
    vmem = pl.BlockSpec(memory_space=pltpu.VMEM)
    hbm = pl.BlockSpec(memory_space=pl.ANY)

    def local(fluid_temp, active, fin_temp, fin_source, wall_owner, wall_target):
        cells, rows, width = fluid_temp.shape
        depth, fin_rows, fin_width = fin_temp.shape
        assert rows == LANES and width == fin_width == 2 * rows and fin_rows == 2 * cells
        assert 2 * depth <= LANES and depth % 8 == 0 and depth >= 24 and cells % 2 == 0 and cells >= 4 and rows % ROWS == 0 and fin_rows == ROWS
        dims = (cells, rows, width, depth, fin_rows, fin_width)
        sizes = (groups, count)
        half = rows // 2
        pairs = cells // 2
        face_rows = half + depth
        wall_rows = fin_rows + cells
        small_rows = cells + fin_rows
        gx_rows = face_rows + (wall_rows if ring else 0)
        owners = wall_owner.reshape(cells, rows)
        targets = wall_target.reshape(cells, rows)
        f32 = lambda *shape: jax.ShapeDtypeStruct(shape, jnp.float32)
        params = pltpu.CompilerParams(vmem_limit_bytes=32 * 1024 * 1024)
        fluid_pad = f32(cells + 2, rows + 2 * PAD, width)
        fin_pad = f32(depth + 2, fin_rows + 2 * PAD, fin_width)
        faces = (f32(small_rows, width), f32(small_rows, width), f32(small_rows, width))

        def start_gx_kernel(fluid_hbm, fin_hbm, own_hbm, tgt_hbm, fluid, fin, gxa, gxb, wall,
                            planes, bottom, low_rows, high_rows, root, own, tgt, sems):
            def copy(k, source, target):
                return pltpu.make_async_copy(source, target, sems.at[k])

            last = cells - 1
            copies = [
                copy(0, own_hbm, own),
                copy(1, tgt_hbm, tgt),
                copy(2, fluid_hbm.at[:, :, pl.ds(0, LANES)], bottom),
                copy(3, fin_hbm.at[0], root),
                copy(4, fluid_hbm.at[0], planes.at[0]),
                copy(5, fluid_hbm.at[last], planes.at[1]),
                copy(6, fin_hbm.at[:, pl.ds(0, PAD), :], low_rows),
                copy(7, fin_hbm.at[:, pl.ds(fin_rows - PAD, PAD), :], high_rows),
            ]
            loads = [
                copy(8, fluid_hbm, fluid.at[pl.ds(1, cells), pl.ds(PAD, rows), :]),
                copy(9, fin_hbm, fin.at[pl.ds(1, depth), pl.ds(PAD, fin_rows), :]),
            ]
            for item in copies:
                item.start()
            for item in copies:
                item.wait()
            for item in loads:
                item.start()
            shape = (cells, rows)
            shift = tgt[...] - 2 * (iota(shape, 0) * fin_width + iota(shape, 1))
            row_shift = (shift >= fin_width).astype(jnp.int32)
            code = own[...] * 4 + row_shift * 2 + (shift - row_shift * fin_width)
            wall[fin_rows:, LANES:] = code.astype(jnp.float32)
            wall[fin_rows:, 0:LANES] = lane_column(lambda i: bottom[i, :, 0:1], cells, rows)
            even_rows = dot(interleave_matrix(fin_rows), root[...], ((0,), (0,)))
            wall[0:fin_rows, :] = dot(even_rows, interleave_matrix(fin_width), ((1,), (0,)))
            gx = lax.axis_index("gx")
            pack_gx(
                lambda high: planes[jnp.where(high, 1, 0)],
                lambda d, high: jnp.where(high, high_rows[d, PAD - 1 : PAD, :], low_rows[d, 0:1, :]),
                1, gx, gxa, gxb, dims,
            )
            if ring:
                gxa[face_rows:, :] = wall[...]
                gxb[face_rows:, :] = wall[...]
            for item in loads:
                item.wait()

        fluid_hbm, fin_hbm, owners, targets = (
            pltpu.with_memory_space_constraint(v, pltpu.HBM)
            for v in (fluid_temp, fin_temp, owners, targets)
        )
        in_hbm = pl.BlockSpec(memory_space=pltpu.HBM)
        buffer = lambda *shape: pltpu.VMEM(shape, jnp.float32)
        fluid0, fin0, gxa, gxb, wall = pl.pallas_call(
            start_gx_kernel,
            out_shape=(fluid_pad, fin_pad, f32(gx_rows, width), f32(gx_rows, width),
                       f32(wall_rows, width)),
            in_specs=[in_hbm] * 4,
            out_specs=(vmem,) * 5,
            scratch_shapes=[buffer(2, rows, width), buffer(cells, rows, LANES),
                            buffer(depth, PAD, fin_width), buffer(depth, PAD, fin_width),
                            buffer(fin_rows, fin_width), pltpu.VMEM((cells, rows), jnp.int32),
                            pltpu.VMEM((cells, rows), jnp.int32), pltpu.SemaphoreType.DMA((10,))],
            compiler_params=params,
            name="start_gx",
        )(fluid_hbm, fin_hbm, owners, targets)

        def start_rest_kernel(fluid, fin, grpa, grpb, gyx):
            pack_rest(fluid, fin, grpa, grpb, gyx, my_place(), dims)

        grpa, grpb, gyx = pl.pallas_call(
            start_rest_kernel,
            out_shape=faces,
            in_specs=[vmem, vmem],
            out_specs=(vmem,) * 3,
            compiler_params=params,
            name="start_rest",
        )(fluid0, fin0)

        def pairings(axis, size):
            cores = [(g, c) for g in range(size) for c in range(sides)]
            number = {core: k for k, core in enumerate(cores)}

            def partner(g, c):
                other = g - 1 if g % 2 == 0 else g + 1
                return (other, c) if 0 <= other < size else (g, 1 - c)

            first = [(number[g, c], number[g ^ 1, c]) for g, c in cores]
            second = [(number[g, c], number[partner(g, c)]) for g, c in cores]
            return (axis, "gy"), first, second

        def exchange(axis, size, paira, pairb):
            axes, first, second = pairings(axis, size)
            return lax.ppermute(paira, axes, first), lax.ppermute(pairb, axes, second)

        def swap(side):
            return lax.ppermute(side, "gy", [(0, 1), (1, 0)])

        def mixed_with(k):
            return [(i, i ^ k) for i in range(count)]

        if ring:
            gxa = lax.ppermute(gxa, "gx", mixed_with(1))
            gxb = lax.ppermute(gxb, "gx", mixed_with(3))
            walls = [wall, lax.ppermute(wall, "gx", mixed_with(2))]
        else:
            gxa, gxb = exchange("gx", count, gxa, gxb)
            walls = [wall, lax.all_gather(wall, "gx")]
        side = swap(gyx)
        grpa, grpb = exchange("grp", groups, grpa, grpb)

        def fin_depth_halos(fin, paira, pairb):
            below, above = grp_halos(paira, pairb, lax.axis_index("grp"), groups)
            fin[0, PAD : PAD + fin_rows, :] = below[cells:, :]
            fin[depth + 1, PAD : PAD + fin_rows, :] = above[cells:, :]

        def middle_fin_kernel(_, src, paira, pairb, side, fin, first, rest):
            fin_depth_halos(fin, paira, pairb)
            empty = jnp.zeros((depth, PAD, fin_width), jnp.float32)
            fin[1 : depth + 1, 0:PAD, :] = empty
            fin[1 : depth + 1, PAD + fin_rows :, :] = empty
            hedge = side[cells : cells + fin_rows, 0:LANES]

            def layer(d):
                here, total = fin_neighbours(fin, d, hedge, fin_rows)
                rhs = here + src[d]
                first[d + 1, PAD : PAD + fin_rows, :] = (rhs + FIN_CONDUCTION * total) * (1.0 / DIAG)
                rest[d] = rhs * (OMEGA / DIAG) + here * (1.0 - OMEGA)

            repeat(depth, layer)

        _, first, rest = pl.pallas_call(
            middle_fin_kernel,
            out_shape=(fin_pad, fin_pad, f32(depth, fin_rows, fin_width)),
            in_specs=[vmem] * 5,
            out_specs=(vmem,) * 3,
            input_output_aliases={0: 0},
            compiler_params=params,
            name="middle_fin",
        )(fin0, fin_source, grpa, grpb, side)

        def middle_gx_kernel(_0, _1, _2, act, gxa_in, gxb_in, paira, pairb, side, own, other_wall,
                             fluid, first, rest, ghost_out, zedge, gxa, gxb,
                             zrows, other):
            place = my_place()
            grp, gx, gy = place
            on_wall = grp == 0
            own_code = own[fin_rows:, LANES:]
            if ring:
                slots = [(gx, own), (gx ^ 1, gxa_in.at[pl.ds(face_rows, wall_rows), :]),
                         (gx ^ 3, gxb_in.at[pl.ds(face_rows, wall_rows), :]), (gx ^ 2, other_wall)]
            else:
                slots = [(s, other_wall.at[s]) for s in range(count)]
            quadrants = [(a * cells, b * LANES) for a in range(2) for b in range(2)]
            ghost = jnp.zeros((cells, rows), jnp.float32)
            deposits = [jnp.zeros((cells, rows), jnp.float32) for _ in quadrants]
            mine = (4 * gx).astype(jnp.float32)
            for owner, ref in slots:
                theirs = own_code - (4 * jnp.asarray(owner, jnp.int32)).astype(jnp.float32)
                temps = ref[fin_rows:, 0:LANES]
                wanted = ref[fin_rows:, LANES:] - mine
                for q, (r, c) in enumerate(quadrants):
                    ghost = jnp.where(theirs == q, ref[r : r + cells, c : c + LANES], ghost)
                    flux = HEAT_COEF * (temps - own[r : r + cells, c : c + LANES])
                    deposits[q] = deposits[q] + jnp.where(wanted == q, flux, 0.0)
            ghost_out[...] = ghost

            @pl.when(on_wall)
            def _():
                split = jnp.concatenate(
                    [jnp.concatenate(deposits[0:2], axis=1), jnp.concatenate(deposits[2:4], axis=1)],
                    axis=0,
                )
                mixed = dot(split, interleave_matrix(fin_width), ((1,), (1,)))
                landed = dot(interleave_matrix(fin_rows), mixed, ((1,), (0,)))
                first[1, PAD : PAD + fin_rows, :] += landed * (1.0 / DIAG)
                rest[0] += landed * (OMEGA / DIAG)

            even, inside = sides_of(gx, count)
            high_row = PAD + fin_rows - 1
            row_a = jnp.where(even, high_row, PAD)
            row_b = PAD + high_row - row_a
            scale = FIN_CONDUCTION / DIAG

            def add_row(d):
                first[d + 1, pl.ds(row_a, 1), :] += gxa_in[pl.ds(half + d, 1), :] * scale
                first[d + 1, pl.ds(row_b, 1), :] += gxb_in[pl.ds(half + d, 1), :] * (scale * inside)

            repeat(depth, add_row)
            below, above = grp_halos(paira, pairb, grp, groups)
            low_face = jnp.where(on_wall, ghost, below[0:cells, 0:LANES])
            unpack_fluid(fluid, zrows, zedge, gxa_in, gxb_in, low_face, above[0:cells, 0:LANES],
                         side, 0, place, count, dims)
            fluid_sweep(fluid, act, zedge, other, 0, dims, (0, pairs - 1, 2))
            pack_gx(
                lambda high: fluid[jnp.where(high, cells, 1), PAD : PAD + rows, :],
                lambda d, high: first[d + 1, pl.ds(jnp.where(high, high_row, PAD), 1), :],
                0, gx, gxa, gxb, dims,
            )

        zrows_buffer, zedge_buffer = buffer(LANES, rows), buffer(rows, LANES)
        other_buffer = buffer(rows + 2 * PAD, width)
        fluid1, first, rest, ghost, zedge, gxa, gxb = pl.pallas_call(
            middle_gx_kernel,
            out_shape=(fluid_pad, fin_pad, f32(depth, fin_rows, fin_width), f32(cells, rows),
                       f32(rows, LANES), f32(face_rows, width), f32(face_rows, width)),
            in_specs=[vmem] * 11,
            out_specs=(vmem,) * 7,
            scratch_shapes=[zrows_buffer, other_buffer],
            input_output_aliases={0: 0, 1: 1, 2: 2},
            compiler_params=params,
            name="middle_gx",
        )(fluid0, first, rest, active, gxa, gxb, grpa, grpb, side, *walls)
        gxa, gxb = exchange("gx", count, gxa, gxb)

        def middle_rest_kernel(_, act, zedge, first, fluid, grpa, grpb, gyx, other):
            fluid_sweep(fluid, act, zedge, other, 0, dims, (1, 1, pairs - 2))
            pack_rest(fluid, first, grpa, grpb, gyx, my_place(), dims)

        fluid2, grpa, grpb, gyx = pl.pallas_call(
            middle_rest_kernel,
            out_shape=(fluid_pad,) + faces,
            in_specs=[vmem] * 4,
            out_specs=(vmem,) * 4,
            scratch_shapes=[other_buffer],
            input_output_aliases={0: 0},
            compiler_params=params,
            name="middle_rest",
        )(fluid1, active, zedge, first)
        side = swap(gyx)
        grpa, grpb = exchange("grp", groups, grpa, grpb)

        def fin_second(first, rest, hedge, block):
            for j in range(8):
                d = block * 8 + j
                _, total = fin_neighbours(first, d, hedge, fin_rows)
                rest[d] = rest[d] + (OMEGA * FIN_CONDUCTION / DIAG) * total

        blocks = depth // 8

        def end_fin_kernel(_0, _1, gxa, gxb, side, first, rest):
            even, inside = sides_of(lax.axis_index("gx"), count)
            row_a = jnp.where(even, PAD + fin_rows, PAD - 1)
            row_b = 2 * PAD + fin_rows - 1 - row_a

            def halo_row(d):
                first[d + 1, pl.ds(row_a, 1), :] = gxa[pl.ds(half + d, 1), :]
                first[d + 1, pl.ds(row_b, 1), :] = gxb[pl.ds(half + d, 1), :] * inside

            repeat(depth, halo_row)
            hedge = side[cells : cells + fin_rows, 0:LANES]

            def layers(k, carry):
                fin_second(first, rest, hedge, k)
                return carry

            lax.fori_loop(1, blocks - 1, layers, 0)

        first, rest = pl.pallas_call(
            end_fin_kernel,
            out_shape=(fin_pad, f32(depth, fin_rows, fin_width)),
            in_specs=[vmem] * 5,
            out_specs=(vmem,) * 2,
            input_output_aliases={0: 0, 1: 1},
            compiler_params=params,
            name="end_fin",
        )(first, rest, gxa, gxb, side)

        def end_kernel(_0, _1, _2, act, ghost, gxa, gxb, paira, pairb, side,
                       fluid, first, rest, fluid_new, fin_new,
                       zrows, zedge, other, fluid_sems, fin_sems):
            place = my_place()
            on_wall = place[0] == 0

            def fluid_copy(k):
                return pltpu.make_async_copy(
                    fluid.at[pl.ds(2 * k + 1, 2), pl.ds(PAD, rows), :],
                    fluid_new.at[pl.ds(2 * k, 2)], fluid_sems.at[k],
                )

            def fin_copy(k, start, size):
                part = pl.ds(start, size)
                return pltpu.make_async_copy(rest.at[part], fin_new.at[part], fin_sems.at[k])

            fin_copies = [fin_copy(0, 8, depth - 16), fin_copy(1, 0, 8), fin_copy(2, depth - 8, 8)]
            fin_copies[0].start()
            fin_depth_halos(first, paira, pairb)
            hedge = side[cells : cells + fin_rows, 0:LANES]
            for k, block in ((1, 0), (2, blocks - 1)):
                fin_second(first, rest, hedge, block)
                fin_copies[k].start()
            below, above = grp_halos(paira, pairb, place[0], groups)
            low_face = jnp.where(on_wall, ghost[...], below[0:cells, 0:LANES])
            unpack_fluid(fluid, zrows, zedge, gxa, gxb, low_face, above[0:cells, 0:LANES], side, 1,
                         place, count, dims)
            fluid_sweep(fluid, act, zedge, other, 1, dims, (0, 1, pairs),
                        lambda k: fluid_copy(k).start())

            def finish(k, carry):
                fluid_copy(k).wait()
                return carry

            for item in fin_copies:
                item.wait()
            lax.fori_loop(0, pairs, finish, 0)

        results = pl.pallas_call(
            end_kernel,
            out_shape=(fluid_pad, fin_pad, f32(depth, fin_rows, fin_width),
                       f32(cells, rows, width), f32(depth, fin_rows, fin_width)),
            in_specs=[vmem] * 10,
            out_specs=(vmem, vmem, vmem, hbm, hbm),
            scratch_shapes=[zrows_buffer, zedge_buffer, other_buffer,
                            pltpu.SemaphoreType.DMA((pairs,)), pltpu.SemaphoreType.DMA((3,))],
            input_output_aliases={0: 0, 1: 1, 2: 2},
            compiler_params=params,
            name="end",
        )(fluid2, first, rest, active, ghost, gxa, gxb, grpa, grpb, side)
        return results[3], results[4]

    return jax.shard_map(local, mesh=mesh, in_specs=in_specs, out_specs=out_specs, check_vma=False)
```

```python
import jax
import jax.numpy as jnp
from jax import lax
from jax.experimental import pallas as pl
from jax.experimental.pallas import tpu as pltpu
from jax.sharding import PartitionSpec as P


FLUID_DIFFUSION = 1.0
FIN_CONDUCTION = 1.0
HEAT_COEF = 1.0
DIAG = 1.0 + 6.0 * FIN_CONDUCTION
SPECTRAL = 6.0 * FIN_CONDUCTION / DIAG
OMEGA = 1.0 / (1.0 - SPECTRAL * SPECTRAL / 2.0)
FLUID_SCALE = 1.0 / (1.0 + 6.0 * FLUID_DIFFUSION)
LANES = 128
PAD = 8
ROWS = 32
HIGHEST = lax.Precision.HIGHEST


def iota(shape, axis):
    return lax.broadcasted_iota(jnp.int32, shape, axis)


def repeat(count, body, step=8):
    def trip(k, carry):
        for j in range(step):
            body(k * step + j)
        return carry

    lax.fori_loop(0, count // step, trip, 0)


def tiles(value):
    return [value[:, k : k + LANES] for k in range(0, value.shape[1], LANES)]


def lane_neighbours(block, low, high):
    parts = tiles(block)
    lane = iota(parts[0].shape, 1)
    down = [pltpu.roll(part, 1, axis=1) for part in parts]
    up = [pltpu.roll(part, LANES - 1, axis=1) for part in parts]
    below = [jnp.where(lane == 0, a, b) for a, b in zip([low] + down[:-1], down)]
    above = [jnp.where(lane == LANES - 1, a, b) for a, b in zip(up[1:] + [high], up)]
    return jnp.concatenate([a + b for a, b in zip(below, above)], axis=1)


def interleave_matrix(count):
    row = iota((count, count), 0)
    col = iota((count, count), 1)
    half = count // 2
    source = jnp.where(col < half, 2 * col, 2 * (col - half) + 1)
    return (row == source).astype(jnp.float32)


def dot(a, b, contract):
    return lax.dot_general(
        a, b, (contract, ((), ())), precision=HIGHEST, preferred_element_type=jnp.float32
    )


def checker_pack(plane, parity):
    rows = plane.shape[0] // 2
    top = plane[:rows]
    bottom = plane[rows:]
    colour = (iota(top.shape, 0) + iota(top.shape, 1)) & 1
    return jnp.where(colour == parity, top, pltpu.roll(bottom, 1, axis=1))


def lane_column(column, cells, rows):
    kept = jnp.zeros((rows, LANES), jnp.float32)
    lane = iota((rows, LANES), 1)
    for i in range(cells):
        kept = jnp.where(lane == i, column(i), kept)
    return kept.T[:cells]


def pack_gx(plane, row, colour, gx, senda, sendb, dims):
    cells, rows, _, depth, _, _ = dims
    half = rows // 2
    even = gx % 2 == 0
    for send, high in ((senda, even), (sendb, jnp.logical_not(even))):
        parity = jnp.where(high, (colour + cells - 1) % 2, colour)
        send[0:half, :] = checker_pack(plane(high), parity)

    def lines(d):
        senda[pl.ds(half + d, 1), :] = row(d, even)
        sendb[pl.ds(half + d, 1), :] = row(d, jnp.logical_not(even))

    repeat(depth, lines)


def pack_rest(fluid, fin, grpa, grpb, gyx, place, dims):
    cells, rows, width, depth, fin_rows, fin_width = dims
    grp, _, gy = place
    even = grp % 2 == 0
    low, high = (
        lane_column(lambda i: fluid[i + 1, PAD : PAD + rows, k : k + 1], cells, rows)
        for k in (0, width - 1)
    )
    grpa[0:cells, 0:LANES] = jnp.where(even, high, low)
    grpb[0:cells, 0:LANES] = jnp.where(even, low, high)
    up = jnp.where(even, depth, 1)
    grpa[cells : cells + fin_rows, :] = fin[up, PAD : PAD + fin_rows, :]
    grpb[cells : cells + fin_rows, :] = fin[depth + 1 - up, PAD : PAD + fin_rows, :]
    edge = PAD + (1 - gy) * (rows - 1)
    for i in range(cells):
        gyx[i : i + 1, :] = fluid[i + 1, pl.ds(edge, 1), :]
    lane = iota((fin_rows, LANES), 1)

    def columns(at, side):
        kept = jnp.zeros((fin_rows, LANES), jnp.float32)
        for d in range(depth):
            column = fin[d + 1, PAD : PAD + fin_rows, at : at + 1]
            kept = jnp.where(lane == 2 * d + side, column, kept)
        gyx[cells : cells + fin_rows, 0:LANES] = kept

    @pl.when(gy == 0)
    def _():
        columns(fin_width - 1, 1)

    @pl.when(gy != 0)
    def _():
        columns(0, 0)


def my_place():
    return [lax.axis_index(name) for name in ("grp", "gx", "gy")]


def sides_of(at, count):
    return at % 2 == 0, jnp.where((at == 0) | (at == count - 1), 0.0, 1.0)


def grp_halos(paira, pairb, grp, groups):
    even, inside = sides_of(grp, groups)
    a, b = paira[...], pairb[...] * inside
    return jnp.where(even, b, a), jnp.where(even, a, b)


def unpack_fluid(fluid, zrows, zedge, paira, pairb, low_face, high_face, side, colour, place,
                 count, dims):
    cells, rows, width, _, _, _ = dims
    half = rows // 2
    _, gx, gy = place
    even, inside = sides_of(gx, count)
    high_plane = jnp.where(even, cells + 1, 0)
    for plane, ref, on in ((high_plane, paira, 1.0), (cells + 1 - high_plane, pairb, inside)):
        packed = ref[0:half, :] * on
        fluid[plane, PAD : PAD + half, :] = packed
        fluid[plane, PAD + half : PAD + rows, :] = pltpu.roll(packed, width - 1, axis=1)
    low_on = jnp.where(gy == 0, 0.0, 1.0)
    high_on = 1.0 - low_on
    for i in range(cells):
        line = side[i : i + 1, :]
        fluid[i + 1, PAD - 1 : PAD, :] = line * low_on
        fluid[i + 1, PAD + rows : PAD + rows + 1, :] = line * high_on
    odd_row = (iota((1, rows), 1) & 1) == 1
    for k in range(cells // 2):
        for lane, face, swap in ((2 * k, high_face, colour == 1), (2 * k + 1, low_face, colour == 0)):
            first, second = face[2 * k : 2 * k + 1, :], face[2 * k + 1 : 2 * k + 2, :]
            zrows[lane : lane + 1, :] = jnp.where(odd_row == swap, second, first)
    zrows[cells:, :] = jnp.zeros((LANES - cells, rows), jnp.float32)
    zedge[...] = zrows[...].T


def fluid_sweep(fluid, active, zedge, other, colour, dims, pairs, done=None):
    _, rows, width, _, _, _ = dims
    parity = (iota((ROWS, width), 0) + iota((ROWS, width), 1)) & 1
    updating = parity == colour
    off = parity ^ colour
    end_parity = iota((1, width), 1) & 1

    first_pair, step, count = pairs

    def pair(j, carry):
        k = first_pair + step * j
        a, b = 2 * k + 1, 2 * k + 2
        for at, swap in ((PAD - 1, 1 - colour), (PAD + rows, colour)):
            line = slice(at, at + 1)
            other[line, :] = jnp.where(end_parity == swap, fluid[b, line, :], fluid[a, line, :])
        for start in range(0, rows, ROWS):
            inner = slice(PAD + start, PAD + start + ROWS)
            other[inner, :] = jnp.where(updating, fluid[b, inner, :], fluid[a, inner, :])
        for start in range(0, rows, ROWS):
            inner = slice(PAD + start, PAD + start + ROWS)
            edge = pltpu.roll(zedge[start : start + ROWS, :], LANES - 1 - 2 * k, axis=1)
            shared = (
                other[PAD + start - 1 : PAD + start + ROWS - 1, :]
                + other[PAD + start + 1 : PAD + start + ROWS + 1, :]
                + lane_neighbours(other[inner, :], edge, edge)
            )
            here_a = fluid[a, inner, :]
            here_b = fluid[b, inner, :]
            total_a = shared + fluid[a - 1, inner, :] + here_b
            total_b = shared + fluid[b + 1, inner, :] + here_a
            new_a = (here_a + FLUID_DIFFUSION * total_a) * FLUID_SCALE
            new_b = (here_b + FLUID_DIFFUSION * total_b) * FLUID_SCALE
            mask_a = active[a - 1, start : start + ROWS, :] > off
            mask_b = active[b - 1, start : start + ROWS, :] > 1 - off
            fluid[a, inner, :] = jnp.where(mask_a, new_a, here_a)
            fluid[b, inner, :] = jnp.where(mask_b, new_b, here_b)
        if done is not None:
            done(k)
        return carry

    lax.fori_loop(0, count, pair, 0)


def fin_neighbours(fin, d, hedge, fin_rows):
    inner = slice(PAD, PAD + fin_rows)
    here = fin[d + 1, inner, :]
    edge = pltpu.roll(hedge, LANES - 1 - 2 * d, axis=1)
    total = (
        fin[d, inner, :]
        + fin[d + 2, inner, :]
        + fin[d + 1, PAD - 1 : PAD + fin_rows - 1, :]
        + fin[d + 1, PAD + 1 : PAD + fin_rows + 1, :]
        + lane_neighbours(here, edge, edge)
    )
    return here, total


def solution(mesh):
    in_specs = (
        P("gx", "gy", "grp"),
        P("gx", "gy", "grp"),
        P("grp", "gx", "gy"),
        P("grp", "gx", "gy"),
        P("gx", "gy", None, None),
        P("gx", "gy", None),
    )
    out_specs = (P("gx", "gy", "grp"), P("grp", "gx", "gy"))
    count = mesh.shape["gx"]
    groups = mesh.shape["grp"]
    sides = mesh.shape["gy"]
    assert sides == 2 and groups % 2 == 0 and count % 2 == 0
    ring = count == 4
    vmem = pl.BlockSpec(memory_space=pltpu.VMEM)
    hbm = pl.BlockSpec(memory_space=pl.ANY)

    def local(fluid_temp, active, fin_temp, fin_source, wall_owner, wall_target):
        cells, rows, width = fluid_temp.shape
        depth, fin_rows, fin_width = fin_temp.shape
        assert rows == LANES and width == fin_width == 2 * rows and fin_rows == 2 * cells
        assert 2 * depth <= LANES and depth % 8 == 0 and depth >= 24 and cells % 2 == 0 and cells >= 4 and rows % ROWS == 0 and fin_rows == ROWS
        dims = (cells, rows, width, depth, fin_rows, fin_width)
        half = rows // 2
        pairs = cells // 2
        face_rows = half + depth
        wall_rows = fin_rows + cells
        small_rows = cells + fin_rows
        gx_rows = face_rows + (wall_rows if ring else 0)
        owners = wall_owner.reshape(cells, rows)
        targets = wall_target.reshape(cells, rows)
        f32 = lambda *shape: jax.ShapeDtypeStruct(shape, jnp.float32)
        params = pltpu.CompilerParams(vmem_limit_bytes=32 * 1024 * 1024)
        fluid_pad = f32(cells + 2, rows + 2 * PAD, width)
        fin_pad = f32(depth + 2, fin_rows + 2 * PAD, fin_width)
        faces = (f32(small_rows, width), f32(small_rows, width), f32(small_rows, width))

        def start_gx_kernel(fluid_hbm, fin_hbm, own_hbm, tgt_hbm, gxa, gxb, wall,
                            planes, bottom, low_rows, high_rows, root, own, tgt, sems):
            def copy(k, source, target):
                return pltpu.make_async_copy(source, target, sems.at[k])

            last = cells - 1
            copies = [
                copy(0, own_hbm, own),
                copy(1, tgt_hbm, tgt),
                copy(2, fluid_hbm.at[:, :, pl.ds(0, LANES)], bottom),
                copy(3, fin_hbm.at[0], root),
                copy(4, fluid_hbm.at[0], planes.at[0]),
                copy(5, fluid_hbm.at[last], planes.at[1]),
                copy(6, fin_hbm.at[:, pl.ds(0, PAD), :], low_rows),
                copy(7, fin_hbm.at[:, pl.ds(fin_rows - PAD, PAD), :], high_rows),
            ]
            for item in copies:
                item.start()
            for item in copies:
                item.wait()
            shape = (cells, rows)
            shift = tgt[...] - 2 * (iota(shape, 0) * fin_width + iota(shape, 1))
            row_shift = (shift >= fin_width).astype(jnp.int32)
            code = own[...] * 4 + row_shift * 2 + (shift - row_shift * fin_width)
            wall[fin_rows:, LANES:] = code.astype(jnp.float32)
            wall[fin_rows:, 0:LANES] = lane_column(lambda i: bottom[i, :, 0:1], cells, rows)
            even_rows = dot(interleave_matrix(fin_rows), root[...], ((0,), (0,)))
            wall[0:fin_rows, :] = dot(even_rows, interleave_matrix(fin_width), ((1,), (0,)))
            gx = lax.axis_index("gx")
            pack_gx(
                lambda high: planes[jnp.where(high, 1, 0)],
                lambda d, high: jnp.where(high, high_rows[d, PAD - 1 : PAD, :], low_rows[d, 0:1, :]),
                1, gx, gxa, gxb, dims,
            )
            if ring:
                gxa[face_rows:, :] = wall[...]
                gxb[face_rows:, :] = wall[...]

        fluid_hbm, fin_hbm, owners, targets = (
            pltpu.with_memory_space_constraint(v, pltpu.HBM)
            for v in (fluid_temp, fin_temp, owners, targets)
        )
        in_hbm = pl.BlockSpec(memory_space=pltpu.HBM)
        buffer = lambda *shape: pltpu.VMEM(shape, jnp.float32)
        gxa, gxb, wall = pl.pallas_call(
            start_gx_kernel,
            out_shape=(f32(gx_rows, width), f32(gx_rows, width), f32(wall_rows, width)),
            in_specs=[in_hbm] * 4,
            out_specs=(vmem,) * 3,
            scratch_shapes=[buffer(2, rows, width), buffer(cells, rows, LANES),
                            buffer(depth, PAD, fin_width), buffer(depth, PAD, fin_width),
                            buffer(fin_rows, fin_width), pltpu.VMEM((cells, rows), jnp.int32),
                            pltpu.VMEM((cells, rows), jnp.int32), pltpu.SemaphoreType.DMA((8,))],
            compiler_params=params,
            name="start_gx",
        )(fluid_hbm, fin_hbm, owners, targets)

        def start_rest_kernel(fluid_in, fin_in, fluid, fin, grpa, grpb, gyx):
            def fluid_plane(i):
                fluid[i + 1, PAD : PAD + rows, :] = fluid_in[i]

            def fin_plane(d):
                fin[d + 1, PAD : PAD + fin_rows, :] = fin_in[d]

            repeat(cells, fluid_plane, 2)
            repeat(depth, fin_plane, 8)
            clear_rows(fin)
            pack_rest(fluid, fin, grpa, grpb, gyx, my_place(), dims)

        def clear_rows(fin):
            empty = jnp.zeros((depth, PAD, fin_width), jnp.float32)
            fin[1 : depth + 1, 0:PAD, :] = empty
            fin[1 : depth + 1, PAD + fin_rows :, :] = empty

        fluid0, fin0, grpa, grpb, gyx = pl.pallas_call(
            start_rest_kernel,
            out_shape=(fluid_pad, fin_pad) + faces,
            in_specs=[vmem, vmem],
            out_specs=(vmem,) * 5,
            compiler_params=params,
            name="start_rest",
        )(fluid_temp, fin_temp)

        def pairings(axis, size):
            cores = [(g, c) for g in range(size) for c in range(sides)]
            number = {core: k for k, core in enumerate(cores)}

            def partner(g, c):
                other = g - 1 if g % 2 == 0 else g + 1
                return (other, c) if 0 <= other < size else (g, 1 - c)

            first = [(number[g, c], number[g ^ 1, c]) for g, c in cores]
            second = [(number[g, c], number[partner(g, c)]) for g, c in cores]
            return (axis, "gy"), first, second

        def exchange(axis, size, paira, pairb):
            axes, first, second = pairings(axis, size)
            return lax.ppermute(paira, axes, first), lax.ppermute(pairb, axes, second)

        def swap(side):
            return lax.ppermute(side, "gy", [(0, 1), (1, 0)])

        def mixed_with(k):
            return [(i, i ^ k) for i in range(count)]

        if ring:
            walls = [wall, lax.ppermute(wall, "gx", mixed_with(2))]
            gxa = lax.ppermute(gxa, "gx", mixed_with(1))
            gxb = lax.ppermute(gxb, "gx", mixed_with(3))
        else:
            gxa, gxb = exchange("gx", count, gxa, gxb)
            walls = [wall, lax.all_gather(wall, "gx")]
        side = swap(gyx)
        grpa, grpb = exchange("grp", groups, grpa, grpb)

        def fin_depth_halos(fin, paira, pairb):
            below, above = grp_halos(paira, pairb, lax.axis_index("grp"), groups)
            fin[0, PAD : PAD + fin_rows, :] = below[cells:, :]
            fin[depth + 1, PAD : PAD + fin_rows, :] = above[cells:, :]

        def fin_first(fin, src, first, rest, hedge, block):
            for j in range(8):
                d = block * 8 + j
                here, total = fin_neighbours(fin, d, hedge, fin_rows)
                rhs = here + src[d]
                first[d + 1, PAD : PAD + fin_rows, :] = (rhs + FIN_CONDUCTION * total) * (1.0 / DIAG)
                rest[d] = rhs * (OMEGA / DIAG) + here * (1.0 - OMEGA)

        def fin_second(first, rest, hedge, block):
            for j in range(8):
                d = block * 8 + j
                _, total = fin_neighbours(first, d, hedge, fin_rows)
                rest[d] = rest[d] + (OMEGA * FIN_CONDUCTION / DIAG) * total

        blocks = depth // 8

        def inner_blocks(body):
            def step(k, carry):
                body(k)
                return carry

            lax.fori_loop(1, blocks - 1, step, 0)

        def middle_fin_kernel(fin, src, side, first, rest):
            hedge = side[cells : cells + fin_rows, 0:LANES]
            inner_blocks(lambda k: fin_first(fin, src, first, rest, hedge, k))
            clear_rows(first)

        first, rest = pl.pallas_call(
            middle_fin_kernel,
            out_shape=(fin_pad, f32(depth, fin_rows, fin_width)),
            in_specs=[vmem] * 3,
            out_specs=(vmem,) * 2,
            compiler_params=params,
            name="middle_fin",
        )(fin0, fin_source, side)

        def middle_gx_kernel(_0, _1, _2, _3, src, act, gxa_in, gxb_in, paira, pairb, side, own,
                             other_wall, fluid, fin, first, rest, ghost_out, zedge, gxa, gxb,
                             zrows, other):
            place = my_place()
            grp, gx, _ = place
            on_wall = grp == 0
            fin_depth_halos(fin, paira, pairb)
            hedge = side[cells : cells + fin_rows, 0:LANES]
            for block in (0, blocks - 1):
                fin_first(fin, src, first, rest, hedge, block)
            own_code = own[fin_rows:, LANES:]
            if ring:
                slots = [(gx, own), (gx ^ 1, gxa_in.at[pl.ds(face_rows, wall_rows), :]),
                         (gx ^ 3, gxb_in.at[pl.ds(face_rows, wall_rows), :]), (gx ^ 2, other_wall)]
            else:
                slots = [(s, other_wall.at[s]) for s in range(count)]
            quadrants = [(a * cells, b * LANES) for a in range(2) for b in range(2)]
            ghost = jnp.zeros((cells, rows), jnp.float32)
            deposits = [jnp.zeros((cells, rows), jnp.float32) for _ in quadrants]
            mine = (4 * gx).astype(jnp.float32)
            for owner, ref in slots:
                theirs = own_code - (4 * jnp.asarray(owner, jnp.int32)).astype(jnp.float32)
                temps = ref[fin_rows:, 0:LANES]
                wanted = ref[fin_rows:, LANES:] - mine
                for q, (r, c) in enumerate(quadrants):
                    ghost = jnp.where(theirs == q, ref[r : r + cells, c : c + LANES], ghost)
                    flux = HEAT_COEF * (temps - own[r : r + cells, c : c + LANES])
                    deposits[q] = deposits[q] + jnp.where(wanted == q, flux, 0.0)
            ghost_out[...] = ghost

            @pl.when(on_wall)
            def _():
                split = jnp.concatenate(
                    [jnp.concatenate(deposits[0:2], axis=1), jnp.concatenate(deposits[2:4], axis=1)],
                    axis=0,
                )
                mixed = dot(split, interleave_matrix(fin_width), ((1,), (1,)))
                landed = dot(interleave_matrix(fin_rows), mixed, ((1,), (0,)))
                first[1, PAD : PAD + fin_rows, :] += landed * (1.0 / DIAG)
                rest[0] += landed * (OMEGA / DIAG)

            even, inside = sides_of(gx, count)
            high_row = PAD + fin_rows - 1
            row_a = jnp.where(even, high_row, PAD)
            row_b = PAD + high_row - row_a
            scale = FIN_CONDUCTION / DIAG

            def add_row(d):
                first[d + 1, pl.ds(row_a, 1), :] += gxa_in[pl.ds(half + d, 1), :] * scale
                first[d + 1, pl.ds(row_b, 1), :] += gxb_in[pl.ds(half + d, 1), :] * (scale * inside)

            repeat(depth, add_row)
            below, above = grp_halos(paira, pairb, grp, groups)
            low_face = jnp.where(on_wall, ghost, below[0:cells, 0:LANES])
            unpack_fluid(fluid, zrows, zedge, gxa_in, gxb_in, low_face, above[0:cells, 0:LANES],
                         side, 0, place, count, dims)
            fluid_sweep(fluid, act, zedge, other, 0, dims, (0, pairs - 1, 2))
            pack_gx(
                lambda high: fluid[jnp.where(high, cells, 1), PAD : PAD + rows, :],
                lambda d, high: first[d + 1, pl.ds(jnp.where(high, high_row, PAD), 1), :],
                0, gx, gxa, gxb, dims,
            )

        zrows_buffer, zedge_buffer = buffer(LANES, rows), buffer(rows, LANES)
        other_buffer = buffer(rows + 2 * PAD, width)
        fluid1, _, first, rest, ghost, zedge, gxa, gxb = pl.pallas_call(
            middle_gx_kernel,
            out_shape=(fluid_pad, fin_pad, fin_pad, f32(depth, fin_rows, fin_width), f32(cells, rows),
                       f32(rows, LANES), f32(face_rows, width), f32(face_rows, width)),
            in_specs=[vmem] * 13,
            out_specs=(vmem,) * 8,
            scratch_shapes=[zrows_buffer, other_buffer],
            input_output_aliases={0: 0, 1: 1, 2: 2, 3: 3},
            compiler_params=params,
            name="middle_gx",
        )(fluid0, fin0, first, rest, fin_source, active, gxa, gxb, grpa, grpb, side, *walls)
        gxa, gxb = exchange("gx", count, gxa, gxb)

        def middle_rest_kernel(_, act, zedge, first, fluid, grpa, grpb, gyx, other):
            fluid_sweep(fluid, act, zedge, other, 0, dims, (1, 1, pairs - 2))
            pack_rest(fluid, first, grpa, grpb, gyx, my_place(), dims)

        fluid2, grpa, grpb, gyx = pl.pallas_call(
            middle_rest_kernel,
            out_shape=(fluid_pad,) + faces,
            in_specs=[vmem] * 4,
            out_specs=(vmem,) * 4,
            scratch_shapes=[other_buffer],
            input_output_aliases={0: 0},
            compiler_params=params,
            name="middle_rest",
        )(fluid1, active, zedge, first)
        side = swap(gyx)
        grpa, grpb = exchange("grp", groups, grpa, grpb)

        def end_fin_kernel(_, first, side, rest):
            hedge = side[cells : cells + fin_rows, 0:LANES]
            inner_blocks(lambda k: fin_second(first, rest, hedge, k))

        rest = pl.pallas_call(
            end_fin_kernel,
            out_shape=f32(depth, fin_rows, fin_width),
            in_specs=[vmem] * 3,
            out_specs=vmem,
            input_output_aliases={0: 0},
            compiler_params=params,
            name="end_fin",
        )(rest, first, side)

        def end_kernel(_0, _1, _2, act, ghost, gxa, gxb, paira, pairb, side,
                       fluid, first, rest, fluid_new, fin_new,
                       zrows, zedge, other, fluid_sems, fin_sems):
            place = my_place()
            on_wall = place[0] == 0

            def fluid_copy(k):
                return pltpu.make_async_copy(
                    fluid.at[pl.ds(2 * k + 1, 2), pl.ds(PAD, rows), :],
                    fluid_new.at[pl.ds(2 * k, 2)], fluid_sems.at[k],
                )

            def fin_copy(k, start, size):
                part = pl.ds(start, size)
                return pltpu.make_async_copy(rest.at[part], fin_new.at[part], fin_sems.at[k])

            fin_depth_halos(first, paira, pairb)
            hedge = side[cells : cells + fin_rows, 0:LANES]
            for block in (0, blocks - 1):
                fin_second(first, rest, hedge, block)
            even, inside = sides_of(place[1], count)
            row_a = jnp.where(even, fin_rows - 1, 0)
            row_b = fin_rows - 1 - row_a
            scale = OMEGA * FIN_CONDUCTION / DIAG

            def add_row(d):
                rest[d, pl.ds(row_a, 1), :] += gxa[pl.ds(half + d, 1), :] * scale
                rest[d, pl.ds(row_b, 1), :] += gxb[pl.ds(half + d, 1), :] * (scale * inside)

            repeat(depth, add_row)
            fin_copies = [fin_copy(0, 0, depth)]
            fin_copies[0].start()
            below, above = grp_halos(paira, pairb, place[0], groups)
            low_face = jnp.where(on_wall, ghost[...], below[0:cells, 0:LANES])
            unpack_fluid(fluid, zrows, zedge, gxa, gxb, low_face, above[0:cells, 0:LANES], side, 1,
                         place, count, dims)
            fluid_sweep(fluid, act, zedge, other, 1, dims, (0, 1, pairs),
                        lambda k: fluid_copy(k).start())

            def finish(k, carry):
                fluid_copy(k).wait()
                return carry

            for item in fin_copies:
                item.wait()
            lax.fori_loop(0, pairs, finish, 0)

        results = pl.pallas_call(
            end_kernel,
            out_shape=(fluid_pad, fin_pad, f32(depth, fin_rows, fin_width),
                       f32(cells, rows, width), f32(depth, fin_rows, fin_width)),
            in_specs=[vmem] * 10,
            out_specs=(vmem, vmem, vmem, hbm, hbm),
            scratch_shapes=[zrows_buffer, zedge_buffer, other_buffer,
                            pltpu.SemaphoreType.DMA((pairs,)), pltpu.SemaphoreType.DMA((1,))],
            input_output_aliases={0: 0, 1: 1, 2: 2},
            compiler_params=params,
            name="end",
        )(fluid2, first, rest, active, ghost, gxa, gxb, grpa, grpb, side)
        return results[3], results[4]

    return jax.shard_map(local, mesh=mesh, in_specs=in_specs, out_specs=out_specs, check_vma=False)
```

```python
import jax
import jax.numpy as jnp
from jax import lax
from jax.experimental import pallas as pl
from jax.experimental.pallas import tpu as pltpu
from jax.sharding import PartitionSpec as P


FLUID_DIFFUSION = 1.0
FIN_CONDUCTION = 1.0
HEAT_COEF = 1.0
DIAG = 1.0 + 6.0 * FIN_CONDUCTION
SPECTRAL = 6.0 * FIN_CONDUCTION / DIAG
OMEGA = 1.0 / (1.0 - SPECTRAL * SPECTRAL / 2.0)
FLUID_SCALE = 1.0 / (1.0 + 6.0 * FLUID_DIFFUSION)
LANES = 128
PAD = 8
ROWS = 32
HIGHEST = lax.Precision.HIGHEST


def iota(shape, axis):
    return lax.broadcasted_iota(jnp.int32, shape, axis)


def repeat(count, body, step=8):
    def trip(k, carry):
        for j in range(step):
            body(k * step + j)
        return carry

    lax.fori_loop(0, count // step, trip, 0)


def tiles(value):
    return [value[:, k : k + LANES] for k in range(0, value.shape[1], LANES)]


def lane_neighbours(block, low, high):
    parts = tiles(block)
    lane = iota(parts[0].shape, 1)
    down = [pltpu.roll(part, 1, axis=1) for part in parts]
    up = [pltpu.roll(part, LANES - 1, axis=1) for part in parts]
    below = [jnp.where(lane == 0, a, b) for a, b in zip([low] + down[:-1], down)]
    above = [jnp.where(lane == LANES - 1, a, b) for a, b in zip(up[1:] + [high], up)]
    return jnp.concatenate([a + b for a, b in zip(below, above)], axis=1)


def interleave_matrix(count):
    row = iota((count, count), 0)
    col = iota((count, count), 1)
    half = count // 2
    source = jnp.where(col < half, 2 * col, 2 * (col - half) + 1)
    return (row == source).astype(jnp.float32)


def dot(a, b, contract):
    return lax.dot_general(
        a, b, (contract, ((), ())), precision=HIGHEST, preferred_element_type=jnp.float32
    )


def checker_pack(plane, parity):
    rows = plane.shape[0] // 2
    top = plane[:rows]
    bottom = plane[rows:]
    colour = (iota(top.shape, 0) + iota(top.shape, 1)) & 1
    return jnp.where(colour == parity, top, pltpu.roll(bottom, 1, axis=1))


def lane_column(column, cells, rows):
    kept = jnp.zeros((rows, LANES), jnp.float32)
    lane = iota((rows, LANES), 1)
    for i in range(cells):
        kept = jnp.where(lane == i, column(i), kept)
    return kept.T[:cells]


def pack_gx(plane, row, colour, gx, senda, sendb, dims):
    cells, rows, _, depth, _, _ = dims
    half = rows // 2
    even = gx % 2 == 0
    for send, high in ((senda, even), (sendb, jnp.logical_not(even))):
        parity = jnp.where(high, (colour + cells - 1) % 2, colour)
        send[0:half, :] = checker_pack(plane(high), parity)

    def lines(d):
        senda[pl.ds(half + d, 1), :] = row(d, even)
        sendb[pl.ds(half + d, 1), :] = row(d, jnp.logical_not(even))

    repeat(depth, lines)


def pack_rest(fluid, fin, colour, grpa, grpb, gyx, place, dims):
    cells, rows, width, depth, fin_rows, fin_width = dims
    grp, _, gy = place
    even = grp % 2 == 0
    odd_row = (iota((rows, 1), 0) & 1) == 1
    inner = slice(PAD, PAD + rows)

    def face(lane, swap):
        column = slice(lane, lane + 1)
        return lane_column(
            lambda k: jnp.where(
                odd_row == swap, fluid[2 * k + 2, inner, column], fluid[2 * k + 1, inner, column]
            ),
            cells // 2, rows,
        )

    low, high = face(0, colour == 1), face(width - 1, colour == 0)
    grpa[0 : cells // 2, 0:LANES] = jnp.where(even, high, low)
    grpb[0 : cells // 2, 0:LANES] = jnp.where(even, low, high)
    up = jnp.where(even, depth, 1)
    grpa[cells : cells + fin_rows, :] = fin[up, PAD : PAD + fin_rows, :]
    grpb[cells : cells + fin_rows, :] = fin[depth + 1 - up, PAD : PAD + fin_rows, :]
    edge = PAD + (1 - gy) * (rows - 1)
    for i in range(cells):
        gyx[i : i + 1, :] = fluid[i + 1, pl.ds(edge, 1), :]
    lane = iota((fin_rows, LANES), 1)

    def columns(at, side):
        kept = jnp.zeros((fin_rows, LANES), jnp.float32)
        for d in range(depth):
            column = fin[d + 1, PAD : PAD + fin_rows, at : at + 1]
            kept = jnp.where(lane == 2 * d + side, column, kept)
        gyx[cells : cells + fin_rows, 0:LANES] = kept

    @pl.when(gy == 0)
    def _():
        columns(fin_width - 1, 1)

    @pl.when(gy != 0)
    def _():
        columns(0, 0)


def my_place():
    return [lax.axis_index(name) for name in ("grp", "gx", "gy")]


def sides_of(at, count):
    return at % 2 == 0, jnp.where((at == 0) | (at == count - 1), 0.0, 1.0)


def grp_halos(paira, pairb, grp, groups):
    even, inside = sides_of(grp, groups)
    a, b = paira[...], pairb[...] * inside
    return jnp.where(even, b, a), jnp.where(even, a, b)


def unpack_lines(fluid, side, gy, dims):
    cells, rows, _, _, _, _ = dims
    low_on = jnp.where(gy == 0, 0.0, 1.0)
    high_on = 1.0 - low_on
    for i in range(cells):
        line = side[i : i + 1, :]
        fluid[i + 1, PAD - 1 : PAD, :] = line * low_on
        fluid[i + 1, PAD + rows : PAD + rows + 1, :] = line * high_on


def unpack_fluid(fluid, zrows, zedge, paira, pairb, ghost, below, above, colour, place, count,
                 dims):
    cells, rows, width, _, _, _ = dims
    half = rows // 2
    grp, gx, _ = place
    even, inside = sides_of(gx, count)
    high_plane = jnp.where(even, cells + 1, 0)
    for plane, ref, on in ((high_plane, paira, 1.0), (cells + 1 - high_plane, pairb, inside)):
        packed = ref[0:half, :] * on
        fluid[plane, PAD : PAD + half, :] = packed
        fluid[plane, PAD + half : PAD + rows, :] = pltpu.roll(packed, width - 1, axis=1)
    odd_row = (iota((1, rows), 1) & 1) == 1
    for k in range(cells // 2):
        first, second = ghost[2 * k : 2 * k + 1, :], ghost[2 * k + 1 : 2 * k + 2, :]
        merged = jnp.where(odd_row == (colour == 0), second, first)
        zrows[2 * k : 2 * k + 1, :] = above[k : k + 1, 0:rows]
        zrows[2 * k + 1 : 2 * k + 2, :] = jnp.where(grp == 0, merged, below[k : k + 1, 0:rows])
    zrows[cells:, :] = jnp.zeros((LANES - cells, rows), jnp.float32)
    zedge[...] = zrows[...].T


def fluid_sweep(fluid, active, zedge, other, colour, dims, pairs, done=None):
    _, rows, width, _, _, _ = dims
    parity = (iota((ROWS, width), 0) + iota((ROWS, width), 1)) & 1
    updating = parity == colour
    off = parity ^ colour
    end_parity = iota((1, width), 1) & 1

    first_pair, step, count = pairs

    def pair(j, carry):
        k = first_pair + step * j
        a, b = 2 * k + 1, 2 * k + 2
        for at, swap in ((PAD - 1, 1 - colour), (PAD + rows, colour)):
            line = slice(at, at + 1)
            other[line, :] = jnp.where(end_parity == swap, fluid[b, line, :], fluid[a, line, :])
        for start in range(0, rows, ROWS):
            inner = slice(PAD + start, PAD + start + ROWS)
            other[inner, :] = jnp.where(updating, fluid[b, inner, :], fluid[a, inner, :])
        for start in range(0, rows, ROWS):
            inner = slice(PAD + start, PAD + start + ROWS)
            edge = pltpu.roll(zedge[start : start + ROWS, :], LANES - 1 - 2 * k, axis=1)
            shared = (
                other[PAD + start - 1 : PAD + start + ROWS - 1, :]
                + other[PAD + start + 1 : PAD + start + ROWS + 1, :]
                + lane_neighbours(other[inner, :], edge, edge)
            )
            here_a = fluid[a, inner, :]
            here_b = fluid[b, inner, :]
            total_a = shared + fluid[a - 1, inner, :] + here_b
            total_b = shared + fluid[b + 1, inner, :] + here_a
            new_a = (here_a + FLUID_DIFFUSION * total_a) * FLUID_SCALE
            new_b = (here_b + FLUID_DIFFUSION * total_b) * FLUID_SCALE
            mask_a = active[a - 1, start : start + ROWS, :] > off
            mask_b = active[b - 1, start : start + ROWS, :] > 1 - off
            fluid[a, inner, :] = jnp.where(mask_a, new_a, here_a)
            fluid[b, inner, :] = jnp.where(mask_b, new_b, here_b)
        if done is not None:
            done(k)
        return carry

    lax.fori_loop(0, count, pair, 0)


def fin_neighbours(fin, d, hedge, fin_rows):
    inner = slice(PAD, PAD + fin_rows)
    here = fin[d + 1, inner, :]
    edge = pltpu.roll(hedge, LANES - 1 - 2 * d, axis=1)
    total = (
        fin[d, inner, :]
        + fin[d + 2, inner, :]
        + fin[d + 1, PAD - 1 : PAD + fin_rows - 1, :]
        + fin[d + 1, PAD + 1 : PAD + fin_rows + 1, :]
        + lane_neighbours(here, edge, edge)
    )
    return here, total


def solution(mesh):
    in_specs = (
        P("gx", "gy", "grp"),
        P("gx", "gy", "grp"),
        P("grp", "gx", "gy"),
        P("grp", "gx", "gy"),
        P("gx", "gy", None, None),
        P("gx", "gy", None),
    )
    out_specs = (P("gx", "gy", "grp"), P("grp", "gx", "gy"))
    count = mesh.shape["gx"]
    groups = mesh.shape["grp"]
    sides = mesh.shape["gy"]
    assert sides == 2 and groups % 2 == 0 and count % 2 == 0
    ring = count == 4
    vmem = pl.BlockSpec(memory_space=pltpu.VMEM)
    hbm = pl.BlockSpec(memory_space=pl.ANY)

    def local(fluid_temp, active, fin_temp, fin_source, wall_owner, wall_target):
        cells, rows, width = fluid_temp.shape
        depth, fin_rows, fin_width = fin_temp.shape
        assert rows == LANES and width == fin_width == 2 * rows and fin_rows == 2 * cells
        assert 2 * depth <= LANES and depth % 8 == 0 and depth >= 24 and cells % 2 == 0 and cells >= 4 and rows % ROWS == 0 and fin_rows == ROWS
        dims = (cells, rows, width, depth, fin_rows, fin_width)
        half = rows // 2
        pairs = cells // 2
        face_rows = half + depth
        wall_rows = fin_rows + cells
        gx_rows = face_rows + (wall_rows if ring else 0)
        small_rows = cells + fin_rows
        owners = wall_owner.reshape(cells, rows)
        targets = wall_target.reshape(cells, rows)
        f32 = lambda *shape: jax.ShapeDtypeStruct(shape, jnp.float32)
        params = pltpu.CompilerParams(vmem_limit_bytes=32 * 1024 * 1024)
        fluid_pad = f32(cells + 2, rows + 2 * PAD, width)
        fin_pad = f32(depth + 2, fin_rows + 2 * PAD, fin_width)
        faces = (f32(small_rows, width), f32(small_rows, width), f32(small_rows, width))

        def start_gx_kernel(fluid_hbm, fin_hbm, own_hbm, tgt_hbm, gxa, gxb, wall,
                            planes, bottom, low_rows, high_rows, root, own, tgt, sems):
            def copy(k, source, target):
                return pltpu.make_async_copy(source, target, sems.at[k])

            last = cells - 1
            copies = [
                copy(0, own_hbm, own),
                copy(1, tgt_hbm, tgt),
                copy(2, fluid_hbm.at[:, :, pl.ds(0, LANES)], bottom),
                copy(3, fin_hbm.at[0], root),
                copy(4, fluid_hbm.at[0], planes.at[0]),
                copy(5, fluid_hbm.at[last], planes.at[1]),
                copy(6, fin_hbm.at[:, pl.ds(0, PAD), :], low_rows),
                copy(7, fin_hbm.at[:, pl.ds(fin_rows - PAD, PAD), :], high_rows),
            ]
            for item in copies:
                item.start()
            for item in copies:
                item.wait()
            shape = (cells, rows)
            shift = tgt[...] - 2 * (iota(shape, 0) * fin_width + iota(shape, 1))
            row_shift = (shift >= fin_width).astype(jnp.int32)
            code = own[...] * 4 + row_shift * 2 + (shift - row_shift * fin_width)
            wall[fin_rows:, LANES:] = code.astype(jnp.float32)
            wall[fin_rows:, 0:LANES] = lane_column(lambda i: bottom[i, :, 0:1], cells, rows)
            even_rows = dot(interleave_matrix(fin_rows), root[...], ((0,), (0,)))
            wall[0:fin_rows, :] = dot(even_rows, interleave_matrix(fin_width), ((1,), (0,)))
            gx = lax.axis_index("gx")
            pack_gx(
                lambda high: planes[jnp.where(high, 1, 0)],
                lambda d, high: jnp.where(high, high_rows[d, PAD - 1 : PAD, :], low_rows[d, 0:1, :]),
                1, gx, gxa, gxb, dims,
            )
            if ring:
                gxa[face_rows:, :] = wall[...]
                gxb[face_rows:, :] = wall[...]

        fluid_hbm, fin_hbm, owners, targets = (
            pltpu.with_memory_space_constraint(v, pltpu.HBM)
            for v in (fluid_temp, fin_temp, owners, targets)
        )
        in_hbm = pl.BlockSpec(memory_space=pltpu.HBM)
        buffer = lambda *shape: pltpu.VMEM(shape, jnp.float32)
        gxa, gxb, wall = pl.pallas_call(
            start_gx_kernel,
            out_shape=(f32(gx_rows, width), f32(gx_rows, width), f32(wall_rows, width)),
            in_specs=[in_hbm] * 4,
            out_specs=(vmem,) * 3,
            scratch_shapes=[buffer(2, rows, width), buffer(cells, rows, LANES),
                            buffer(depth, PAD, fin_width), buffer(depth, PAD, fin_width),
                            buffer(fin_rows, fin_width), pltpu.VMEM((cells, rows), jnp.int32),
                            pltpu.VMEM((cells, rows), jnp.int32), pltpu.SemaphoreType.DMA((8,))],
            compiler_params=params,
            name="start_gx",
        )(fluid_hbm, fin_hbm, owners, targets)

        def start_rest_kernel(fluid_in, fin_in, fluid, fin, grpa, grpb, gyx):
            def fluid_plane(i):
                fluid[i + 1, PAD : PAD + rows, :] = fluid_in[i]

            def fin_plane(d):
                fin[d + 1, PAD : PAD + fin_rows, :] = fin_in[d]

            repeat(cells, fluid_plane, 2)
            repeat(depth, fin_plane, 8)
            clear_rows(fin)
            pack_rest(fluid, fin, 0, grpa, grpb, gyx, my_place(), dims)

        def clear_rows(fin):
            empty = jnp.zeros((depth, PAD, fin_width), jnp.float32)
            fin[1 : depth + 1, 0:PAD, :] = empty
            fin[1 : depth + 1, PAD + fin_rows :, :] = empty

        fluid0, fin0, grpa, grpb, gyx = pl.pallas_call(
            start_rest_kernel,
            out_shape=(fluid_pad, fin_pad) + faces,
            in_specs=[vmem, vmem],
            out_specs=(vmem,) * 5,
            compiler_params=params,
            name="start_rest",
        )(fluid_temp, fin_temp)

        def pairings(axis, size):
            cores = [(g, c) for g in range(size) for c in range(sides)]
            number = {core: k for k, core in enumerate(cores)}

            def partner(g, c):
                other = g - 1 if g % 2 == 0 else g + 1
                return (other, c) if 0 <= other < size else (g, 1 - c)

            first = [(number[g, c], number[g ^ 1, c]) for g, c in cores]
            second = [(number[g, c], number[partner(g, c)]) for g, c in cores]
            return (axis, "gy"), first, second

        def exchange(axis, size, paira, pairb):
            axes, first, second = pairings(axis, size)
            paira = lax.ppermute(paira, axes, first)
            pairb = lax.ppermute(pairb, axes, second)
            return paira, pairb

        def swap(side):
            return lax.ppermute(side, "gy", [(0, 1), (1, 0)])

        def mixed_with(k):
            return [(i, i ^ k) for i in range(count)]

        if ring:
            walls = [wall, lax.ppermute(wall, "gx", mixed_with(2))]
            gxa = lax.ppermute(gxa, "gx", mixed_with(1))
            gxb = lax.ppermute(gxb, "gx", mixed_with(3))
        else:
            gxa, gxb = exchange("gx", count, gxa, gxb)
            walls = [wall, lax.all_gather(wall, "gx")]
        side = swap(gyx)
        grpa, grpb = exchange("grp", groups, grpa, grpb)

        def fin_depth_halos(fin, paira, pairb):
            below, above = grp_halos(paira, pairb, lax.axis_index("grp"), groups)
            fin[0, PAD : PAD + fin_rows, :] = below[cells:, :]
            fin[depth + 1, PAD : PAD + fin_rows, :] = above[cells:, :]

        def fin_first(fin, src, first, rest, hedge, block):
            for j in range(8):
                d = block * 8 + j
                here, total = fin_neighbours(fin, d, hedge, fin_rows)
                rhs = here + src[d]
                first[d + 1, PAD : PAD + fin_rows, :] = (rhs + FIN_CONDUCTION * total) * (1.0 / DIAG)
                rest[d] = rhs * (OMEGA / DIAG) + here * (1.0 - OMEGA)

        def fin_second(first, rest, hedge, block):
            for j in range(8):
                d = block * 8 + j
                _, total = fin_neighbours(first, d, hedge, fin_rows)
                rest[d] = rest[d] + (OMEGA * FIN_CONDUCTION / DIAG) * total

        blocks = depth // 8

        def inner_blocks(body):
            def step(k, carry):
                body(k)
                return carry

            lax.fori_loop(1, blocks - 1, step, 0)

        def middle_fin_kernel(fin, src, side, _, first, rest):
            hedge = side[cells : cells + fin_rows, 0:LANES]
            inner_blocks(lambda k: fin_first(fin, src, first, rest, hedge, k))
            clear_rows(first)

        first, rest = pl.pallas_call(
            middle_fin_kernel,
            out_shape=(fin_pad, f32(depth, fin_rows, fin_width)),
            in_specs=[vmem] * 4,
            out_specs=(vmem,) * 2,
            compiler_params=params,
            name="middle_fin",
        )(fin0, fin_source, side, active)

        def middle_grp_kernel(_0, _1, _2, _3, src, paira, pairb, side, fluid, fin, first, rest):
            fin_depth_halos(fin, paira, pairb)
            hedge = side[cells : cells + fin_rows, 0:LANES]
            for block in (0, blocks - 1):
                fin_first(fin, src, first, rest, hedge, block)
            unpack_lines(fluid, side, lax.axis_index("gy"), dims)

        fin_rest = f32(depth, fin_rows, fin_width)
        fluid0, _, first, rest = pl.pallas_call(
            middle_grp_kernel,
            out_shape=(fluid_pad, fin_pad, fin_pad, fin_rest),
            in_specs=[vmem] * 8,
            out_specs=(vmem,) * 4,
            input_output_aliases={0: 0, 1: 1, 2: 2, 3: 3},
            compiler_params=params,
            name="middle_grp",
        )(fluid0, fin0, first, rest, fin_source, grpa, grpb, side)

        def middle_gx_kernel(*refs):
            (act, gxa_in, gxb_in, paira, pairb, own), refs = refs[3:9], refs[9:]
            wall_refs, refs = refs[: len(walls) - 1], refs[len(walls) - 1 :]
            fluid, first, rest, ghost_out, zedge, gxa, gxb, zrows, other = refs
            place = my_place()
            grp, gx, _ = place
            on_wall = grp == 0
            own_code = own[fin_rows:, LANES:]
            if ring:
                slots = [(gx, own), (gx ^ 1, gxa_in.at[pl.ds(face_rows, wall_rows), :]),
                         (gx ^ 3, gxb_in.at[pl.ds(face_rows, wall_rows), :]), (gx ^ 2, wall_refs[0])]
            else:
                slots = [(s, wall_refs[0].at[s]) for s in range(count)]
            quadrants = [(a * cells, b * LANES) for a in range(2) for b in range(2)]
            ghost = jnp.zeros((cells, rows), jnp.float32)
            deposits = [jnp.zeros((cells, rows), jnp.float32) for _ in quadrants]
            mine = (4 * gx).astype(jnp.float32)
            for owner, ref in slots:
                theirs = own_code - (4 * jnp.asarray(owner, jnp.int32)).astype(jnp.float32)
                temps = ref[fin_rows:, 0:LANES]
                wanted = ref[fin_rows:, LANES:] - mine
                for q, (r, c) in enumerate(quadrants):
                    ghost = jnp.where(theirs == q, ref[r : r + cells, c : c + LANES], ghost)
                    flux = HEAT_COEF * (temps - own[r : r + cells, c : c + LANES])
                    deposits[q] = deposits[q] + jnp.where(wanted == q, flux, 0.0)
            ghost_out[...] = ghost

            @pl.when(on_wall)
            def _():
                split = jnp.concatenate(
                    [jnp.concatenate(deposits[0:2], axis=1), jnp.concatenate(deposits[2:4], axis=1)],
                    axis=0,
                )
                mixed = dot(split, interleave_matrix(fin_width), ((1,), (1,)))
                landed = dot(interleave_matrix(fin_rows), mixed, ((1,), (0,)))
                first[1, PAD : PAD + fin_rows, :] += landed * (1.0 / DIAG)
                rest[0] += landed * (OMEGA / DIAG)

            even, inside = sides_of(gx, count)
            high_row = PAD + fin_rows - 1
            row_a = jnp.where(even, high_row, PAD)
            row_b = PAD + high_row - row_a
            scale = FIN_CONDUCTION / DIAG

            def add_row(d):
                first[d + 1, pl.ds(row_a, 1), :] += gxa_in[pl.ds(half + d, 1), :] * scale
                first[d + 1, pl.ds(row_b, 1), :] += gxb_in[pl.ds(half + d, 1), :] * (scale * inside)

            repeat(depth, add_row)
            below, above = grp_halos(paira, pairb, grp, groups)
            unpack_fluid(fluid, zrows, zedge, gxa_in, gxb_in, ghost, below, above, 0, place, count,
                         dims)
            fluid_sweep(fluid, act, zedge, other, 0, dims, (0, pairs - 1, 2))
            pack_gx(
                lambda high: fluid[jnp.where(high, cells, 1), PAD : PAD + rows, :],
                lambda d, high: first[d + 1, pl.ds(jnp.where(high, high_row, PAD), 1), :],
                0, gx, gxa, gxb, dims,
            )

        zrows_buffer, zedge_buffer = buffer(LANES, rows), buffer(rows, LANES)
        other_buffer = buffer(rows + 2 * PAD, width)
        fluid1, first, rest, ghost, zedge, gxa, gxb = pl.pallas_call(
            middle_gx_kernel,
            out_shape=(fluid_pad, fin_pad, fin_rest, f32(cells, rows),
                       f32(rows, LANES), f32(face_rows, width), f32(face_rows, width)),
            in_specs=[vmem] * (8 + len(walls)),
            out_specs=(vmem,) * 7,
            scratch_shapes=[zrows_buffer, other_buffer],
            input_output_aliases={0: 0, 1: 1, 2: 2},
            compiler_params=params,
            name="middle_gx",
        )(fluid0, first, rest, active, gxa, gxb, grpa, grpb, *walls)
        gxa, gxb = exchange("gx", count, gxa, gxb)

        def middle_rest_kernel(_, act, zedge, first, fluid, grpa, grpb, gyx, other):
            fluid_sweep(fluid, act, zedge, other, 0, dims, (1, 1, pairs - 2))
            pack_rest(fluid, first, 1, grpa, grpb, gyx, my_place(), dims)

        fluid2, grpa, grpb, gyx = pl.pallas_call(
            middle_rest_kernel,
            out_shape=(fluid_pad,) + faces,
            in_specs=[vmem] * 4,
            out_specs=(vmem,) * 4,
            scratch_shapes=[other_buffer],
            input_output_aliases={0: 0},
            compiler_params=params,
            name="middle_rest",
        )(fluid1, active, zedge, first)
        side = swap(gyx)
        grpa, grpb = exchange("grp", groups, grpa, grpb)

        def end_fin_kernel(_0, _1, first, side, rest, fluid):
            unpack_lines(fluid, side, lax.axis_index("gy"), dims)
            hedge = side[cells : cells + fin_rows, 0:LANES]
            inner_blocks(lambda k: fin_second(first, rest, hedge, k))

        rest, fluid3 = pl.pallas_call(
            end_fin_kernel,
            out_shape=(fin_rest, fluid_pad),
            in_specs=[vmem] * 4,
            out_specs=(vmem,) * 2,
            input_output_aliases={0: 0, 1: 1},
            compiler_params=params,
            name="end_fin",
        )(rest, fluid2, first, side)

        def end_kernel(_0, _1, _2, act, ghost, gxa, gxb, paira, pairb, side,
                       fluid, first, rest, fluid_new, fin_new,
                       zrows, zedge, other, fluid_sems, fin_sems):
            place = my_place()

            def fluid_copy(k):
                return pltpu.make_async_copy(
                    fluid.at[pl.ds(2 * k + 1, 2), pl.ds(PAD, rows), :],
                    fluid_new.at[pl.ds(2 * k, 2)], fluid_sems.at[k],
                )

            def fin_copy(k, start, size):
                part = pl.ds(start, size)
                return pltpu.make_async_copy(rest.at[part], fin_new.at[part], fin_sems.at[k])

            fin_depth_halos(first, paira, pairb)
            hedge = side[cells : cells + fin_rows, 0:LANES]
            for block in (0, blocks - 1):
                fin_second(first, rest, hedge, block)
            even, inside = sides_of(place[1], count)
            row_a = jnp.where(even, fin_rows - 1, 0)
            row_b = fin_rows - 1 - row_a
            scale = OMEGA * FIN_CONDUCTION / DIAG

            def add_row(d):
                rest[d, pl.ds(row_a, 1), :] += gxa[pl.ds(half + d, 1), :] * scale
                rest[d, pl.ds(row_b, 1), :] += gxb[pl.ds(half + d, 1), :] * (scale * inside)

            repeat(depth, add_row)
            fin_copies = [fin_copy(0, 0, depth)]
            fin_copies[0].start()
            below, above = grp_halos(paira, pairb, place[0], groups)
            unpack_fluid(fluid, zrows, zedge, gxa, gxb, ghost, below, above, 1, place, count, dims)
            fluid_sweep(fluid, act, zedge, other, 1, dims, (0, 1, pairs),
                        lambda k: fluid_copy(k).start())

            def finish(k, carry):
                fluid_copy(k).wait()
                return carry

            for item in fin_copies:
                item.wait()
            lax.fori_loop(0, pairs, finish, 0)

        results = pl.pallas_call(
            end_kernel,
            out_shape=(fluid_pad, fin_pad, f32(depth, fin_rows, fin_width),
                       f32(cells, rows, width), f32(depth, fin_rows, fin_width)),
            in_specs=[vmem] * 10,
            out_specs=(vmem, vmem, vmem, hbm, hbm),
            scratch_shapes=[zrows_buffer, zedge_buffer, other_buffer,
                            pltpu.SemaphoreType.DMA((pairs,)), pltpu.SemaphoreType.DMA((1,))],
            input_output_aliases={0: 0, 1: 1, 2: 2},
            compiler_params=params,
            name="end",
        )(fluid3, first, rest, active, ghost, gxa, gxb, grpa, grpb, side)
        return results[3], results[4]

    return jax.shard_map(local, mesh=mesh, in_specs=in_specs, out_specs=out_specs, check_vma=False)
```

```python
import jax
import jax.numpy as jnp
from jax import lax
from jax.experimental import pallas as pl
from jax.experimental.pallas import tpu as pltpu
from jax.sharding import PartitionSpec as P


FLUID_DIFFUSION = 1.0
FIN_CONDUCTION = 1.0
HEAT_COEF = 1.0
DIAG = 1.0 + 6.0 * FIN_CONDUCTION
SPECTRAL = 6.0 * FIN_CONDUCTION / DIAG
OMEGA = 1.0 / (1.0 - SPECTRAL * SPECTRAL / 2.0)
FLUID_SCALE = 1.0 / (1.0 + 6.0 * FLUID_DIFFUSION)
LANES = 128
PAD = 8
ROWS = 16
HIGHEST = lax.Precision.HIGHEST


def iota(shape, axis):
    return lax.broadcasted_iota(jnp.int32, shape, axis)


def repeat(count, body, step=8):
    def trip(k, carry):
        for j in range(step):
            body(k * step + j)
        return carry

    lax.fori_loop(0, count // step, trip, 0)


def tiles(value):
    return [value[:, k : k + LANES] for k in range(0, value.shape[1], LANES)]


def lane_neighbours(block, low, high):
    parts = tiles(block)
    lane = iota(parts[0].shape, 1)
    down = [pltpu.roll(part, 1, axis=1) for part in parts]
    up = [pltpu.roll(part, LANES - 1, axis=1) for part in parts]
    below = [jnp.where(lane == 0, a, b) for a, b in zip([low] + down[:-1], down)]
    above = [jnp.where(lane == LANES - 1, a, b) for a, b in zip(up[1:] + [high], up)]
    return jnp.concatenate([a + b for a, b in zip(below, above)], axis=1)


def interleave_matrix(count):
    row = iota((count, count), 0)
    col = iota((count, count), 1)
    half = count // 2
    source = jnp.where(col < half, 2 * col, 2 * (col - half) + 1)
    return (row == source).astype(jnp.float32)


def dot(a, b, contract):
    return lax.dot_general(
        a, b, (contract, ((), ())), precision=HIGHEST, preferred_element_type=jnp.float32
    )


def checker_pack(plane, parity):
    rows = plane.shape[0] // 2
    top = plane[:rows]
    bottom = plane[rows:]
    colour = (iota(top.shape, 0) + iota(top.shape, 1)) & 1
    return jnp.where(colour == parity, top, pltpu.roll(bottom, 1, axis=1))


def lane_column(column, cells, rows):
    kept = jnp.zeros((rows, LANES), jnp.float32)
    lane = iota((rows, LANES), 1)
    for i in range(cells):
        kept = jnp.where(lane == i, column(i), kept)
    return kept.T[:cells]


def pack_gx(plane, colour, gx, senda, sendb, dims):
    cells, rows, _, _, _, _ = dims
    half = rows // 2
    even = gx % 2 == 0
    for send, high in ((senda, even), (sendb, jnp.logical_not(even))):
        parity = jnp.where(high, (colour + cells - 1) % 2, colour)
        send[0:half, :] = checker_pack(plane(high), parity)


def pack_rest(fluid, fin, colour, grpa, grpb, gyx, place, dims):
    cells, rows, width, depth, fin_rows, fin_width = dims
    grp, _, gy = place
    even = grp % 2 == 0
    odd_row = (iota((rows, 1), 0) & 1) == 1
    inner = slice(PAD, PAD + rows)

    def face(lane, swap):
        column = slice(lane, lane + 1)
        return lane_column(
            lambda k: jnp.where(
                odd_row == swap, fluid[2 * k + 2, inner, column], fluid[2 * k + 1, inner, column]
            ),
            cells // 2, rows,
        )

    low, high = face(0, colour == 1), face(width - 1, colour == 0)
    grpa[0 : cells // 2, 0:LANES] = jnp.where(even, high, low)
    grpb[0 : cells // 2, 0:LANES] = jnp.where(even, low, high)
    up = jnp.where(even, depth, 1)
    grpa[cells : cells + fin_rows, :] = fin[up, PAD : PAD + fin_rows, :]
    grpb[cells : cells + fin_rows, :] = fin[depth + 1 - up, PAD : PAD + fin_rows, :]
    edge = PAD + (1 - gy) * (rows - 1)
    for i in range(cells):
        gyx[i : i + 1, :] = fluid[i + 1, pl.ds(edge, 1), :]
    lane = iota((fin_rows, LANES), 1)

    def columns(at, side):
        kept = jnp.zeros((fin_rows, LANES), jnp.float32)
        for d in range(depth):
            column = fin[d + 1, PAD : PAD + fin_rows, at : at + 1]
            kept = jnp.where(lane == 2 * d + side, column, kept)
        gyx[cells : cells + fin_rows, 0:LANES] = kept

    @pl.when(gy == 0)
    def _():
        columns(fin_width - 1, 1)

    @pl.when(gy != 0)
    def _():
        columns(0, 0)


def my_place():
    return [lax.axis_index(name) for name in ("grp", "gx", "gy")]


def sides_of(at, count):
    return at % 2 == 0, jnp.where((at == 0) | (at == count - 1), 0.0, 1.0)


def grp_halos(paira, pairb, grp, groups):
    even, inside = sides_of(grp, groups)
    a, b = paira[...], pairb[...] * inside
    return jnp.where(even, b, a), jnp.where(even, a, b)


def unpack_lines(fluid, side, gy, dims):
    cells, rows, _, _, _, _ = dims
    low_on = jnp.where(gy == 0, 0.0, 1.0)
    high_on = 1.0 - low_on
    for i in range(cells):
        line = side[i : i + 1, :]
        fluid[i + 1, PAD - 1 : PAD, :] = line * low_on
        fluid[i + 1, PAD + rows : PAD + rows + 1, :] = line * high_on


def unpack_fluid(fluid, zrows, zedge, paira, pairb, ghost, below, above, colour, place, count,
                 dims):
    cells, rows, width, _, _, _ = dims
    half = rows // 2
    grp, gx, _ = place
    even, inside = sides_of(gx, count)
    high_plane = jnp.where(even, cells + 1, 0)
    for plane, ref, on in ((high_plane, paira, 1.0), (cells + 1 - high_plane, pairb, inside)):
        packed = ref[0:half, :] * on
        fluid[plane, PAD : PAD + half, :] = packed
        fluid[plane, PAD + half : PAD + rows, :] = pltpu.roll(packed, width - 1, axis=1)
    odd_row = (iota((1, rows), 1) & 1) == 1
    for k in range(cells // 2):
        first, second = ghost[2 * k : 2 * k + 1, :], ghost[2 * k + 1 : 2 * k + 2, :]
        merged = jnp.where(odd_row == (colour == 0), second, first)
        zrows[2 * k : 2 * k + 1, :] = above[k : k + 1, 0:rows]
        zrows[2 * k + 1 : 2 * k + 2, :] = jnp.where(grp == 0, merged, below[k : k + 1, 0:rows])
    zrows[cells:, :] = jnp.zeros((LANES - cells, rows), jnp.float32)
    zedge[...] = zrows[...].T


def fluid_sweep(fluid, active, zedge, others, colour, dims, pairs, done=None):
    _, rows, width, _, _, _ = dims
    parity = (iota((ROWS, width), 0) + iota((ROWS, width), 1)) & 1
    updating = parity == colour
    off = parity ^ colour
    end_parity = iota((1, width), 1) & 1
    first_pair, step, trips, group = pairs

    def merge(k, other):
        a, b = 2 * k + 1, 2 * k + 2
        for at, swap in ((PAD - 1, 1 - colour), (PAD + rows, colour)):
            line = slice(at, at + 1)
            other[line, :] = jnp.where(end_parity == swap, fluid[b, line, :], fluid[a, line, :])
        for start in range(0, rows, ROWS):
            inner = slice(PAD + start, PAD + start + ROWS)
            other[inner, :] = jnp.where(updating, fluid[b, inner, :], fluid[a, inner, :])

    def update(k, other):
        a, b = 2 * k + 1, 2 * k + 2
        for start in range(0, rows, ROWS):
            inner = slice(PAD + start, PAD + start + ROWS)
            edge = pltpu.roll(zedge[start : start + ROWS, :], LANES - 1 - 2 * k, axis=1)
            shared = (
                other[PAD + start - 1 : PAD + start + ROWS - 1, :]
                + other[PAD + start + 1 : PAD + start + ROWS + 1, :]
                + lane_neighbours(other[inner, :], edge, edge)
            )
            here_a = fluid[a, inner, :]
            here_b = fluid[b, inner, :]
            total_a = shared + fluid[a - 1, inner, :] + here_b
            total_b = shared + fluid[b + 1, inner, :] + here_a
            new_a = (here_a + FLUID_DIFFUSION * total_a) * FLUID_SCALE
            new_b = (here_b + FLUID_DIFFUSION * total_b) * FLUID_SCALE
            mask_a = active[a - 1, start : start + ROWS, :] > off
            mask_b = active[b - 1, start : start + ROWS, :] > 1 - off
            fluid[a, inner, :] = jnp.where(mask_a, new_a, here_a)
            fluid[b, inner, :] = jnp.where(mask_b, new_b, here_b)

    def trip(j, carry):
        ks = [first_pair + step * (group * j + u) for u in range(group)]
        for u, k in enumerate(ks):
            merge(k, others.at[u])
        for u, k in enumerate(ks):
            update(k, others.at[u])
            if done is not None:
                done(k)
        return carry

    lax.fori_loop(0, trips, trip, 0)


def add_gx_rows(target, offset, rows_at, received, half, scales, depth, sends=None):
    def block(k, carry):
        part = pl.ds(half + 8 * k, 8)
        for n, (row, ref, scale) in enumerate(zip(rows_at, received, scales)):
            halo = ref[part, :] * scale
            new = [
                target[8 * k + j + offset, pl.ds(row, 1), :] + halo[j : j + 1, :] for j in range(8)
            ]
            for j in range(8):
                target[8 * k + j + offset, pl.ds(row, 1), :] = new[j]
            if sends is not None:
                sends[n][part, :] = jnp.concatenate(new, axis=0)
        return carry

    lax.fori_loop(0, depth // 8, block, 0)


def fin_neighbours(fin, d, hedge, fin_rows):
    inner = slice(PAD, PAD + fin_rows)
    here = fin[d + 1, inner, :]
    edge = pltpu.roll(hedge, LANES - 1 - 2 * d, axis=1)
    total = (
        fin[d, inner, :]
        + fin[d + 2, inner, :]
        + fin[d + 1, PAD - 1 : PAD + fin_rows - 1, :]
        + fin[d + 1, PAD + 1 : PAD + fin_rows + 1, :]
        + lane_neighbours(here, edge, edge)
    )
    return here, total


def solution(mesh):
    in_specs = (
        P("gx", "gy", "grp"),
        P("gx", "gy", "grp"),
        P("grp", "gx", "gy"),
        P("grp", "gx", "gy"),
        P("gx", "gy", None, None),
        P("gx", "gy", None),
    )
    out_specs = (P("gx", "gy", "grp"), P("grp", "gx", "gy"))
    count = mesh.shape["gx"]
    groups = mesh.shape["grp"]
    sides = mesh.shape["gy"]
    assert sides == 2 and groups % 2 == 0 and count % 2 == 0
    ring = count == 4
    vmem = pl.BlockSpec(memory_space=pltpu.VMEM)
    hbm = pl.BlockSpec(memory_space=pl.ANY)

    def local(fluid_temp, active, fin_temp, fin_source, wall_owner, wall_target):
        cells, rows, width = fluid_temp.shape
        depth, fin_rows, fin_width = fin_temp.shape
        assert rows == LANES and width == fin_width == 2 * rows and fin_rows == 2 * cells
        assert 2 * depth <= LANES and depth % 8 == 0 and depth >= 24 and cells % 2 == 0 and cells >= 4 and rows % ROWS == 0 and fin_rows % 8 == 0
        dims = (cells, rows, width, depth, fin_rows, fin_width)
        half = rows // 2
        pairs = cells // 2
        outer_group = max(g for g in (1, 2, 4) if pairs % g == 0)
        inner_group = max(g for g in (1, 2, 3) if (pairs - 2) % g == 0)
        face_rows = half + depth
        wall_rows = fin_rows + cells
        gx_rows = face_rows + (wall_rows if ring else 0)
        small_rows = cells + fin_rows
        owners = wall_owner.reshape(cells, rows)
        targets = wall_target.reshape(cells, rows)
        f32 = lambda *shape: jax.ShapeDtypeStruct(shape, jnp.float32)
        params = pltpu.CompilerParams(vmem_limit_bytes=32 * 1024 * 1024)
        fluid_pad = f32(cells + 2, rows + 2 * PAD, width)
        fin_pad = f32(depth + 2, fin_rows + 2 * PAD, fin_width)
        faces = (f32(small_rows, width), f32(small_rows, width), f32(small_rows, width))

        def start_gx_kernel(fluid_hbm, fin_hbm, own_hbm, tgt_hbm, gxa, gxb, wall,
                            planes, bottom, low_rows, high_rows, root, own, tgt, sems):
            def copy(k, source, target):
                return pltpu.make_async_copy(source, target, sems.at[k])

            last = cells - 1
            copies = [
                copy(0, own_hbm, own),
                copy(1, tgt_hbm, tgt),
                copy(2, fluid_hbm.at[:, :, pl.ds(0, LANES)], bottom),
                copy(3, fin_hbm.at[0], root),
                copy(4, fluid_hbm.at[0], planes.at[0]),
                copy(5, fluid_hbm.at[last], planes.at[1]),
                copy(6, fin_hbm.at[:, pl.ds(0, PAD), :], low_rows),
                copy(7, fin_hbm.at[:, pl.ds(fin_rows - PAD, PAD), :], high_rows),
            ]
            for item in copies:
                item.start()
            for item in copies[:4]:
                item.wait()
            shape = (cells, rows)
            shift = tgt[...] - 2 * (iota(shape, 0) * fin_width + iota(shape, 1))
            row_shift = (shift >= fin_width).astype(jnp.int32)
            code = own[...] * 4 + row_shift * 2 + (shift - row_shift * fin_width)
            wall[fin_rows:, LANES:] = code.astype(jnp.float32)
            wall[fin_rows:, 0:LANES] = lane_column(lambda i: bottom[i, :, 0:1], cells, rows)
            even_rows = dot(interleave_matrix(fin_rows), root[...], ((0,), (0,)))
            wall[0:fin_rows, :] = dot(even_rows, interleave_matrix(fin_width), ((1,), (0,)))
            gx = lax.axis_index("gx")
            for item in copies[4:]:
                item.wait()
            pack_gx(lambda high: planes[jnp.where(high, 1, 0)], 1, gx, gxa, gxb, dims)
            even = gx % 2 == 0

            def lines(k, carry):
                part = pl.ds(half + 8 * k, 8)
                low = jnp.concatenate([low_rows[8 * k + j, 0:1, :] for j in range(8)], axis=0)
                high = jnp.concatenate(
                    [high_rows[8 * k + j, PAD - 1 : PAD, :] for j in range(8)], axis=0
                )
                gxa[part, :] = jnp.where(even, high, low)
                gxb[part, :] = jnp.where(even, low, high)
                return carry

            lax.fori_loop(0, depth // 8, lines, 0)
            if ring:
                gxa[face_rows:, :] = wall[...]
                gxb[face_rows:, :] = wall[...]

        fluid_hbm, fin_hbm, owners, targets = (
            pltpu.with_memory_space_constraint(v, pltpu.HBM)
            for v in (fluid_temp, fin_temp, owners, targets)
        )
        in_hbm = pl.BlockSpec(memory_space=pltpu.HBM)
        buffer = lambda *shape: pltpu.VMEM(shape, jnp.float32)
        gxa, gxb, wall = pl.pallas_call(
            start_gx_kernel,
            out_shape=(f32(gx_rows, width), f32(gx_rows, width), f32(wall_rows, width)),
            in_specs=[in_hbm] * 4,
            out_specs=(vmem,) * 3,
            scratch_shapes=[buffer(2, rows, width), buffer(cells, rows, LANES),
                            buffer(depth, PAD, fin_width), buffer(depth, PAD, fin_width),
                            buffer(fin_rows, fin_width), pltpu.VMEM((cells, rows), jnp.int32),
                            pltpu.VMEM((cells, rows), jnp.int32), pltpu.SemaphoreType.DMA((8,))],
            compiler_params=params,
            name="start_gx",
        )(fluid_hbm, fin_hbm, owners, targets)

        def start_rest_kernel(fluid_in, fin_in, fluid, fin, grpa, grpb, gyx):
            def fluid_plane(i):
                fluid[i + 1, PAD : PAD + rows, :] = fluid_in[i]

            def fin_plane(d):
                fin[d + 1, PAD : PAD + fin_rows, :] = fin_in[d]

            repeat(cells, fluid_plane, 2)
            repeat(depth, fin_plane, 8)
            clear_rows(fin)
            pack_rest(fluid, fin, 0, grpa, grpb, gyx, my_place(), dims)

        def clear_rows(fin):
            empty = jnp.zeros((depth, PAD, fin_width), jnp.float32)
            fin[1 : depth + 1, 0:PAD, :] = empty
            fin[1 : depth + 1, PAD + fin_rows :, :] = empty

        fluid0, fin0, grpa, grpb, gyx = pl.pallas_call(
            start_rest_kernel,
            out_shape=(fluid_pad, fin_pad) + faces,
            in_specs=[vmem, vmem],
            out_specs=(vmem,) * 5,
            compiler_params=params,
            name="start_rest",
        )(fluid_temp, fin_temp)

        def pairings(axis, size):
            cores = [(g, c) for g in range(size) for c in range(sides)]
            number = {core: k for k, core in enumerate(cores)}

            def partner(g, c):
                other = g - 1 if g % 2 == 0 else g + 1
                return (other, c) if 0 <= other < size else (g, 1 - c)

            first = [(number[g, c], number[g ^ 1, c]) for g, c in cores]
            second = [(number[g, c], number[partner(g, c)]) for g, c in cores]
            return (axis, "gy"), first, second

        def exchange(axis, size, paira, pairb):
            axes, first, second = pairings(axis, size)
            paira = lax.ppermute(paira, axes, first)
            pairb = lax.ppermute(pairb, axes, second)
            return paira, pairb

        def swap(side):
            return lax.ppermute(side, "gy", [(0, 1), (1, 0)])

        def mixed_with(k):
            return [(i, i ^ k) for i in range(count)]

        if ring:
            walls = [wall, lax.ppermute(wall, "gx", mixed_with(2))]
            gxa = lax.ppermute(gxa, "gx", mixed_with(1))
            gxb = lax.ppermute(gxb, "gx", mixed_with(3))
        else:
            gxa, gxb = exchange("gx", count, gxa, gxb)
            walls = [wall, lax.all_gather(wall, "gx")]
        side = swap(gyx)
        grpa, grpb = exchange("grp", groups, grpa, grpb)

        def fin_depth_halos(fin, paira, pairb):
            below, above = grp_halos(paira, pairb, lax.axis_index("grp"), groups)
            fin[0, PAD : PAD + fin_rows, :] = below[cells:, :]
            fin[depth + 1, PAD : PAD + fin_rows, :] = above[cells:, :]

        def fin_first(fin, src, first, rest, hedge, block):
            for j in range(8):
                d = block * 8 + j
                here, total = fin_neighbours(fin, d, hedge, fin_rows)
                rhs = here + src[d]
                first[d + 1, PAD : PAD + fin_rows, :] = (rhs + FIN_CONDUCTION * total) * (1.0 / DIAG)
                rest[d] = rhs * (OMEGA / DIAG) + here * (1.0 - OMEGA)

        def fin_second(first, rest, hedge, block):
            for j in range(8):
                d = block * 8 + j
                _, total = fin_neighbours(first, d, hedge, fin_rows)
                rest[d] = rest[d] + (OMEGA * FIN_CONDUCTION / DIAG) * total

        blocks = depth // 8

        def inner_blocks(body):
            def step(k, carry):
                body(k)
                return carry

            lax.fori_loop(1, blocks - 1, step, 0)

        def middle_fin_kernel(fin, src, side, _, first, rest):
            hedge = side[cells : cells + fin_rows, 0:LANES]
            inner_blocks(lambda k: fin_first(fin, src, first, rest, hedge, k))
            clear_rows(first)

        first, rest = pl.pallas_call(
            middle_fin_kernel,
            out_shape=(fin_pad, f32(depth, fin_rows, fin_width)),
            in_specs=[vmem] * 4,
            out_specs=(vmem,) * 2,
            compiler_params=params,
            name="middle_fin",
        )(fin0, fin_source, side, active)

        def middle_grp_kernel(_0, _1, _2, _3, src, paira, pairb, side, fluid, fin, first, rest):
            fin_depth_halos(fin, paira, pairb)
            hedge = side[cells : cells + fin_rows, 0:LANES]
            for block in (0, blocks - 1):
                fin_first(fin, src, first, rest, hedge, block)
            unpack_lines(fluid, side, lax.axis_index("gy"), dims)

        fin_rest = f32(depth, fin_rows, fin_width)
        fluid0, _, first, rest = pl.pallas_call(
            middle_grp_kernel,
            out_shape=(fluid_pad, fin_pad, fin_pad, fin_rest),
            in_specs=[vmem] * 8,
            out_specs=(vmem,) * 4,
            input_output_aliases={0: 0, 1: 1, 2: 2, 3: 3},
            compiler_params=params,
            name="middle_grp",
        )(fluid0, fin0, first, rest, fin_source, grpa, grpb, side)

        def middle_gx_kernel(*refs):
            (act, gxa_in, gxb_in, paira, pairb, own), refs = refs[3:9], refs[9:]
            wall_refs, refs = refs[: len(walls) - 1], refs[len(walls) - 1 :]
            fluid, first, rest, ghost_out, zedge, gxa, gxb, zrows, other = refs
            place = my_place()
            grp, gx, _ = place
            on_wall = grp == 0
            own_code = own[fin_rows:, LANES:]
            if ring:
                slots = [(gx, own), (gx ^ 1, gxa_in.at[pl.ds(face_rows, wall_rows), :]),
                         (gx ^ 3, gxb_in.at[pl.ds(face_rows, wall_rows), :]), (gx ^ 2, wall_refs[0])]
            else:
                slots = [(s, wall_refs[0].at[s]) for s in range(count)]
            quadrants = [(a * cells, b * LANES) for a in range(2) for b in range(2)]
            ghost = jnp.zeros((cells, rows), jnp.float32)
            deposits = [jnp.zeros((cells, rows), jnp.float32) for _ in quadrants]
            mine = (4 * gx).astype(jnp.float32)
            for owner, ref in slots:
                theirs = own_code - (4 * jnp.asarray(owner, jnp.int32)).astype(jnp.float32)
                temps = ref[fin_rows:, 0:LANES]
                wanted = ref[fin_rows:, LANES:] - mine
                for q, (r, c) in enumerate(quadrants):
                    ghost = jnp.where(theirs == q, ref[r : r + cells, c : c + LANES], ghost)
                    flux = HEAT_COEF * (temps - own[r : r + cells, c : c + LANES])
                    deposits[q] = deposits[q] + jnp.where(wanted == q, flux, 0.0)
            ghost_out[...] = ghost

            @pl.when(on_wall)
            def _():
                split = jnp.concatenate(
                    [jnp.concatenate(deposits[0:2], axis=1), jnp.concatenate(deposits[2:4], axis=1)],
                    axis=0,
                )
                mixed = dot(split, interleave_matrix(fin_width), ((1,), (1,)))
                landed = dot(interleave_matrix(fin_rows), mixed, ((1,), (0,)))
                first[1, PAD : PAD + fin_rows, :] += landed * (1.0 / DIAG)
                rest[0] += landed * (OMEGA / DIAG)

            even, inside = sides_of(gx, count)
            high_row = PAD + fin_rows - 1
            row_a = jnp.where(even, high_row, PAD)
            row_b = PAD + high_row - row_a
            scale = FIN_CONDUCTION / DIAG
            add_gx_rows(first, 1, (row_a, row_b), (gxa_in, gxb_in), half, (scale, scale * inside),
                        depth, (gxa, gxb))
            below, above = grp_halos(paira, pairb, grp, groups)
            unpack_fluid(fluid, zrows, zedge, gxa_in, gxb_in, ghost, below, above, 0, place, count,
                         dims)
            fluid_sweep(fluid, act, zedge, other, 0, dims, (0, pairs - 1, 1, 2))
            pack_gx(
                lambda high: fluid[jnp.where(high, cells, 1), PAD : PAD + rows, :], 0, gx, gxa, gxb,
                dims,
            )

        zrows_buffer, zedge_buffer = buffer(LANES, rows), buffer(rows, LANES)
        other_buffer = lambda planes: buffer(planes, rows + 2 * PAD, width)
        fluid1, first, rest, ghost, zedge, gxa, gxb = pl.pallas_call(
            middle_gx_kernel,
            out_shape=(fluid_pad, fin_pad, fin_rest, f32(cells, rows),
                       f32(rows, LANES), f32(face_rows, width), f32(face_rows, width)),
            in_specs=[vmem] * (8 + len(walls)),
            out_specs=(vmem,) * 7,
            scratch_shapes=[zrows_buffer, other_buffer(2)],
            input_output_aliases={0: 0, 1: 1, 2: 2},
            compiler_params=params,
            name="middle_gx",
        )(fluid0, first, rest, active, gxa, gxb, grpa, grpb, *walls)
        gxa, gxb = exchange("gx", count, gxa, gxb)

        def middle_rest_kernel(_, act, zedge, first, fluid, grpa, grpb, gyx, other):
            fluid_sweep(fluid, act, zedge, other, 0, dims, (1, 1, (pairs - 2) // inner_group, inner_group))
            pack_rest(fluid, first, 1, grpa, grpb, gyx, my_place(), dims)

        fluid2, grpa, grpb, gyx = pl.pallas_call(
            middle_rest_kernel,
            out_shape=(fluid_pad,) + faces,
            in_specs=[vmem] * 4,
            out_specs=(vmem,) * 4,
            scratch_shapes=[other_buffer(inner_group)],
            input_output_aliases={0: 0},
            compiler_params=params,
            name="middle_rest",
        )(fluid1, active, zedge, first)
        side = swap(gyx)
        grpa, grpb = exchange("grp", groups, grpa, grpb)

        def end_fin_kernel(_0, _1, first, side, rest, fluid):
            unpack_lines(fluid, side, lax.axis_index("gy"), dims)
            hedge = side[cells : cells + fin_rows, 0:LANES]
            inner_blocks(lambda k: fin_second(first, rest, hedge, k))

        rest, fluid3 = pl.pallas_call(
            end_fin_kernel,
            out_shape=(fin_rest, fluid_pad),
            in_specs=[vmem] * 4,
            out_specs=(vmem,) * 2,
            input_output_aliases={0: 0, 1: 1},
            compiler_params=params,
            name="end_fin",
        )(rest, fluid2, first, side)

        def end_kernel(_0, _1, _2, act, ghost, gxa, gxb, paira, pairb, side,
                       fluid, first, rest, fluid_new, fin_new,
                       zrows, zedge, other, fluid_sems, fin_sems):
            place = my_place()

            def fluid_copy(k):
                return pltpu.make_async_copy(
                    fluid.at[pl.ds(2 * k + 1, 2), pl.ds(PAD, rows), :],
                    fluid_new.at[pl.ds(2 * k, 2)], fluid_sems.at[k],
                )

            def fin_copy(k, start, size):
                part = pl.ds(start, size)
                return pltpu.make_async_copy(rest.at[part], fin_new.at[part], fin_sems.at[k])

            fin_depth_halos(first, paira, pairb)
            hedge = side[cells : cells + fin_rows, 0:LANES]
            for block in (0, blocks - 1):
                fin_second(first, rest, hedge, block)
            even, inside = sides_of(place[1], count)
            row_a = jnp.where(even, fin_rows - 1, 0)
            row_b = fin_rows - 1 - row_a
            scale = OMEGA * FIN_CONDUCTION / DIAG
            add_gx_rows(rest, 0, (row_a, row_b), (gxa, gxb), half, (scale, scale * inside), depth)
            fin_copies = [fin_copy(0, 0, depth)]
            fin_copies[0].start()
            below, above = grp_halos(paira, pairb, place[0], groups)
            unpack_fluid(fluid, zrows, zedge, gxa, gxb, ghost, below, above, 1, place, count, dims)
            fluid_sweep(fluid, act, zedge, other, 1, dims, (0, 1, pairs // outer_group, outer_group),
                        lambda k: fluid_copy(k).start())

            def finish(k, carry):
                fluid_copy(k).wait()
                return carry

            for item in fin_copies:
                item.wait()
            lax.fori_loop(0, pairs, finish, 0)

        results = pl.pallas_call(
            end_kernel,
            out_shape=(fluid_pad, fin_pad, f32(depth, fin_rows, fin_width),
                       f32(cells, rows, width), f32(depth, fin_rows, fin_width)),
            in_specs=[vmem] * 10,
            out_specs=(vmem, vmem, vmem, hbm, hbm),
            scratch_shapes=[zrows_buffer, zedge_buffer, other_buffer(outer_group),
                            pltpu.SemaphoreType.DMA((pairs,)), pltpu.SemaphoreType.DMA((1,))],
            input_output_aliases={0: 0, 1: 1, 2: 2},
            compiler_params=params,
            name="end",
        )(fluid3, first, rest, active, ghost, gxa, gxb, grpa, grpb, side)
        return results[3], results[4]

    return jax.shard_map(local, mesh=mesh, in_specs=in_specs, out_specs=out_specs, check_vma=False)
```

```python
import jax
import jax.numpy as jnp
from jax import lax
from jax.experimental import pallas as pl
from jax.experimental.pallas import tpu as pltpu
from jax.sharding import PartitionSpec as P


FLUID_DIFFUSION = 1.0
FIN_CONDUCTION = 1.0
HEAT_COEF = 1.0
DIAG = 1.0 + 6.0 * FIN_CONDUCTION
SPECTRAL = 6.0 * FIN_CONDUCTION / DIAG
OMEGA = 1.0 / (1.0 - SPECTRAL * SPECTRAL / 2.0)
FLUID_SCALE = 1.0 / (1.0 + 6.0 * FLUID_DIFFUSION)
LANES = 128
PAD = 8
ROWS = 16
HIGHEST = lax.Precision.HIGHEST


def iota(shape, axis):
    return lax.broadcasted_iota(jnp.int32, shape, axis)


def repeat(count, body, step=8):
    def trip(k, carry):
        for j in range(step):
            body(k * step + j)
        return carry

    lax.fori_loop(0, count // step, trip, 0)


def tiles(value):
    return [value[:, k : k + LANES] for k in range(0, value.shape[1], LANES)]


def lane_neighbours(block, low, high):
    parts = tiles(block)
    lane = iota(parts[0].shape, 1)
    down = [pltpu.roll(part, 1, axis=1) for part in parts]
    up = [pltpu.roll(part, LANES - 1, axis=1) for part in parts]
    below = [jnp.where(lane == 0, a, b) for a, b in zip([low] + down[:-1], down)]
    above = [jnp.where(lane == LANES - 1, a, b) for a, b in zip(up[1:] + [high], up)]
    return jnp.concatenate([a + b for a, b in zip(below, above)], axis=1)


def interleave_matrix(count):
    row = iota((count, count), 0)
    col = iota((count, count), 1)
    half = count // 2
    source = jnp.where(col < half, 2 * col, 2 * (col - half) + 1)
    return (row == source).astype(jnp.float32)


def dot(a, b, contract):
    return lax.dot_general(
        a, b, (contract, ((), ())), precision=HIGHEST, preferred_element_type=jnp.float32
    )


def checker_pack(plane, parity):
    rows = plane.shape[0] // 2
    top = plane[:rows]
    bottom = plane[rows:]
    colour = (iota(top.shape, 0) + iota(top.shape, 1)) & 1
    return jnp.where(colour == parity, top, pltpu.roll(bottom, 1, axis=1))


def lane_column(column, cells, rows):
    kept = jnp.zeros((rows, LANES), jnp.float32)
    lane = iota((rows, LANES), 1)
    for i in range(cells):
        kept = jnp.where(lane == i, column(i), kept)
    return kept.T[:cells]


def pack_gx(plane, colour, gx, senda, sendb, dims):
    cells, rows, _, _, _, _ = dims
    half = rows // 2
    even = gx % 2 == 0
    for send, high in ((senda, even), (sendb, jnp.logical_not(even))):
        parity = jnp.where(high, (colour + cells - 1) % 2, colour)
        send[0:half, :] = checker_pack(plane(high), parity)


def pack_rest(fluid, fin, colour, grpa, grpb, gyx, place, dims):
    cells, rows, width, depth, fin_rows, fin_width = dims
    grp, _, gy = place
    even = grp % 2 == 0
    odd_row = (iota((rows, 1), 0) & 1) == 1
    inner = slice(PAD, PAD + rows)

    def face(lane, swap):
        column = slice(lane, lane + 1)
        return lane_column(
            lambda k: jnp.where(
                odd_row == swap, fluid[2 * k + 2, inner, column], fluid[2 * k + 1, inner, column]
            ),
            cells // 2, rows,
        )

    low, high = face(0, colour == 1), face(width - 1, colour == 0)
    grpa[0 : cells // 2, 0:LANES] = jnp.where(even, high, low)
    grpb[0 : cells // 2, 0:LANES] = jnp.where(even, low, high)
    up = jnp.where(even, depth, 1)
    grpa[cells : cells + fin_rows, :] = fin[up, PAD : PAD + fin_rows, :]
    grpb[cells : cells + fin_rows, :] = fin[depth + 1 - up, PAD : PAD + fin_rows, :]
    edge = PAD + (1 - gy) * (rows - 1)
    for i in range(cells):
        gyx[i : i + 1, :] = fluid[i + 1, pl.ds(edge, 1), :]
    lane = iota((fin_rows, LANES), 1)

    def columns(at, side):
        kept = jnp.zeros((fin_rows, LANES), jnp.float32)
        for d in range(depth):
            column = fin[d + 1, PAD : PAD + fin_rows, at : at + 1]
            kept = jnp.where(lane == 2 * d + side, column, kept)
        gyx[cells : cells + fin_rows, 0:LANES] = kept

    @pl.when(gy == 0)
    def _():
        columns(fin_width - 1, 1)

    @pl.when(gy != 0)
    def _():
        columns(0, 0)


def my_place():
    return [lax.axis_index(name) for name in ("grp", "gx", "gy")]


def sides_of(at, count):
    return at % 2 == 0, jnp.where((at == 0) | (at == count - 1), 0.0, 1.0)


def grp_halos(paira, pairb, grp, groups):
    even, inside = sides_of(grp, groups)
    a, b = paira[...], pairb[...] * inside
    return jnp.where(even, b, a), jnp.where(even, a, b)


def unpack_lines(fluid, side, gy, dims):
    cells, rows, _, _, _, _ = dims
    low_on = jnp.where(gy == 0, 0.0, 1.0)
    high_on = 1.0 - low_on
    for i in range(cells):
        line = side[i : i + 1, :]
        fluid[i + 1, PAD - 1 : PAD, :] = line * low_on
        fluid[i + 1, PAD + rows : PAD + rows + 1, :] = line * high_on


def unpack_fluid(fluid, zrows, zedge, paira, pairb, ghost, below, above, colour, place, count,
                 dims):
    cells, rows, width, _, _, _ = dims
    half = rows // 2
    grp, gx, _ = place
    even, inside = sides_of(gx, count)
    high_plane = jnp.where(even, cells + 1, 0)
    for plane, ref, on in ((high_plane, paira, 1.0), (cells + 1 - high_plane, pairb, inside)):
        packed = ref[0:half, :] * on
        fluid[plane, PAD : PAD + half, :] = packed
        fluid[plane, PAD + half : PAD + rows, :] = pltpu.roll(packed, width - 1, axis=1)
    odd_row = (iota((1, rows), 1) & 1) == 1
    for k in range(cells // 2):
        first, second = ghost[2 * k : 2 * k + 1, :], ghost[2 * k + 1 : 2 * k + 2, :]
        merged = jnp.where(odd_row == (colour == 0), second, first)
        zrows[2 * k : 2 * k + 1, :] = above[k : k + 1, 0:rows]
        zrows[2 * k + 1 : 2 * k + 2, :] = jnp.where(grp == 0, merged, below[k : k + 1, 0:rows])
    zrows[cells:, :] = jnp.zeros((LANES - cells, rows), jnp.float32)
    zedge[...] = zrows[...].T


def neighbour_sums(fluid, others, sums, colour, dims, pairs):
    _, rows, width, _, _, _ = dims
    updating = ((iota((ROWS, width), 0) + iota((ROWS, width), 1)) & 1) == colour
    end_parity = iota((1, width), 1) & 1
    first_pair, step, trips, group = pairs
    empty = jnp.zeros((ROWS, LANES), jnp.float32)

    def merge(k, other):
        a, b = 2 * k + 1, 2 * k + 2
        for at, swap in ((PAD - 1, 1 - colour), (PAD + rows, colour)):
            line = slice(at, at + 1)
            other[line, :] = jnp.where(end_parity == swap, fluid[b, line, :], fluid[a, line, :])
        for start in range(0, rows, ROWS):
            inner = slice(PAD + start, PAD + start + ROWS)
            other[inner, :] = jnp.where(updating, fluid[b, inner, :], fluid[a, inner, :])

    def add(other, total):
        for start in range(0, rows, ROWS):
            inner = slice(PAD + start, PAD + start + ROWS)
            total[start : start + ROWS, :] = (
                other[PAD + start - 1 : PAD + start + ROWS - 1, :]
                + other[PAD + start + 1 : PAD + start + ROWS + 1, :]
                + lane_neighbours(other[inner, :], empty, empty)
            )

    def trip(j, carry):
        ns = [group * j + u for u in range(group)]
        for u, n in enumerate(ns):
            merge(first_pair + step * n, others.at[u])
        for u, n in enumerate(ns):
            add(others.at[u], sums.at[n])
        return carry

    lax.fori_loop(0, trips, trip, 0)


def fluid_update(fluid, active, zedge, sums, colour, dims, pairs, done=None):
    _, rows, width, _, _, _ = dims
    off = ((iota((ROWS, width), 0) + iota((ROWS, width), 1)) & 1) ^ colour
    lane = iota((ROWS, LANES), 1)
    first_pair, step, trips, group = pairs

    def update(k, total):
        a, b = 2 * k + 1, 2 * k + 2
        for start in range(0, rows, ROWS):
            inner = slice(PAD + start, PAD + start + ROWS)
            edge = pltpu.roll(zedge[start : start + ROWS, :], LANES - 1 - 2 * k, axis=1)
            parts = tiles(total[start : start + ROWS, :])
            parts[0] = parts[0] + jnp.where(lane == 0, edge, 0.0)
            parts[-1] = parts[-1] + jnp.where(lane == LANES - 1, edge, 0.0)
            shared = jnp.concatenate(parts, axis=1)
            here_a = fluid[a, inner, :]
            here_b = fluid[b, inner, :]
            total_a = shared + fluid[a - 1, inner, :] + here_b
            total_b = shared + fluid[b + 1, inner, :] + here_a
            new_a = (here_a + FLUID_DIFFUSION * total_a) * FLUID_SCALE
            new_b = (here_b + FLUID_DIFFUSION * total_b) * FLUID_SCALE
            mask_a = active[a - 1, start : start + ROWS, :] > off
            mask_b = active[b - 1, start : start + ROWS, :] > 1 - off
            fluid[a, inner, :] = jnp.where(mask_a, new_a, here_a)
            fluid[b, inner, :] = jnp.where(mask_b, new_b, here_b)

    def trip(j, carry):
        for u in range(group):
            n = group * j + u
            update(first_pair + step * n, sums.at[n])
            if done is not None:
                done(first_pair + step * n)
        return carry

    lax.fori_loop(0, trips, trip, 0)


def add_gx_rows(target, offset, rows_at, received, half, scales, depth, sends=None):
    def block(k, carry):
        part = pl.ds(half + 8 * k, 8)
        for n, (row, ref, scale) in enumerate(zip(rows_at, received, scales)):
            halo = ref[part, :] * scale
            new = [
                target[8 * k + j + offset, pl.ds(row, 1), :] + halo[j : j + 1, :] for j in range(8)
            ]
            for j in range(8):
                target[8 * k + j + offset, pl.ds(row, 1), :] = new[j]
            if sends is not None:
                sends[n][part, :] = jnp.concatenate(new, axis=0)
        return carry

    lax.fori_loop(0, depth // 8, block, 0)


def fin_neighbours(fin, d, hedge, fin_rows):
    inner = slice(PAD, PAD + fin_rows)
    here = fin[d + 1, inner, :]
    edge = pltpu.roll(hedge, LANES - 1 - 2 * d, axis=1)
    total = (
        fin[d, inner, :]
        + fin[d + 2, inner, :]
        + fin[d + 1, PAD - 1 : PAD + fin_rows - 1, :]
        + fin[d + 1, PAD + 1 : PAD + fin_rows + 1, :]
        + lane_neighbours(here, edge, edge)
    )
    return here, total


def solution(mesh):
    in_specs = (
        P("gx", "gy", "grp"),
        P("gx", "gy", "grp"),
        P("grp", "gx", "gy"),
        P("grp", "gx", "gy"),
        P("gx", "gy", None, None),
        P("gx", "gy", None),
    )
    out_specs = (P("gx", "gy", "grp"), P("grp", "gx", "gy"))
    count = mesh.shape["gx"]
    groups = mesh.shape["grp"]
    sides = mesh.shape["gy"]
    assert sides == 2 and groups % 2 == 0 and count % 2 == 0
    ring = count == 4
    vmem = pl.BlockSpec(memory_space=pltpu.VMEM)
    hbm = pl.BlockSpec(memory_space=pl.ANY)

    def local(fluid_temp, active, fin_temp, fin_source, wall_owner, wall_target):
        cells, rows, width = fluid_temp.shape
        depth, fin_rows, fin_width = fin_temp.shape
        assert rows == LANES and width == fin_width == 2 * rows and fin_rows == 2 * cells
        assert 2 * depth <= LANES and depth % 8 == 0 and depth >= 24 and cells % 2 == 0 and cells >= 4 and rows % ROWS == 0 and fin_rows % 8 == 0
        dims = (cells, rows, width, depth, fin_rows, fin_width)
        half = rows // 2
        pairs = cells // 2
        outer_group = max(g for g in (1, 2, 4) if pairs % g == 0)
        inner_group = max(g for g in (1, 2, 3) if (pairs - 2) % g == 0)
        face_rows = half + depth
        wall_rows = fin_rows + cells
        gx_rows = face_rows + (wall_rows if ring else 0)
        small_rows = cells + fin_rows
        owners = wall_owner.reshape(cells, rows)
        targets = wall_target.reshape(cells, rows)
        f32 = lambda *shape: jax.ShapeDtypeStruct(shape, jnp.float32)
        params = pltpu.CompilerParams(vmem_limit_bytes=32 * 1024 * 1024)
        fluid_pad = f32(cells + 2, rows + 2 * PAD, width)
        fin_pad = f32(depth + 2, fin_rows + 2 * PAD, fin_width)
        faces = (f32(small_rows, width), f32(small_rows, width), f32(small_rows, width))

        def start_gx_kernel(fluid_hbm, fin_hbm, own_hbm, tgt_hbm, gxa, gxb, wall,
                            planes, bottom, low_rows, high_rows, root, own, tgt, sems):
            def copy(k, source, target):
                return pltpu.make_async_copy(source, target, sems.at[k])

            last = cells - 1
            copies = [
                copy(0, own_hbm, own),
                copy(1, tgt_hbm, tgt),
                copy(2, fluid_hbm.at[:, :, pl.ds(0, LANES)], bottom),
                copy(3, fin_hbm.at[0], root),
                copy(4, fluid_hbm.at[0], planes.at[0]),
                copy(5, fluid_hbm.at[last], planes.at[1]),
                copy(6, fin_hbm.at[:, pl.ds(0, PAD), :], low_rows),
                copy(7, fin_hbm.at[:, pl.ds(fin_rows - PAD, PAD), :], high_rows),
            ]
            for item in copies:
                item.start()
            for item in copies[:4]:
                item.wait()
            shape = (cells, rows)
            shift = tgt[...] - 2 * (iota(shape, 0) * fin_width + iota(shape, 1))
            row_shift = (shift >= fin_width).astype(jnp.int32)
            code = own[...] * 4 + row_shift * 2 + (shift - row_shift * fin_width)
            wall[fin_rows:, LANES:] = code.astype(jnp.float32)
            wall[fin_rows:, 0:LANES] = lane_column(lambda i: bottom[i, :, 0:1], cells, rows)
            even_rows = dot(interleave_matrix(fin_rows), root[...], ((0,), (0,)))
            wall[0:fin_rows, :] = dot(even_rows, interleave_matrix(fin_width), ((1,), (0,)))
            gx = lax.axis_index("gx")
            for item in copies[4:]:
                item.wait()
            pack_gx(lambda high: planes[jnp.where(high, 1, 0)], 1, gx, gxa, gxb, dims)
            even = gx % 2 == 0

            def lines(k, carry):
                part = pl.ds(half + 8 * k, 8)
                low = jnp.concatenate([low_rows[8 * k + j, 0:1, :] for j in range(8)], axis=0)
                high = jnp.concatenate(
                    [high_rows[8 * k + j, PAD - 1 : PAD, :] for j in range(8)], axis=0
                )
                gxa[part, :] = jnp.where(even, high, low)
                gxb[part, :] = jnp.where(even, low, high)
                return carry

            lax.fori_loop(0, depth // 8, lines, 0)
            if ring:
                gxa[face_rows:, :] = wall[...]
                gxb[face_rows:, :] = wall[...]

        fluid_hbm, fin_hbm, owners, targets = (
            pltpu.with_memory_space_constraint(v, pltpu.HBM)
            for v in (fluid_temp, fin_temp, owners, targets)
        )
        in_hbm = pl.BlockSpec(memory_space=pltpu.HBM)
        buffer = lambda *shape: pltpu.VMEM(shape, jnp.float32)
        gxa, gxb, wall = pl.pallas_call(
            start_gx_kernel,
            out_shape=(f32(gx_rows, width), f32(gx_rows, width), f32(wall_rows, width)),
            in_specs=[in_hbm] * 4,
            out_specs=(vmem,) * 3,
            scratch_shapes=[buffer(2, rows, width), buffer(cells, rows, LANES),
                            buffer(depth, PAD, fin_width), buffer(depth, PAD, fin_width),
                            buffer(fin_rows, fin_width), pltpu.VMEM((cells, rows), jnp.int32),
                            pltpu.VMEM((cells, rows), jnp.int32), pltpu.SemaphoreType.DMA((8,))],
            compiler_params=params,
            name="start_gx",
        )(fluid_hbm, fin_hbm, owners, targets)

        def start_rest_kernel(fluid_in, fin_in, fluid, fin, grpa, grpb, gyx):
            def fluid_plane(i):
                fluid[i + 1, PAD : PAD + rows, :] = fluid_in[i]

            def fin_plane(d):
                fin[d + 1, PAD : PAD + fin_rows, :] = fin_in[d]

            repeat(cells, fluid_plane, 2)
            repeat(depth, fin_plane, 8)
            clear_rows(fin)
            pack_rest(fluid, fin, 0, grpa, grpb, gyx, my_place(), dims)

        def clear_rows(fin):
            empty = jnp.zeros((depth, PAD, fin_width), jnp.float32)
            fin[1 : depth + 1, 0:PAD, :] = empty
            fin[1 : depth + 1, PAD + fin_rows :, :] = empty

        fluid0, fin0, grpa, grpb, gyx = pl.pallas_call(
            start_rest_kernel,
            out_shape=(fluid_pad, fin_pad) + faces,
            in_specs=[vmem, vmem],
            out_specs=(vmem,) * 5,
            compiler_params=params,
            name="start_rest",
        )(fluid_temp, fin_temp)

        def pairings(axis, size):
            cores = [(g, c) for g in range(size) for c in range(sides)]
            number = {core: k for k, core in enumerate(cores)}

            def partner(g, c):
                other = g - 1 if g % 2 == 0 else g + 1
                return (other, c) if 0 <= other < size else (g, 1 - c)

            first = [(number[g, c], number[g ^ 1, c]) for g, c in cores]
            second = [(number[g, c], number[partner(g, c)]) for g, c in cores]
            return (axis, "gy"), first, second

        def exchange(axis, size, paira, pairb):
            axes, first, second = pairings(axis, size)
            paira = lax.ppermute(paira, axes, first)
            pairb = lax.ppermute(pairb, axes, second)
            return paira, pairb

        def swap(side):
            return lax.ppermute(side, "gy", [(0, 1), (1, 0)])

        def mixed_with(k):
            return [(i, i ^ k) for i in range(count)]

        if ring:
            walls = [wall, lax.ppermute(wall, "gx", mixed_with(2))]
            gxa = lax.ppermute(gxa, "gx", mixed_with(1))
            gxb = lax.ppermute(gxb, "gx", mixed_with(3))
        else:
            gxa, gxb = exchange("gx", count, gxa, gxb)
            walls = [wall, lax.all_gather(wall, "gx")]
        side = swap(gyx)
        grpa, grpb = exchange("grp", groups, grpa, grpb)

        def fin_depth_halos(fin, paira, pairb):
            below, above = grp_halos(paira, pairb, lax.axis_index("grp"), groups)
            fin[0, PAD : PAD + fin_rows, :] = below[cells:, :]
            fin[depth + 1, PAD : PAD + fin_rows, :] = above[cells:, :]

        def fin_first(fin, src, first, rest, hedge, block):
            for j in range(8):
                d = block * 8 + j
                here, total = fin_neighbours(fin, d, hedge, fin_rows)
                rhs = here + src[d]
                first[d + 1, PAD : PAD + fin_rows, :] = (rhs + FIN_CONDUCTION * total) * (1.0 / DIAG)
                rest[d] = rhs * (OMEGA / DIAG) + here * (1.0 - OMEGA)

        def fin_second(first, rest, hedge, block):
            for j in range(8):
                d = block * 8 + j
                _, total = fin_neighbours(first, d, hedge, fin_rows)
                rest[d] = rest[d] + (OMEGA * FIN_CONDUCTION / DIAG) * total

        blocks = depth // 8

        def inner_blocks(body):
            def step(k, carry):
                body(k)
                return carry

            lax.fori_loop(1, blocks - 1, step, 0)

        def middle_fin_kernel(fin, src, side, _, first, rest):
            hedge = side[cells : cells + fin_rows, 0:LANES]
            inner_blocks(lambda k: fin_first(fin, src, first, rest, hedge, k))
            clear_rows(first)

        first, rest = pl.pallas_call(
            middle_fin_kernel,
            out_shape=(fin_pad, f32(depth, fin_rows, fin_width)),
            in_specs=[vmem] * 4,
            out_specs=(vmem,) * 2,
            compiler_params=params,
            name="middle_fin",
        )(fin0, fin_source, side, active)

        def middle_grp_kernel(_0, _1, _2, _3, src, paira, pairb, side, fluid, fin, first, rest,
                              sums, others):
            fin_depth_halos(fin, paira, pairb)
            hedge = side[cells : cells + fin_rows, 0:LANES]
            for block in (0, blocks - 1):
                fin_first(fin, src, first, rest, hedge, block)
            unpack_lines(fluid, side, lax.axis_index("gy"), dims)
            neighbour_sums(fluid, others, sums, 0, dims, outer_pairs)

        fin_rest = f32(depth, fin_rows, fin_width)
        other_buffer = lambda planes: buffer(planes, rows + 2 * PAD, width)
        outer_pairs = (0, pairs - 1, 1, 2)
        fluid0, _, first, rest, sums = pl.pallas_call(
            middle_grp_kernel,
            out_shape=(fluid_pad, fin_pad, fin_pad, fin_rest, f32(2, rows, width)),
            in_specs=[vmem] * 8,
            out_specs=(vmem,) * 5,
            scratch_shapes=[other_buffer(2)],
            input_output_aliases={0: 0, 1: 1, 2: 2, 3: 3},
            compiler_params=params,
            name="middle_grp",
        )(fluid0, fin0, first, rest, fin_source, grpa, grpb, side)

        def middle_gx_kernel(*refs):
            (act, sums, gxa_in, gxb_in, paira, pairb, own), refs = refs[3:10], refs[10:]
            wall_refs, refs = refs[: len(walls) - 1], refs[len(walls) - 1 :]
            fluid, first, rest, ghost_out, zedge, gxa, gxb, zrows = refs
            place = my_place()
            grp, gx, _ = place
            on_wall = grp == 0
            own_code = own[fin_rows:, LANES:]
            if ring:
                slots = [(gx, own), (gx ^ 1, gxa_in.at[pl.ds(face_rows, wall_rows), :]),
                         (gx ^ 3, gxb_in.at[pl.ds(face_rows, wall_rows), :]), (gx ^ 2, wall_refs[0])]
            else:
                slots = [(s, wall_refs[0].at[s]) for s in range(count)]
            quadrants = [(a * cells, b * LANES) for a in range(2) for b in range(2)]
            ghost = jnp.zeros((cells, rows), jnp.float32)
            deposits = [jnp.zeros((cells, rows), jnp.float32) for _ in quadrants]
            mine = (4 * gx).astype(jnp.float32)
            for owner, ref in slots:
                theirs = own_code - (4 * jnp.asarray(owner, jnp.int32)).astype(jnp.float32)
                temps = ref[fin_rows:, 0:LANES]
                wanted = ref[fin_rows:, LANES:] - mine
                for q, (r, c) in enumerate(quadrants):
                    ghost = jnp.where(theirs == q, ref[r : r + cells, c : c + LANES], ghost)
                    flux = HEAT_COEF * (temps - own[r : r + cells, c : c + LANES])
                    deposits[q] = deposits[q] + jnp.where(wanted == q, flux, 0.0)
            ghost_out[...] = ghost

            @pl.when(on_wall)
            def _():
                split = jnp.concatenate(
                    [jnp.concatenate(deposits[0:2], axis=1), jnp.concatenate(deposits[2:4], axis=1)],
                    axis=0,
                )
                mixed = dot(split, interleave_matrix(fin_width), ((1,), (1,)))
                landed = dot(interleave_matrix(fin_rows), mixed, ((1,), (0,)))
                first[1, PAD : PAD + fin_rows, :] += landed * (1.0 / DIAG)
                rest[0] += landed * (OMEGA / DIAG)

            even, inside = sides_of(gx, count)
            high_row = PAD + fin_rows - 1
            row_a = jnp.where(even, high_row, PAD)
            row_b = PAD + high_row - row_a
            scale = FIN_CONDUCTION / DIAG
            add_gx_rows(first, 1, (row_a, row_b), (gxa_in, gxb_in), half, (scale, scale * inside),
                        depth, (gxa, gxb))
            below, above = grp_halos(paira, pairb, grp, groups)
            unpack_fluid(fluid, zrows, zedge, gxa_in, gxb_in, ghost, below, above, 0, place, count,
                         dims)
            fluid_update(fluid, act, zedge, sums, 0, dims, outer_pairs)
            pack_gx(
                lambda high: fluid[jnp.where(high, cells, 1), PAD : PAD + rows, :], 0, gx, gxa, gxb,
                dims,
            )

        zrows_buffer, zedge_buffer = buffer(LANES, rows), buffer(rows, LANES)
        fluid1, first, rest, ghost, zedge, gxa, gxb = pl.pallas_call(
            middle_gx_kernel,
            out_shape=(fluid_pad, fin_pad, fin_rest, f32(cells, rows),
                       f32(rows, LANES), f32(face_rows, width), f32(face_rows, width)),
            in_specs=[vmem] * (9 + len(walls)),
            out_specs=(vmem,) * 7,
            scratch_shapes=[zrows_buffer],
            input_output_aliases={0: 0, 1: 1, 2: 2},
            compiler_params=params,
            name="middle_gx",
        )(fluid0, first, rest, active, sums, gxa, gxb, grpa, grpb, *walls)
        gxa, gxb = exchange("gx", count, gxa, gxb)

        def middle_rest_kernel(_, act, zedge, first, fluid, grpa, grpb, gyx, others, sums):
            inner_pairs = (1, 1, (pairs - 2) // inner_group, inner_group)
            neighbour_sums(fluid, others, sums, 0, dims, inner_pairs)
            fluid_update(fluid, act, zedge, sums, 0, dims, inner_pairs)
            pack_rest(fluid, first, 1, grpa, grpb, gyx, my_place(), dims)

        fluid2, grpa, grpb, gyx = pl.pallas_call(
            middle_rest_kernel,
            out_shape=(fluid_pad,) + faces,
            in_specs=[vmem] * 4,
            out_specs=(vmem,) * 4,
            scratch_shapes=[other_buffer(inner_group), buffer(pairs - 2, rows, width)],
            input_output_aliases={0: 0},
            compiler_params=params,
            name="middle_rest",
        )(fluid1, active, zedge, first)
        side = swap(gyx)
        grpa, grpb = exchange("grp", groups, grpa, grpb)

        def end_fin_kernel(_0, _1, first, side, rest, fluid, sums, others):
            unpack_lines(fluid, side, lax.axis_index("gy"), dims)
            hedge = side[cells : cells + fin_rows, 0:LANES]
            inner_blocks(lambda k: fin_second(first, rest, hedge, k))
            neighbour_sums(fluid, others, sums, 1, dims, all_pairs)

        all_pairs = (0, 1, pairs // outer_group, outer_group)
        rest, fluid3, sums = pl.pallas_call(
            end_fin_kernel,
            out_shape=(fin_rest, fluid_pad, f32(pairs, rows, width)),
            in_specs=[vmem] * 4,
            out_specs=(vmem,) * 3,
            scratch_shapes=[other_buffer(outer_group)],
            input_output_aliases={0: 0, 1: 1},
            compiler_params=params,
            name="end_fin",
        )(rest, fluid2, first, side)

        def end_kernel(_0, _1, _2, act, ghost, gxa, gxb, paira, pairb, side, sums,
                       fluid, first, rest, fluid_new, fin_new,
                       zrows, zedge, fluid_sems, fin_sems):
            place = my_place()

            def fluid_copy(k):
                return pltpu.make_async_copy(
                    fluid.at[pl.ds(2 * k + 1, 2), pl.ds(PAD, rows), :],
                    fluid_new.at[pl.ds(2 * k, 2)], fluid_sems.at[k],
                )

            def fin_copy(k, start, size):
                part = pl.ds(start, size)
                return pltpu.make_async_copy(rest.at[part], fin_new.at[part], fin_sems.at[k])

            fin_depth_halos(first, paira, pairb)
            hedge = side[cells : cells + fin_rows, 0:LANES]
            for block in (0, blocks - 1):
                fin_second(first, rest, hedge, block)
            even, inside = sides_of(place[1], count)
            row_a = jnp.where(even, fin_rows - 1, 0)
            row_b = fin_rows - 1 - row_a
            scale = OMEGA * FIN_CONDUCTION / DIAG
            add_gx_rows(rest, 0, (row_a, row_b), (gxa, gxb), half, (scale, scale * inside), depth)
            fin_copies = [fin_copy(0, 0, depth)]
            fin_copies[0].start()
            below, above = grp_halos(paira, pairb, place[0], groups)
            unpack_fluid(fluid, zrows, zedge, gxa, gxb, ghost, below, above, 1, place, count, dims)
            fluid_update(fluid, act, zedge, sums, 1, dims, all_pairs,
                         lambda k: fluid_copy(k).start())

            def finish(k, carry):
                fluid_copy(k).wait()
                return carry

            for item in fin_copies:
                item.wait()
            lax.fori_loop(0, pairs, finish, 0)

        results = pl.pallas_call(
            end_kernel,
            out_shape=(fluid_pad, fin_pad, f32(depth, fin_rows, fin_width),
                       f32(cells, rows, width), f32(depth, fin_rows, fin_width)),
            in_specs=[vmem] * 11,
            out_specs=(vmem, vmem, vmem, hbm, hbm),
            scratch_shapes=[zrows_buffer, zedge_buffer,
                            pltpu.SemaphoreType.DMA((pairs,)), pltpu.SemaphoreType.DMA((1,))],
            input_output_aliases={0: 0, 1: 1, 2: 2},
            compiler_params=params,
            name="end",
        )(fluid3, first, rest, active, ghost, gxa, gxb, grpa, grpb, side, sums)
        return results[3], results[4]

    return jax.shard_map(local, mesh=mesh, in_specs=in_specs, out_specs=out_specs, check_vma=False)
```

```python
import jax
import jax.numpy as jnp
from jax import lax
from jax.experimental import pallas as pl
from jax.experimental.pallas import tpu as pltpu
from jax.sharding import PartitionSpec as P


FLUID_DIFFUSION = 1.0
FIN_CONDUCTION = 1.0
HEAT_COEF = 1.0
DIAG = 1.0 + 6.0 * FIN_CONDUCTION
SPECTRAL = 6.0 * FIN_CONDUCTION / DIAG
OMEGA = 1.0 / (1.0 - SPECTRAL * SPECTRAL / 2.0)
FLUID_SCALE = 1.0 / (1.0 + 6.0 * FLUID_DIFFUSION)
LANES = 128
PAD = 8
ROWS = 16
HIGHEST = lax.Precision.HIGHEST


def iota(shape, axis):
    return lax.broadcasted_iota(jnp.int32, shape, axis)


def repeat(count, body, step=8):
    def trip(k, carry):
        for j in range(step):
            body(k * step + j)
        return carry

    lax.fori_loop(0, count // step, trip, 0)


def tiles(value):
    return [value[:, k : k + LANES] for k in range(0, value.shape[1], LANES)]


def lane_neighbours(block, low, high):
    parts = tiles(block)
    lane = iota(parts[0].shape, 1)
    down = [pltpu.roll(part, 1, axis=1) for part in parts]
    up = [pltpu.roll(part, LANES - 1, axis=1) for part in parts]
    below = [jnp.where(lane == 0, a, b) for a, b in zip([low] + down[:-1], down)]
    above = [jnp.where(lane == LANES - 1, a, b) for a, b in zip(up[1:] + [high], up)]
    return jnp.concatenate([a + b for a, b in zip(below, above)], axis=1)


def interleave_matrix(count):
    row = iota((count, count), 0)
    col = iota((count, count), 1)
    half = count // 2
    source = jnp.where(col < half, 2 * col, 2 * (col - half) + 1)
    return (row == source).astype(jnp.float32)


def dot(a, b, contract):
    return lax.dot_general(
        a, b, (contract, ((), ())), precision=HIGHEST, preferred_element_type=jnp.float32
    )


def checker_pack(plane, parity):
    rows = plane.shape[0] // 2
    top = plane[:rows]
    bottom = plane[rows:]
    colour = (iota(top.shape, 0) + iota(top.shape, 1)) & 1
    return jnp.where(colour == parity, top, pltpu.roll(bottom, 1, axis=1))


def lane_column(column, cells, rows):
    kept = jnp.zeros((rows, LANES), jnp.float32)
    lane = iota((rows, LANES), 1)
    for i in range(cells):
        kept = jnp.where(lane == i, column(i), kept)
    return kept.T[:cells]


def pack_gx(plane, colour, gx, senda, sendb, dims):
    cells, rows, _, _, _, _ = dims
    half = rows // 2
    even = gx % 2 == 0
    for send, high in ((senda, even), (sendb, jnp.logical_not(even))):
        parity = jnp.where(high, (colour + cells - 1) % 2, colour)
        send[0:half, :] = checker_pack(plane(high), parity)


def pack_rest(fluid, fin, colour, grpa, grpb, gyx, place, dims):
    cells, rows, width, depth, fin_rows, fin_width = dims
    grp, _, gy = place
    even = grp % 2 == 0
    odd_row = (iota((rows, 1), 0) & 1) == 1
    inner = slice(PAD, PAD + rows)

    def face(lane, swap):
        column = slice(lane, lane + 1)
        return lane_column(
            lambda k: jnp.where(
                odd_row == swap, fluid[2 * k + 2, inner, column], fluid[2 * k + 1, inner, column]
            ),
            cells // 2, rows,
        )

    low, high = face(0, colour == 1), face(width - 1, colour == 0)
    grpa[0 : cells // 2, 0:LANES] = jnp.where(even, high, low)
    grpb[0 : cells // 2, 0:LANES] = jnp.where(even, low, high)
    up = jnp.where(even, depth, 1)
    grpa[cells : cells + fin_rows, :] = fin[up, PAD : PAD + fin_rows, :]
    grpb[cells : cells + fin_rows, :] = fin[depth + 1 - up, PAD : PAD + fin_rows, :]
    edge = PAD + (1 - gy) * (rows - 1)
    for i in range(cells):
        gyx[i : i + 1, :] = fluid[i + 1, pl.ds(edge, 1), :]
    lane = iota((fin_rows, LANES), 1)

    def columns(at, side):
        kept = jnp.zeros((fin_rows, LANES), jnp.float32)
        for d in range(depth):
            column = fin[d + 1, PAD : PAD + fin_rows, at : at + 1]
            kept = jnp.where(lane == 2 * d + side, column, kept)
        gyx[cells : cells + fin_rows, 0:LANES] = kept

    @pl.when(gy == 0)
    def _():
        columns(fin_width - 1, 1)

    @pl.when(gy != 0)
    def _():
        columns(0, 0)


def my_place():
    return [lax.axis_index(name) for name in ("grp", "gx", "gy")]


def sides_of(at, count):
    return at % 2 == 0, jnp.where((at == 0) | (at == count - 1), 0.0, 1.0)


def grp_halos(paira, pairb, grp, groups):
    even, inside = sides_of(grp, groups)
    a, b = paira[...], pairb[...] * inside
    return jnp.where(even, b, a), jnp.where(even, a, b)


def unpack_lines(fluid, side, gy, dims):
    cells, rows, _, _, _, _ = dims
    low_on = jnp.where(gy == 0, 0.0, 1.0)
    high_on = 1.0 - low_on
    for i in range(cells):
        line = side[i : i + 1, :]
        fluid[i + 1, PAD - 1 : PAD, :] = line * low_on
        fluid[i + 1, PAD + rows : PAD + rows + 1, :] = line * high_on


def unpack_fluid(fluid, zrows, zedge, paira, pairb, ghost, below, above, colour, place, count,
                 dims):
    cells, rows, width, _, _, _ = dims
    half = rows // 2
    grp, gx, _ = place
    even, inside = sides_of(gx, count)
    high_plane = jnp.where(even, cells + 1, 0)
    for plane, ref, on in ((high_plane, paira, 1.0), (cells + 1 - high_plane, pairb, inside)):
        packed = ref[0:half, :] * on
        fluid[plane, PAD : PAD + half, :] = packed
        fluid[plane, PAD + half : PAD + rows, :] = pltpu.roll(packed, width - 1, axis=1)
    odd_row = (iota((1, rows), 1) & 1) == 1
    for k in range(cells // 2):
        first, second = ghost[2 * k : 2 * k + 1, :], ghost[2 * k + 1 : 2 * k + 2, :]
        merged = jnp.where(odd_row == (colour == 0), second, first)
        zrows[2 * k : 2 * k + 1, :] = above[k : k + 1, 0:rows]
        zrows[2 * k + 1 : 2 * k + 2, :] = jnp.where(grp == 0, merged, below[k : k + 1, 0:rows])
    zrows[cells:, :] = jnp.zeros((LANES - cells, rows), jnp.float32)
    zedge[...] = zrows[...].T


def neighbour_sums(fluid, others, sums, colour, dims, pairs):
    _, rows, width, _, _, _ = dims
    updating = ((iota((ROWS, width), 0) + iota((ROWS, width), 1)) & 1) == colour
    end_parity = iota((1, width), 1) & 1
    first_pair, step, trips, group = pairs
    empty = jnp.zeros((ROWS, LANES), jnp.float32)

    def merge(k, other):
        a, b = 2 * k + 1, 2 * k + 2
        for at, swap in ((PAD - 1, 1 - colour), (PAD + rows, colour)):
            line = slice(at, at + 1)
            other[line, :] = jnp.where(end_parity == swap, fluid[b, line, :], fluid[a, line, :])
        for start in range(0, rows, ROWS):
            inner = slice(PAD + start, PAD + start + ROWS)
            other[inner, :] = jnp.where(updating, fluid[b, inner, :], fluid[a, inner, :])

    def add(other, total):
        for start in range(0, rows, ROWS):
            inner = slice(PAD + start, PAD + start + ROWS)
            total[start : start + ROWS, :] = (
                other[PAD + start - 1 : PAD + start + ROWS - 1, :]
                + other[PAD + start + 1 : PAD + start + ROWS + 1, :]
                + lane_neighbours(other[inner, :], empty, empty)
            )

    def trip(j, carry):
        ks = [first_pair + step * (group * j + u) for u in range(group)]
        for u, k in enumerate(ks):
            merge(k, others.at[u])
        for u, k in enumerate(ks):
            add(others.at[u], sums.at[k])
        return carry

    lax.fori_loop(0, trips, trip, 0)


def fluid_update(fluid, active, zedge, sums, colour, dims, pairs, done=None):
    _, rows, width, _, _, _ = dims
    off = ((iota((ROWS, width), 0) + iota((ROWS, width), 1)) & 1) ^ colour
    lane = iota((ROWS, LANES), 1)
    first_pair, step, trips, group = pairs

    def update(k, total):
        a, b = 2 * k + 1, 2 * k + 2
        for start in range(0, rows, ROWS):
            inner = slice(PAD + start, PAD + start + ROWS)
            edge = pltpu.roll(zedge[start : start + ROWS, :], LANES - 1 - 2 * k, axis=1)
            parts = tiles(total[start : start + ROWS, :])
            parts[0] = parts[0] + jnp.where(lane == 0, edge, 0.0)
            parts[-1] = parts[-1] + jnp.where(lane == LANES - 1, edge, 0.0)
            shared = jnp.concatenate(parts, axis=1)
            here_a = fluid[a, inner, :]
            here_b = fluid[b, inner, :]
            total_a = shared + fluid[a - 1, inner, :] + here_b
            total_b = shared + fluid[b + 1, inner, :] + here_a
            new_a = (here_a + FLUID_DIFFUSION * total_a) * FLUID_SCALE
            new_b = (here_b + FLUID_DIFFUSION * total_b) * FLUID_SCALE
            mask_a = active[a - 1, start : start + ROWS, :] > off
            mask_b = active[b - 1, start : start + ROWS, :] > 1 - off
            fluid[a, inner, :] = jnp.where(mask_a, new_a, here_a)
            fluid[b, inner, :] = jnp.where(mask_b, new_b, here_b)

    def trip(j, carry):
        for u in range(group):
            k = first_pair + step * (group * j + u)
            update(k, sums.at[k])
            if done is not None:
                done(k)
        return carry

    lax.fori_loop(0, trips, trip, 0)


def add_gx_rows(target, offset, rows_at, received, half, scales, depth, sends=None):
    def block(k, carry):
        part = pl.ds(half + 8 * k, 8)
        for n, (row, ref, scale) in enumerate(zip(rows_at, received, scales)):
            halo = ref[part, :] * scale
            new = [
                target[8 * k + j + offset, pl.ds(row, 1), :] + halo[j : j + 1, :] for j in range(8)
            ]
            for j in range(8):
                target[8 * k + j + offset, pl.ds(row, 1), :] = new[j]
            if sends is not None:
                sends[n][part, :] = jnp.concatenate(new, axis=0)
        return carry

    lax.fori_loop(0, depth // 8, block, 0)


def fin_neighbours(fin, d, hedge, fin_rows):
    inner = slice(PAD, PAD + fin_rows)
    here = fin[d + 1, inner, :]
    edge = pltpu.roll(hedge, LANES - 1 - 2 * d, axis=1)
    total = (
        fin[d, inner, :]
        + fin[d + 2, inner, :]
        + fin[d + 1, PAD - 1 : PAD + fin_rows - 1, :]
        + fin[d + 1, PAD + 1 : PAD + fin_rows + 1, :]
        + lane_neighbours(here, edge, edge)
    )
    return here, total


def solution(mesh):
    in_specs = (
        P("gx", "gy", "grp"),
        P("gx", "gy", "grp"),
        P("grp", "gx", "gy"),
        P("grp", "gx", "gy"),
        P("gx", "gy", None, None),
        P("gx", "gy", None),
    )
    out_specs = (P("gx", "gy", "grp"), P("grp", "gx", "gy"))
    count = mesh.shape["gx"]
    groups = mesh.shape["grp"]
    sides = mesh.shape["gy"]
    assert sides == 2 and groups % 2 == 0 and count % 2 == 0
    ring = count == 4
    vmem = pl.BlockSpec(memory_space=pltpu.VMEM)
    hbm = pl.BlockSpec(memory_space=pl.ANY)

    def local(fluid_temp, active, fin_temp, fin_source, wall_owner, wall_target):
        cells, rows, width = fluid_temp.shape
        depth, fin_rows, fin_width = fin_temp.shape
        assert rows == LANES and width == fin_width == 2 * rows and fin_rows == 2 * cells
        assert 2 * depth <= LANES and depth % 8 == 0 and depth >= 24 and cells % 2 == 0 and cells >= 4 and rows % ROWS == 0 and fin_rows % 8 == 0
        dims = (cells, rows, width, depth, fin_rows, fin_width)
        half = rows // 2
        pairs = cells // 2
        outer_group = max(g for g in (1, 2, 4) if pairs % g == 0)
        inner_group = max(g for g in (1, 2, 3) if (pairs - 2) % g == 0)
        face_rows = half + depth
        wall_rows = fin_rows + cells
        gx_rows = face_rows + (wall_rows if ring else 0)
        small_rows = cells + fin_rows
        owners = wall_owner.reshape(cells, rows)
        targets = wall_target.reshape(cells, rows)
        f32 = lambda *shape: jax.ShapeDtypeStruct(shape, jnp.float32)
        params = pltpu.CompilerParams(vmem_limit_bytes=32 * 1024 * 1024)
        fluid_pad = f32(cells + 2, rows + 2 * PAD, width)
        fin_pad = f32(depth + 2, fin_rows + 2 * PAD, fin_width)
        faces = (f32(small_rows, width), f32(small_rows, width), f32(small_rows, width))

        def start_gx_kernel(fluid_hbm, fin_hbm, own_hbm, tgt_hbm, gxa, gxb, wall,
                            planes, bottom, low_rows, high_rows, root, own, tgt, sems):
            def copy(k, source, target):
                return pltpu.make_async_copy(source, target, sems.at[k])

            last = cells - 1
            copies = [
                copy(0, own_hbm, own),
                copy(1, tgt_hbm, tgt),
                copy(2, fluid_hbm.at[:, :, pl.ds(0, LANES)], bottom),
                copy(3, fin_hbm.at[0], root),
                copy(4, fluid_hbm.at[0], planes.at[0]),
                copy(5, fluid_hbm.at[last], planes.at[1]),
                copy(6, fin_hbm.at[:, pl.ds(0, PAD), :], low_rows),
                copy(7, fin_hbm.at[:, pl.ds(fin_rows - PAD, PAD), :], high_rows),
            ]
            for item in copies:
                item.start()
            for item in copies[:4]:
                item.wait()
            shape = (cells, rows)
            shift = tgt[...] - 2 * (iota(shape, 0) * fin_width + iota(shape, 1))
            row_shift = (shift >= fin_width).astype(jnp.int32)
            code = own[...] * 4 + row_shift * 2 + (shift - row_shift * fin_width)
            wall[fin_rows:, LANES:] = code.astype(jnp.float32)
            wall[fin_rows:, 0:LANES] = lane_column(lambda i: bottom[i, :, 0:1], cells, rows)
            even_rows = dot(interleave_matrix(fin_rows), root[...], ((0,), (0,)))
            wall[0:fin_rows, :] = dot(even_rows, interleave_matrix(fin_width), ((1,), (0,)))
            gx = lax.axis_index("gx")
            for item in copies[4:]:
                item.wait()
            pack_gx(lambda high: planes[jnp.where(high, 1, 0)], 1, gx, gxa, gxb, dims)
            even = gx % 2 == 0

            def lines(k, carry):
                part = pl.ds(half + 8 * k, 8)
                low = jnp.concatenate([low_rows[8 * k + j, 0:1, :] for j in range(8)], axis=0)
                high = jnp.concatenate(
                    [high_rows[8 * k + j, PAD - 1 : PAD, :] for j in range(8)], axis=0
                )
                gxa[part, :] = jnp.where(even, high, low)
                gxb[part, :] = jnp.where(even, low, high)
                return carry

            lax.fori_loop(0, depth // 8, lines, 0)
            if ring:
                gxa[face_rows:, :] = wall[...]
                gxb[face_rows:, :] = wall[...]

        fluid_hbm, fin_hbm, owners, targets = (
            pltpu.with_memory_space_constraint(v, pltpu.HBM)
            for v in (fluid_temp, fin_temp, owners, targets)
        )
        in_hbm = pl.BlockSpec(memory_space=pltpu.HBM)
        buffer = lambda *shape: pltpu.VMEM(shape, jnp.float32)
        gxa, gxb, wall = pl.pallas_call(
            start_gx_kernel,
            out_shape=(f32(gx_rows, width), f32(gx_rows, width), f32(wall_rows, width)),
            in_specs=[in_hbm] * 4,
            out_specs=(vmem,) * 3,
            scratch_shapes=[buffer(2, rows, width), buffer(cells, rows, LANES),
                            buffer(depth, PAD, fin_width), buffer(depth, PAD, fin_width),
                            buffer(fin_rows, fin_width), pltpu.VMEM((cells, rows), jnp.int32),
                            pltpu.VMEM((cells, rows), jnp.int32), pltpu.SemaphoreType.DMA((8,))],
            compiler_params=params,
            name="start_gx",
        )(fluid_hbm, fin_hbm, owners, targets)

        def start_rest_kernel(fluid_in, fin_in, fluid, fin, grpa, grpb, gyx):
            def fluid_plane(i):
                fluid[i + 1, PAD : PAD + rows, :] = fluid_in[i]

            def fin_plane(d):
                fin[d + 1, PAD : PAD + fin_rows, :] = fin_in[d]

            repeat(cells, fluid_plane, 2)
            repeat(depth, fin_plane, 8)
            clear_rows(fin)
            pack_rest(fluid, fin, 0, grpa, grpb, gyx, my_place(), dims)

        def clear_rows(fin):
            empty = jnp.zeros((depth, PAD, fin_width), jnp.float32)
            fin[1 : depth + 1, 0:PAD, :] = empty
            fin[1 : depth + 1, PAD + fin_rows :, :] = empty

        fluid0, fin0, grpa, grpb, gyx = pl.pallas_call(
            start_rest_kernel,
            out_shape=(fluid_pad, fin_pad) + faces,
            in_specs=[vmem, vmem],
            out_specs=(vmem,) * 5,
            compiler_params=params,
            name="start_rest",
        )(fluid_temp, fin_temp)

        def pairings(axis, size):
            cores = [(g, c) for g in range(size) for c in range(sides)]
            number = {core: k for k, core in enumerate(cores)}

            def partner(g, c):
                other = g - 1 if g % 2 == 0 else g + 1
                return (other, c) if 0 <= other < size else (g, 1 - c)

            first = [(number[g, c], number[g ^ 1, c]) for g, c in cores]
            second = [(number[g, c], number[partner(g, c)]) for g, c in cores]
            return (axis, "gy"), first, second

        def exchange(axis, size, paira, pairb):
            axes, first, second = pairings(axis, size)
            paira = lax.ppermute(paira, axes, first)
            pairb = lax.ppermute(pairb, axes, second)
            return paira, pairb

        def swap(side):
            return lax.ppermute(side, "gy", [(0, 1), (1, 0)])

        def mixed_with(k):
            return [(i, i ^ k) for i in range(count)]

        if ring:
            walls = [wall, lax.ppermute(wall, "gx", mixed_with(2))]
            gxa = lax.ppermute(gxa, "gx", mixed_with(1))
            gxb = lax.ppermute(gxb, "gx", mixed_with(3))
        else:
            gxa, gxb = exchange("gx", count, gxa, gxb)
            walls = [wall, lax.all_gather(wall, "gx")]
        side = swap(gyx)
        grpa, grpb = exchange("grp", groups, grpa, grpb)

        def fin_depth_halos(fin, paira, pairb):
            below, above = grp_halos(paira, pairb, lax.axis_index("grp"), groups)
            fin[0, PAD : PAD + fin_rows, :] = below[cells:, :]
            fin[depth + 1, PAD : PAD + fin_rows, :] = above[cells:, :]

        def fin_first(fin, src, first, rest, hedge, block):
            for j in range(8):
                d = block * 8 + j
                here, total = fin_neighbours(fin, d, hedge, fin_rows)
                rhs = here + src[d]
                first[d + 1, PAD : PAD + fin_rows, :] = (rhs + FIN_CONDUCTION * total) * (1.0 / DIAG)
                rest[d] = rhs * (OMEGA / DIAG) + here * (1.0 - OMEGA)

        def fin_second(first, rest, hedge, block):
            for j in range(8):
                d = block * 8 + j
                _, total = fin_neighbours(first, d, hedge, fin_rows)
                rest[d] = rest[d] + (OMEGA * FIN_CONDUCTION / DIAG) * total

        blocks = depth // 8

        def inner_blocks(body):
            def step(k, carry):
                body(k)
                return carry

            lax.fori_loop(1, blocks - 1, step, 0)

        def middle_fin_kernel(fin, src, side, _, first, rest):
            hedge = side[cells : cells + fin_rows, 0:LANES]
            inner_blocks(lambda k: fin_first(fin, src, first, rest, hedge, k))
            clear_rows(first)

        first, rest = pl.pallas_call(
            middle_fin_kernel,
            out_shape=(fin_pad, f32(depth, fin_rows, fin_width)),
            in_specs=[vmem] * 4,
            out_specs=(vmem,) * 2,
            compiler_params=params,
            name="middle_fin",
        )(fin0, fin_source, side, active)

        def middle_grp_kernel(_0, _1, _2, _3, src, paira, pairb, side, fluid, fin, first, rest,
                              sums, others):
            fin_depth_halos(fin, paira, pairb)
            hedge = side[cells : cells + fin_rows, 0:LANES]
            for block in (0, blocks - 1):
                fin_first(fin, src, first, rest, hedge, block)
            unpack_lines(fluid, side, lax.axis_index("gy"), dims)
            neighbour_sums(fluid, others, sums, 0, dims, all_pairs)

        fin_rest = f32(depth, fin_rows, fin_width)
        other_buffer = lambda planes: buffer(planes, rows + 2 * PAD, width)
        outer_pairs = (0, pairs - 1, 1, 2)
        all_pairs = (0, 1, pairs // outer_group, outer_group)
        inner_pairs = (1, 1, (pairs - 2) // inner_group, inner_group)
        fluid0, _, first, rest, sums = pl.pallas_call(
            middle_grp_kernel,
            out_shape=(fluid_pad, fin_pad, fin_pad, fin_rest, f32(pairs, rows, width)),
            in_specs=[vmem] * 8,
            out_specs=(vmem,) * 5,
            scratch_shapes=[other_buffer(outer_group)],
            input_output_aliases={0: 0, 1: 1, 2: 2, 3: 3},
            compiler_params=params,
            name="middle_grp",
        )(fluid0, fin0, first, rest, fin_source, grpa, grpb, side)

        def middle_gx_kernel(*refs):
            (act, sums, gxa_in, gxb_in, paira, pairb, own), refs = refs[3:10], refs[10:]
            wall_refs, refs = refs[: len(walls) - 1], refs[len(walls) - 1 :]
            fluid, first, rest, ghost_out, zedge, gxa, gxb, zrows = refs
            place = my_place()
            grp, gx, _ = place
            on_wall = grp == 0
            own_code = own[fin_rows:, LANES:]
            if ring:
                slots = [(gx, own), (gx ^ 1, gxa_in.at[pl.ds(face_rows, wall_rows), :]),
                         (gx ^ 3, gxb_in.at[pl.ds(face_rows, wall_rows), :]), (gx ^ 2, wall_refs[0])]
            else:
                slots = [(s, wall_refs[0].at[s]) for s in range(count)]
            quadrants = [(a * cells, b * LANES) for a in range(2) for b in range(2)]
            ghost = jnp.zeros((cells, rows), jnp.float32)
            deposits = [jnp.zeros((cells, rows), jnp.float32) for _ in quadrants]
            mine = (4 * gx).astype(jnp.float32)
            for owner, ref in slots:
                theirs = own_code - (4 * jnp.asarray(owner, jnp.int32)).astype(jnp.float32)
                temps = ref[fin_rows:, 0:LANES]
                wanted = ref[fin_rows:, LANES:] - mine
                for q, (r, c) in enumerate(quadrants):
                    ghost = jnp.where(theirs == q, ref[r : r + cells, c : c + LANES], ghost)
                    flux = HEAT_COEF * (temps - own[r : r + cells, c : c + LANES])
                    deposits[q] = deposits[q] + jnp.where(wanted == q, flux, 0.0)
            ghost_out[...] = ghost

            @pl.when(on_wall)
            def _():
                split = jnp.concatenate(
                    [jnp.concatenate(deposits[0:2], axis=1), jnp.concatenate(deposits[2:4], axis=1)],
                    axis=0,
                )
                mixed = dot(split, interleave_matrix(fin_width), ((1,), (1,)))
                landed = dot(interleave_matrix(fin_rows), mixed, ((1,), (0,)))
                first[1, PAD : PAD + fin_rows, :] += landed * (1.0 / DIAG)
                rest[0] += landed * (OMEGA / DIAG)

            even, inside = sides_of(gx, count)
            high_row = PAD + fin_rows - 1
            row_a = jnp.where(even, high_row, PAD)
            row_b = PAD + high_row - row_a
            scale = FIN_CONDUCTION / DIAG
            add_gx_rows(first, 1, (row_a, row_b), (gxa_in, gxb_in), half, (scale, scale * inside),
                        depth, (gxa, gxb))
            below, above = grp_halos(paira, pairb, grp, groups)
            unpack_fluid(fluid, zrows, zedge, gxa_in, gxb_in, ghost, below, above, 0, place, count,
                         dims)
            fluid_update(fluid, act, zedge, sums, 0, dims, outer_pairs)
            pack_gx(
                lambda high: fluid[jnp.where(high, cells, 1), PAD : PAD + rows, :], 0, gx, gxa, gxb,
                dims,
            )

        zrows_buffer, zedge_buffer = buffer(LANES, rows), buffer(rows, LANES)
        fluid1, first, rest, ghost, zedge, gxa, gxb = pl.pallas_call(
            middle_gx_kernel,
            out_shape=(fluid_pad, fin_pad, fin_rest, f32(cells, rows),
                       f32(rows, LANES), f32(face_rows, width), f32(face_rows, width)),
            in_specs=[vmem] * (9 + len(walls)),
            out_specs=(vmem,) * 7,
            scratch_shapes=[zrows_buffer],
            input_output_aliases={0: 0, 1: 1, 2: 2},
            compiler_params=params,
            name="middle_gx",
        )(fluid0, first, rest, active, sums, gxa, gxb, grpa, grpb, *walls)
        gxa, gxb = exchange("gx", count, gxa, gxb)

        def middle_rest_kernel(_, act, zedge, first, sums, fluid, grpa, grpb, gyx):
            fluid_update(fluid, act, zedge, sums, 0, dims, inner_pairs)
            pack_rest(fluid, first, 1, grpa, grpb, gyx, my_place(), dims)

        fluid2, grpa, grpb, gyx = pl.pallas_call(
            middle_rest_kernel,
            out_shape=(fluid_pad,) + faces,
            in_specs=[vmem] * 5,
            out_specs=(vmem,) * 4,
            input_output_aliases={0: 0},
            compiler_params=params,
            name="middle_rest",
        )(fluid1, active, zedge, first, sums)
        side = swap(gyx)
        grpa, grpb = exchange("grp", groups, grpa, grpb)

        def end_fin_kernel(_0, _1, first, side, rest, fluid, sums, fin_new, others, sem):
            unpack_lines(fluid, side, lax.axis_index("gy"), dims)
            hedge = side[cells : cells + fin_rows, 0:LANES]
            inner_blocks(lambda k: fin_second(first, rest, hedge, k))
            copy = fin_copy(rest, fin_new, sem.at[0], inner_depths, inner_rows)
            copy.start()
            neighbour_sums(fluid, others, sums, 1, dims, all_pairs)
            copy.wait()

        def fin_copy(rest, fin_new, sem, depths, lines):
            return pltpu.make_async_copy(rest.at[depths, lines], fin_new.at[depths, lines], sem)

        inner_depths, inner_rows = pl.ds(8, depth - 16), pl.ds(PAD, fin_rows - 2 * PAD)
        rest, fluid3, sums, fin_new = pl.pallas_call(
            end_fin_kernel,
            out_shape=(fin_rest, fluid_pad, f32(pairs, rows, width), fin_rest),
            in_specs=[vmem] * 4,
            out_specs=(vmem, vmem, vmem, hbm),
            scratch_shapes=[other_buffer(outer_group), pltpu.SemaphoreType.DMA((1,))],
            input_output_aliases={0: 0, 1: 1},
            compiler_params=params,
            name="end_fin",
        )(rest, fluid2, first, side)

        def end_kernel(_0, _1, _2, _3, act, ghost, gxa, gxb, paira, pairb, side, sums,
                       fluid, first, rest, fluid_new, fin_new,
                       zrows, zedge, fluid_sems, fin_sems):
            place = my_place()

            def fluid_copy(k):
                return pltpu.make_async_copy(
                    fluid.at[pl.ds(2 * k + 1, 2), pl.ds(PAD, rows), :],
                    fluid_new.at[pl.ds(2 * k, 2)], fluid_sems.at[k],
                )

            even, inside = sides_of(place[1], count)
            row_a = jnp.where(even, fin_rows - 1, 0)
            row_b = fin_rows - 1 - row_a
            scale = OMEGA * FIN_CONDUCTION / DIAG
            add_gx_rows(rest, 0, (row_a, row_b), (gxa, gxb), half, (scale, scale * inside), depth)
            whole = pl.ds(0, fin_rows)
            parts = ((inner_depths, pl.ds(0, PAD)), (inner_depths, pl.ds(fin_rows - PAD, PAD)),
                     (pl.ds(0, 8), whole), (pl.ds(depth - 8, 8), whole))
            fin_copies = [
                fin_copy(rest, fin_new, fin_sems.at[k], *part) for k, part in enumerate(parts)
            ]
            for item in fin_copies[:2]:
                item.start()
            fin_depth_halos(first, paira, pairb)
            hedge = side[cells : cells + fin_rows, 0:LANES]
            for block, item in ((0, fin_copies[2]), (blocks - 1, fin_copies[3])):
                fin_second(first, rest, hedge, block)
                item.start()
            below, above = grp_halos(paira, pairb, place[0], groups)
            unpack_fluid(fluid, zrows, zedge, gxa, gxb, ghost, below, above, 1, place, count, dims)
            fluid_update(fluid, act, zedge, sums, 1, dims, all_pairs,
                         lambda k: fluid_copy(k).start())

            def finish(k, carry):
                fluid_copy(k).wait()
                return carry

            for item in fin_copies:
                item.wait()
            lax.fori_loop(0, pairs, finish, 0)

        results = pl.pallas_call(
            end_kernel,
            out_shape=(fluid_pad, fin_pad, f32(depth, fin_rows, fin_width),
                       f32(cells, rows, width), f32(depth, fin_rows, fin_width)),
            in_specs=[vmem] * 3 + [hbm] + [vmem] * 8,
            out_specs=(vmem, vmem, vmem, hbm, hbm),
            scratch_shapes=[zrows_buffer, zedge_buffer,
                            pltpu.SemaphoreType.DMA((pairs,)), pltpu.SemaphoreType.DMA((4,))],
            input_output_aliases={0: 0, 1: 1, 2: 2, 3: 4},
            compiler_params=params,
            name="end",
        )(fluid3, first, rest, fin_new, active, ghost, gxa, gxb, grpa, grpb, side, sums)
        return results[3], results[4]

    return jax.shard_map(local, mesh=mesh, in_specs=in_specs, out_specs=out_specs, check_vma=False)
```

```python
import jax
import jax.numpy as jnp
from jax import lax
from jax.experimental import pallas as pl
from jax.experimental.pallas import tpu as pltpu
from jax.sharding import PartitionSpec as P


FLUID_DIFFUSION = 1.0
FIN_CONDUCTION = 1.0
HEAT_COEF = 1.0
DIAG = 1.0 + 6.0 * FIN_CONDUCTION
SPECTRAL = 6.0 * FIN_CONDUCTION / DIAG
OMEGA = 1.0 / (1.0 - SPECTRAL * SPECTRAL / 2.0)
FLUID_SCALE = 1.0 / (1.0 + 6.0 * FLUID_DIFFUSION)
LANES = 128
PAD = 8
ROWS = 16
HIGHEST = lax.Precision.HIGHEST


def iota(shape, axis):
    return lax.broadcasted_iota(jnp.int32, shape, axis)


def repeat(count, body, step=8):
    def trip(k, carry):
        for j in range(step):
            body(k * step + j)
        return carry

    lax.fori_loop(0, count // step, trip, 0)


def tiles(value):
    return [value[:, k : k + LANES] for k in range(0, value.shape[1], LANES)]


def lane_neighbours(block, low, high):
    parts = tiles(block)
    lane = iota(parts[0].shape, 1)
    down = [pltpu.roll(part, 1, axis=1) for part in parts]
    up = [pltpu.roll(part, LANES - 1, axis=1) for part in parts]
    below = [jnp.where(lane == 0, a, b) for a, b in zip([low] + down[:-1], down)]
    above = [jnp.where(lane == LANES - 1, a, b) for a, b in zip(up[1:] + [high], up)]
    return jnp.concatenate([a + b for a, b in zip(below, above)], axis=1)


def interleave_matrix(count):
    row = iota((count, count), 0)
    col = iota((count, count), 1)
    half = count // 2
    source = jnp.where(col < half, 2 * col, 2 * (col - half) + 1)
    return (row == source).astype(jnp.float32)


def dot(a, b, contract):
    return lax.dot_general(
        a, b, (contract, ((), ())), precision=HIGHEST, preferred_element_type=jnp.float32
    )


def checker_pack(plane, parity):
    rows = plane.shape[0] // 2
    top = plane[:rows]
    bottom = plane[rows:]
    colour = (iota(top.shape, 0) + iota(top.shape, 1)) & 1
    return jnp.where(colour == parity, top, pltpu.roll(bottom, 1, axis=1))


def lane_column(column, cells, rows):
    kept = jnp.zeros((rows, LANES), jnp.float32)
    lane = iota((rows, LANES), 1)
    for i in range(cells):
        kept = jnp.where(lane == i, column(i), kept)
    return kept.T[:cells]


def pack_gx(plane, colour, gx, senda, sendb, dims):
    cells, rows, _, _, _, _ = dims
    half = rows // 2
    even = gx % 2 == 0
    for send, high in ((senda, even), (sendb, jnp.logical_not(even))):
        parity = jnp.where(high, (colour + cells - 1) % 2, colour)
        send[0:half, :] = checker_pack(plane(high), parity)


def pack_rest(fluid, fin, colour, grpa, grpb, gyx, place, dims):
    cells, rows, width, depth, fin_rows, fin_width = dims
    grp, _, gy = place
    even = grp % 2 == 0
    odd_row = (iota((rows, 1), 0) & 1) == 1
    inner = slice(PAD, PAD + rows)

    def face(lane, swap):
        column = slice(lane, lane + 1)
        return lane_column(
            lambda k: jnp.where(
                odd_row == swap, fluid[2 * k + 2, inner, column], fluid[2 * k + 1, inner, column]
            ),
            cells // 2, rows,
        )

    low, high = face(0, colour == 1), face(width - 1, colour == 0)
    grpa[0 : cells // 2, 0:LANES] = jnp.where(even, high, low)
    grpb[0 : cells // 2, 0:LANES] = jnp.where(even, low, high)
    up = jnp.where(even, depth, 1)
    grpa[cells : cells + fin_rows, :] = fin[up, PAD : PAD + fin_rows, :]
    grpb[cells : cells + fin_rows, :] = fin[depth + 1 - up, PAD : PAD + fin_rows, :]
    edge = PAD + (1 - gy) * (rows - 1)
    for i in range(cells):
        gyx[i : i + 1, :] = fluid[i + 1, pl.ds(edge, 1), :]
    lane = iota((fin_rows, LANES), 1)

    def columns(at, side):
        kept = jnp.zeros((fin_rows, LANES), jnp.float32)
        for d in range(depth):
            column = fin[d + 1, PAD : PAD + fin_rows, at : at + 1]
            kept = jnp.where(lane == 2 * d + side, column, kept)
        gyx[cells : cells + fin_rows, 0:LANES] = kept

    @pl.when(gy == 0)
    def _():
        columns(fin_width - 1, 1)

    @pl.when(gy != 0)
    def _():
        columns(0, 0)


def my_place():
    return [lax.axis_index(name) for name in ("grp", "gx", "gy")]


def sides_of(at, count):
    return at % 2 == 0, jnp.where((at == 0) | (at == count - 1), 0.0, 1.0)


def grp_halos(paira, pairb, grp, groups):
    even, inside = sides_of(grp, groups)
    a, b = paira[...], pairb[...] * inside
    return jnp.where(even, b, a), jnp.where(even, a, b)


def unpack_lines(fluid, side, gy, dims):
    cells, rows, _, _, _, _ = dims
    low_on = jnp.where(gy == 0, 0.0, 1.0)
    high_on = 1.0 - low_on
    for i in range(cells):
        line = side[i : i + 1, :]
        fluid[i + 1, PAD - 1 : PAD, :] = line * low_on
        fluid[i + 1, PAD + rows : PAD + rows + 1, :] = line * high_on


def unpack_fluid(fluid, zrows, zedge, paira, pairb, ghost, below, above, colour, place, count,
                 dims):
    cells, rows, width, _, _, _ = dims
    half = rows // 2
    grp, gx, _ = place
    even, inside = sides_of(gx, count)
    high_plane = jnp.where(even, cells + 1, 0)
    for plane, ref, on in ((high_plane, paira, 1.0), (cells + 1 - high_plane, pairb, inside)):
        packed = ref[0:half, :] * on
        fluid[plane, PAD : PAD + half, :] = packed
        fluid[plane, PAD + half : PAD + rows, :] = pltpu.roll(packed, width - 1, axis=1)
    odd_row = (iota((1, rows), 1) & 1) == 1
    for k in range(cells // 2):
        first, second = ghost[2 * k : 2 * k + 1, :], ghost[2 * k + 1 : 2 * k + 2, :]
        merged = jnp.where(odd_row == (colour == 0), second, first)
        zrows[2 * k : 2 * k + 1, :] = above[k : k + 1, 0:rows]
        zrows[2 * k + 1 : 2 * k + 2, :] = jnp.where(grp == 0, merged, below[k : k + 1, 0:rows])
    zrows[cells:, :] = jnp.zeros((LANES - cells, rows), jnp.float32)
    zedge[...] = zrows[...].T


def neighbour_sums(fluid, others, sums, colour, dims, pairs):
    _, rows, width, _, _, _ = dims
    updating = ((iota((ROWS, width), 0) + iota((ROWS, width), 1)) & 1) == colour
    end_parity = iota((1, width), 1) & 1
    first_pair, step, trips, group = pairs
    empty = jnp.zeros((ROWS, LANES), jnp.float32)

    def merge(k, other):
        a, b = 2 * k + 1, 2 * k + 2
        for at, swap in ((PAD - 1, 1 - colour), (PAD + rows, colour)):
            line = slice(at, at + 1)
            other[line, :] = jnp.where(end_parity == swap, fluid[b, line, :], fluid[a, line, :])
        for start in range(0, rows, ROWS):
            inner = slice(PAD + start, PAD + start + ROWS)
            other[inner, :] = jnp.where(updating, fluid[b, inner, :], fluid[a, inner, :])

    def add(other, total):
        for start in range(0, rows, ROWS):
            inner = slice(PAD + start, PAD + start + ROWS)
            total[start : start + ROWS, :] = (
                other[PAD + start - 1 : PAD + start + ROWS - 1, :]
                + other[PAD + start + 1 : PAD + start + ROWS + 1, :]
                + lane_neighbours(other[inner, :], empty, empty)
            )

    def trip(j, carry):
        ks = [first_pair + step * (group * j + u) for u in range(group)]
        for u, k in enumerate(ks):
            merge(k, others.at[u])
        for u, k in enumerate(ks):
            add(others.at[u], sums.at[k])
        return carry

    lax.fori_loop(0, trips, trip, 0)


def fluid_update(fluid, active, zedge, sums, colour, dims, pairs, done=None):
    _, rows, width, _, _, _ = dims
    off = ((iota((ROWS, width), 0) + iota((ROWS, width), 1)) & 1) ^ colour
    lane = iota((ROWS, LANES), 1)
    first_pair, step, trips, group = pairs

    def update(k, total):
        a, b = 2 * k + 1, 2 * k + 2
        for start in range(0, rows, ROWS):
            inner = slice(PAD + start, PAD + start + ROWS)
            edge = pltpu.roll(zedge[start : start + ROWS, :], LANES - 1 - 2 * k, axis=1)
            parts = tiles(total[start : start + ROWS, :])
            parts[0] = parts[0] + jnp.where(lane == 0, edge, 0.0)
            parts[-1] = parts[-1] + jnp.where(lane == LANES - 1, edge, 0.0)
            shared = jnp.concatenate(parts, axis=1)
            here_a = fluid[a, inner, :]
            here_b = fluid[b, inner, :]
            total_a = shared + fluid[a - 1, inner, :] + here_b
            total_b = shared + fluid[b + 1, inner, :] + here_a
            new_a = (here_a + FLUID_DIFFUSION * total_a) * FLUID_SCALE
            new_b = (here_b + FLUID_DIFFUSION * total_b) * FLUID_SCALE
            mask_a = active[a - 1, start : start + ROWS, :] > off
            mask_b = active[b - 1, start : start + ROWS, :] > 1 - off
            fluid[a, inner, :] = jnp.where(mask_a, new_a, here_a)
            fluid[b, inner, :] = jnp.where(mask_b, new_b, here_b)

    def trip(j, carry):
        for u in range(group):
            k = first_pair + step * (group * j + u)
            update(k, sums.at[k])
            if done is not None:
                done(k)
        return carry

    lax.fori_loop(0, trips, trip, 0)


def add_gx_rows(target, offset, rows_at, received, half, scales, depth, sends=None):
    def block(k, carry):
        part = pl.ds(half + 8 * k, 8)
        for n, (row, ref, scale) in enumerate(zip(rows_at, received, scales)):
            halo = ref[part, :] * scale
            new = [
                target[8 * k + j + offset, pl.ds(row, 1), :] + halo[j : j + 1, :] for j in range(8)
            ]
            for j in range(8):
                target[8 * k + j + offset, pl.ds(row, 1), :] = new[j]
            if sends is not None:
                sends[n][part, :] = jnp.concatenate(new, axis=0)
        return carry

    lax.fori_loop(0, depth // 8, block, 0)


def fin_neighbours(fin, d, hedge, fin_rows):
    inner = slice(PAD, PAD + fin_rows)
    here = fin[d + 1, inner, :]
    edge = pltpu.roll(hedge, LANES - 1 - 2 * d, axis=1)
    total = (
        fin[d, inner, :]
        + fin[d + 2, inner, :]
        + fin[d + 1, PAD - 1 : PAD + fin_rows - 1, :]
        + fin[d + 1, PAD + 1 : PAD + fin_rows + 1, :]
        + lane_neighbours(here, edge, edge)
    )
    return here, total


def solution(mesh):
    in_specs = (
        P("gx", "gy", "grp"),
        P("gx", "gy", "grp"),
        P("grp", "gx", "gy"),
        P("grp", "gx", "gy"),
        P("gx", "gy", None, None),
        P("gx", "gy", None),
    )
    out_specs = (P("gx", "gy", "grp"), P("grp", "gx", "gy"))
    count = mesh.shape["gx"]
    groups = mesh.shape["grp"]
    sides = mesh.shape["gy"]
    assert sides == 2 and groups % 2 == 0 and count % 2 == 0
    ring = count == 4
    vmem = pl.BlockSpec(memory_space=pltpu.VMEM)
    hbm = pl.BlockSpec(memory_space=pl.ANY)

    def local(fluid_temp, active, fin_temp, fin_source, wall_owner, wall_target):
        cells, rows, width = fluid_temp.shape
        depth, fin_rows, fin_width = fin_temp.shape
        assert rows == LANES and width == fin_width == 2 * rows and fin_rows == 2 * cells
        assert 2 * depth <= LANES and depth % 8 == 0 and depth >= 24 and cells % 2 == 0 and cells >= 4 and rows % ROWS == 0 and fin_rows % 8 == 0
        dims = (cells, rows, width, depth, fin_rows, fin_width)
        half = rows // 2
        pairs = cells // 2
        outer_group = max(g for g in (1, 2, 4) if pairs % g == 0)
        inner_group = max(g for g in (1, 2, 3) if (pairs - 2) % g == 0)
        face_rows = half + depth
        wall_rows = fin_rows + cells
        gx_rows = face_rows + (wall_rows if ring else 0)
        small_rows = cells + fin_rows
        owners = wall_owner.reshape(cells, rows)
        targets = wall_target.reshape(cells, rows)
        f32 = lambda *shape: jax.ShapeDtypeStruct(shape, jnp.float32)
        params = pltpu.CompilerParams(vmem_limit_bytes=32 * 1024 * 1024)
        fluid_pad = f32(cells + 2, rows + 2 * PAD, width)
        fin_pad = f32(depth + 2, fin_rows + 2 * PAD, fin_width)
        faces = (f32(small_rows, width), f32(small_rows, width), f32(small_rows, width))

        def start_gx_kernel(fluid_hbm, fin_hbm, own_hbm, tgt_hbm, gxa, gxb, wall,
                            planes, bottom, low_rows, high_rows, root, own, tgt, sems):
            def copy(k, source, target):
                return pltpu.make_async_copy(source, target, sems.at[k])

            last = cells - 1
            copies = [
                copy(0, own_hbm, own),
                copy(1, tgt_hbm, tgt),
                copy(2, fluid_hbm.at[:, :, pl.ds(0, LANES)], bottom),
                copy(3, fin_hbm.at[0], root),
                copy(4, fluid_hbm.at[0], planes.at[0]),
                copy(5, fluid_hbm.at[last], planes.at[1]),
                copy(6, fin_hbm.at[:, pl.ds(0, PAD), :], low_rows),
                copy(7, fin_hbm.at[:, pl.ds(fin_rows - PAD, PAD), :], high_rows),
            ]
            for item in copies:
                item.start()
            for item in copies[:4]:
                item.wait()
            shape = (cells, rows)
            shift = tgt[...] - 2 * (iota(shape, 0) * fin_width + iota(shape, 1))
            row_shift = (shift >= fin_width).astype(jnp.int32)
            code = own[...] * 4 + row_shift * 2 + (shift - row_shift * fin_width)
            wall[fin_rows:, LANES:] = code.astype(jnp.float32)
            wall[fin_rows:, 0:LANES] = lane_column(lambda i: bottom[i, :, 0:1], cells, rows)
            even_rows = dot(interleave_matrix(fin_rows), root[...], ((0,), (0,)))
            wall[0:fin_rows, :] = dot(even_rows, interleave_matrix(fin_width), ((1,), (0,)))
            gx = lax.axis_index("gx")
            for item in copies[4:]:
                item.wait()
            pack_gx(lambda high: planes[jnp.where(high, 1, 0)], 1, gx, gxa, gxb, dims)
            even = gx % 2 == 0

            def lines(k, carry):
                part = pl.ds(half + 8 * k, 8)
                low = jnp.concatenate([low_rows[8 * k + j, 0:1, :] for j in range(8)], axis=0)
                high = jnp.concatenate(
                    [high_rows[8 * k + j, PAD - 1 : PAD, :] for j in range(8)], axis=0
                )
                gxa[part, :] = jnp.where(even, high, low)
                gxb[part, :] = jnp.where(even, low, high)
                return carry

            lax.fori_loop(0, depth // 8, lines, 0)
            if ring:
                gxa[face_rows:, :] = wall[...]
                gxb[face_rows:, :] = wall[...]

        fluid_hbm, fin_hbm, owners, targets = (
            pltpu.with_memory_space_constraint(v, pltpu.HBM)
            for v in (fluid_temp, fin_temp, owners, targets)
        )
        in_hbm = pl.BlockSpec(memory_space=pltpu.HBM)
        buffer = lambda *shape: pltpu.VMEM(shape, jnp.float32)
        gxa, gxb, wall = pl.pallas_call(
            start_gx_kernel,
            out_shape=(f32(gx_rows, width), f32(gx_rows, width), f32(wall_rows, width)),
            in_specs=[in_hbm] * 4,
            out_specs=(vmem,) * 3,
            scratch_shapes=[buffer(2, rows, width), buffer(cells, rows, LANES),
                            buffer(depth, PAD, fin_width), buffer(depth, PAD, fin_width),
                            buffer(fin_rows, fin_width), pltpu.VMEM((cells, rows), jnp.int32),
                            pltpu.VMEM((cells, rows), jnp.int32), pltpu.SemaphoreType.DMA((8,))],
            compiler_params=params,
            name="start_gx",
        )(fluid_hbm, fin_hbm, owners, targets)

        def start_rest_kernel(fluid_in, fin_in, fluid, fin, grpa, grpb, gyx):
            def fluid_plane(i):
                fluid[i + 1, PAD : PAD + rows, :] = fluid_in[i]

            def fin_plane(d):
                fin[d + 1, PAD : PAD + fin_rows, :] = fin_in[d]

            repeat(cells, fluid_plane, 2)
            repeat(depth, fin_plane, 8)
            clear_rows(fin)
            pack_rest(fluid, fin, 0, grpa, grpb, gyx, my_place(), dims)

        def clear_rows(fin):
            empty = jnp.zeros((depth, PAD, fin_width), jnp.float32)
            fin[1 : depth + 1, 0:PAD, :] = empty
            fin[1 : depth + 1, PAD + fin_rows :, :] = empty

        fluid0, fin0, grpa, grpb, gyx = pl.pallas_call(
            start_rest_kernel,
            out_shape=(fluid_pad, fin_pad) + faces,
            in_specs=[vmem, vmem],
            out_specs=(vmem,) * 5,
            compiler_params=params,
            name="start_rest",
        )(fluid_temp, fin_temp)

        def pairings(axis, size):
            cores = [(g, c) for g in range(size) for c in range(sides)]
            number = {core: k for k, core in enumerate(cores)}

            def partner(g, c):
                other = g - 1 if g % 2 == 0 else g + 1
                return (other, c) if 0 <= other < size else (g, 1 - c)

            first = [(number[g, c], number[g ^ 1, c]) for g, c in cores]
            second = [(number[g, c], number[partner(g, c)]) for g, c in cores]
            return (axis, "gy"), first, second

        def exchange(axis, size, paira, pairb):
            axes, first, second = pairings(axis, size)
            paira = lax.ppermute(paira, axes, first)
            pairb = lax.ppermute(pairb, axes, second)
            return paira, pairb

        def swap(side):
            return lax.ppermute(side, "gy", [(0, 1), (1, 0)])

        def mixed_with(k):
            return [(i, i ^ k) for i in range(count)]

        if ring:
            walls = [wall, lax.ppermute(wall, "gx", mixed_with(2))]
            gxa = lax.ppermute(gxa, "gx", mixed_with(1))
            gxb = lax.ppermute(gxb, "gx", mixed_with(3))
        else:
            gxa, gxb = exchange("gx", count, gxa, gxb)
            walls = [wall, lax.all_gather(wall, "gx")]
        side = swap(gyx)
        grpa, grpb = exchange("grp", groups, grpa, grpb)

        def fin_depth_halos(fin, paira, pairb):
            below, above = grp_halos(paira, pairb, lax.axis_index("grp"), groups)
            fin[0, PAD : PAD + fin_rows, :] = below[cells:, :]
            fin[depth + 1, PAD : PAD + fin_rows, :] = above[cells:, :]

        def fin_first(fin, src, first, rest, hedge, block):
            for j in range(8):
                d = block * 8 + j
                here, total = fin_neighbours(fin, d, hedge, fin_rows)
                rhs = here + src[d]
                first[d + 1, PAD : PAD + fin_rows, :] = (rhs + FIN_CONDUCTION * total) * (1.0 / DIAG)
                rest[d] = rhs * (OMEGA / DIAG) + here * (1.0 - OMEGA)

        def fin_second(first, rest, hedge, block):
            for j in range(8):
                d = block * 8 + j
                _, total = fin_neighbours(first, d, hedge, fin_rows)
                rest[d] = rest[d] + (OMEGA * FIN_CONDUCTION / DIAG) * total

        blocks = depth // 8

        def inner_blocks(body):
            group = 2 if blocks % 2 == 0 else 1

            def step(k, carry):
                for u in range(group):
                    body(1 + group * k + u)
                return carry

            lax.fori_loop(0, (blocks - 2) // group, step, 0)

        def middle_fin_kernel(fin, src, side, _, first, rest):
            hedge = side[cells : cells + fin_rows, 0:LANES]
            inner_blocks(lambda k: fin_first(fin, src, first, rest, hedge, k))
            clear_rows(first)

        first, rest = pl.pallas_call(
            middle_fin_kernel,
            out_shape=(fin_pad, f32(depth, fin_rows, fin_width)),
            in_specs=[vmem] * 4,
            out_specs=(vmem,) * 2,
            compiler_params=params,
            name="middle_fin",
        )(fin0, fin_source, side, active)

        def middle_grp_kernel(_0, _1, _2, _3, src, paira, pairb, side, fluid, fin, first, rest,
                              sums, others):
            fin_depth_halos(fin, paira, pairb)
            hedge = side[cells : cells + fin_rows, 0:LANES]
            for block in (0, blocks - 1):
                fin_first(fin, src, first, rest, hedge, block)
            unpack_lines(fluid, side, lax.axis_index("gy"), dims)
            neighbour_sums(fluid, others, sums, 0, dims, all_pairs)

        fin_rest = f32(depth, fin_rows, fin_width)
        other_buffer = lambda planes: buffer(planes, rows + 2 * PAD, width)
        outer_pairs = (0, pairs - 1, 1, 2)
        all_pairs = (0, 1, pairs // outer_group, outer_group)
        inner_pairs = (1, 1, (pairs - 2) // inner_group, inner_group)
        fluid0, _, first, rest, sums = pl.pallas_call(
            middle_grp_kernel,
            out_shape=(fluid_pad, fin_pad, fin_pad, fin_rest, f32(pairs, rows, width)),
            in_specs=[vmem] * 8,
            out_specs=(vmem,) * 5,
            scratch_shapes=[other_buffer(outer_group)],
            input_output_aliases={0: 0, 1: 1, 2: 2, 3: 3},
            compiler_params=params,
            name="middle_grp",
        )(fluid0, fin0, first, rest, fin_source, grpa, grpb, side)

        def middle_gx_kernel(*refs):
            (act, sums, gxa_in, gxb_in, paira, pairb, own), refs = refs[3:10], refs[10:]
            wall_refs, refs = refs[: len(walls) - 1], refs[len(walls) - 1 :]
            fluid, first, rest, ghost_out, zedge, gxa, gxb, zrows = refs
            place = my_place()
            grp, gx, _ = place
            on_wall = grp == 0
            own_code = own[fin_rows:, LANES:]
            if ring:
                slots = [(gx, own), (gx ^ 1, gxa_in.at[pl.ds(face_rows, wall_rows), :]),
                         (gx ^ 3, gxb_in.at[pl.ds(face_rows, wall_rows), :]), (gx ^ 2, wall_refs[0])]
            else:
                slots = [(s, wall_refs[0].at[s]) for s in range(count)]
            quadrants = [(a * cells, b * LANES) for a in range(2) for b in range(2)]
            ghost = jnp.zeros((cells, rows), jnp.float32)
            deposits = [jnp.zeros((cells, rows), jnp.float32) for _ in quadrants]
            mine = (4 * gx).astype(jnp.float32)
            for owner, ref in slots:
                theirs = own_code - (4 * jnp.asarray(owner, jnp.int32)).astype(jnp.float32)
                temps = ref[fin_rows:, 0:LANES]
                wanted = ref[fin_rows:, LANES:] - mine
                for q, (r, c) in enumerate(quadrants):
                    ghost = jnp.where(theirs == q, ref[r : r + cells, c : c + LANES], ghost)
                    flux = HEAT_COEF * (temps - own[r : r + cells, c : c + LANES])
                    deposits[q] = deposits[q] + jnp.where(wanted == q, flux, 0.0)
            ghost_out[...] = ghost

            @pl.when(on_wall)
            def _():
                split = jnp.concatenate(
                    [jnp.concatenate(deposits[0:2], axis=1), jnp.concatenate(deposits[2:4], axis=1)],
                    axis=0,
                )
                mixed = dot(split, interleave_matrix(fin_width), ((1,), (1,)))
                landed = dot(interleave_matrix(fin_rows), mixed, ((1,), (0,)))
                first[1, PAD : PAD + fin_rows, :] += landed * (1.0 / DIAG)
                rest[0] += landed * (OMEGA / DIAG)

            even, inside = sides_of(gx, count)
            high_row = PAD + fin_rows - 1
            row_a = jnp.where(even, high_row, PAD)
            row_b = PAD + high_row - row_a
            scale = FIN_CONDUCTION / DIAG
            add_gx_rows(first, 1, (row_a, row_b), (gxa_in, gxb_in), half, (scale, scale * inside),
                        depth, (gxa, gxb))
            below, above = grp_halos(paira, pairb, grp, groups)
            unpack_fluid(fluid, zrows, zedge, gxa_in, gxb_in, ghost, below, above, 0, place, count,
                         dims)
            fluid_update(fluid, act, zedge, sums, 0, dims, outer_pairs)
            pack_gx(
                lambda high: fluid[jnp.where(high, cells, 1), PAD : PAD + rows, :], 0, gx, gxa, gxb,
                dims,
            )

        zrows_buffer, zedge_buffer = buffer(LANES, rows), buffer(rows, LANES)
        fluid1, first, rest, ghost, zedge, gxa, gxb = pl.pallas_call(
            middle_gx_kernel,
            out_shape=(fluid_pad, fin_pad, fin_rest, f32(cells, rows),
                       f32(rows, LANES), f32(face_rows, width), f32(face_rows, width)),
            in_specs=[vmem] * (9 + len(walls)),
            out_specs=(vmem,) * 7,
            scratch_shapes=[zrows_buffer],
            input_output_aliases={0: 0, 1: 1, 2: 2},
            compiler_params=params,
            name="middle_gx",
        )(fluid0, first, rest, active, sums, gxa, gxb, grpa, grpb, *walls)
        gxa, gxb = exchange("gx", count, gxa, gxb)

        def middle_rest_kernel(_, act, zedge, first, sums, fluid, grpa, grpb, gyx):
            fluid_update(fluid, act, zedge, sums, 0, dims, inner_pairs)
            pack_rest(fluid, first, 1, grpa, grpb, gyx, my_place(), dims)

        fluid2, grpa, grpb, gyx = pl.pallas_call(
            middle_rest_kernel,
            out_shape=(fluid_pad,) + faces,
            in_specs=[vmem] * 5,
            out_specs=(vmem,) * 4,
            input_output_aliases={0: 0},
            compiler_params=params,
            name="middle_rest",
        )(fluid1, active, zedge, first, sums)
        side = swap(gyx)
        grpa, grpb = exchange("grp", groups, grpa, grpb)

        def end_fin_kernel(_0, _1, first, side, rest, fluid, sums, fin_new, others, sem):
            unpack_lines(fluid, side, lax.axis_index("gy"), dims)
            hedge = side[cells : cells + fin_rows, 0:LANES]
            inner_blocks(lambda k: fin_second(first, rest, hedge, k))
            copy = fin_copy(rest, fin_new, sem.at[0], inner_depths, inner_rows)
            copy.start()
            neighbour_sums(fluid, others, sums, 1, dims, all_pairs)
            copy.wait()

        def fin_copy(rest, fin_new, sem, depths, lines):
            return pltpu.make_async_copy(rest.at[depths, lines], fin_new.at[depths, lines], sem)

        inner_depths, inner_rows = pl.ds(8, depth - 16), pl.ds(PAD, fin_rows - 2 * PAD)
        rest, fluid3, sums, fin_new = pl.pallas_call(
            end_fin_kernel,
            out_shape=(fin_rest, fluid_pad, f32(pairs, rows, width), fin_rest),
            in_specs=[vmem] * 4,
            out_specs=(vmem, vmem, vmem, hbm),
            scratch_shapes=[other_buffer(outer_group), pltpu.SemaphoreType.DMA((1,))],
            input_output_aliases={0: 0, 1: 1},
            compiler_params=params,
            name="end_fin",
        )(rest, fluid2, first, side)

        def end_kernel(_0, _1, _2, _3, act, ghost, gxa, gxb, paira, pairb, side, sums,
                       fluid, first, rest, fluid_new, fin_new,
                       zrows, zedge, fluid_sems, fin_sems):
            place = my_place()

            def fluid_copy(k):
                return pltpu.make_async_copy(
                    fluid.at[pl.ds(2 * k + 1, 2), pl.ds(PAD, rows), :],
                    fluid_new.at[pl.ds(2 * k, 2)], fluid_sems.at[k],
                )

            even, inside = sides_of(place[1], count)
            row_a = jnp.where(even, fin_rows - 1, 0)
            row_b = fin_rows - 1 - row_a
            scale = OMEGA * FIN_CONDUCTION / DIAG
            add_gx_rows(rest, 0, (row_a, row_b), (gxa, gxb), half, (scale, scale * inside), depth)
            whole = pl.ds(0, fin_rows)
            parts = ((inner_depths, pl.ds(0, PAD)), (inner_depths, pl.ds(fin_rows - PAD, PAD)),
                     (pl.ds(0, 8), whole), (pl.ds(depth - 8, 8), whole))
            fin_copies = [
                fin_copy(rest, fin_new, fin_sems.at[k], *part) for k, part in enumerate(parts)
            ]
            for item in fin_copies[:2]:
                item.start()
            fin_depth_halos(first, paira, pairb)
            hedge = side[cells : cells + fin_rows, 0:LANES]
            for block, item in ((0, fin_copies[2]), (blocks - 1, fin_copies[3])):
                fin_second(first, rest, hedge, block)
                item.start()
            below, above = grp_halos(paira, pairb, place[0], groups)
            unpack_fluid(fluid, zrows, zedge, gxa, gxb, ghost, below, above, 1, place, count, dims)
            fluid_update(fluid, act, zedge, sums, 1, dims, all_pairs,
                         lambda k: fluid_copy(k).start())

            def finish(k, carry):
                fluid_copy(k).wait()
                return carry

            for item in fin_copies:
                item.wait()
            lax.fori_loop(0, pairs, finish, 0)

        results = pl.pallas_call(
            end_kernel,
            out_shape=(fluid_pad, fin_pad, f32(depth, fin_rows, fin_width),
                       f32(cells, rows, width), f32(depth, fin_rows, fin_width)),
            in_specs=[vmem] * 3 + [hbm] + [vmem] * 8,
            out_specs=(vmem, vmem, vmem, hbm, hbm),
            scratch_shapes=[zrows_buffer, zedge_buffer,
                            pltpu.SemaphoreType.DMA((pairs,)), pltpu.SemaphoreType.DMA((4,))],
            input_output_aliases={0: 0, 1: 1, 2: 2, 3: 4},
            compiler_params=params,
            name="end",
        )(fluid3, first, rest, fin_new, active, ghost, gxa, gxb, grpa, grpb, side, sums)
        return results[3], results[4]

    return jax.shard_map(local, mesh=mesh, in_specs=in_specs, out_specs=out_specs, check_vma=False)
```

```python
import jax
import jax.numpy as jnp
from jax import lax
from jax.experimental import pallas as pl
from jax.experimental.pallas import tpu as pltpu
from jax.sharding import PartitionSpec as P


FLUID_DIFFUSION = 1.0
FIN_CONDUCTION = 1.0
HEAT_COEF = 1.0
DIAG = 1.0 + 6.0 * FIN_CONDUCTION
SPECTRAL = 6.0 * FIN_CONDUCTION / DIAG
OMEGA = 1.0 / (1.0 - SPECTRAL * SPECTRAL / 2.0)
FLUID_SCALE = 1.0 / (1.0 + 6.0 * FLUID_DIFFUSION)
LANES = 128
PAD = 8
ROWS = 16
HIGHEST = lax.Precision.HIGHEST


def iota(shape, axis):
    return lax.broadcasted_iota(jnp.int32, shape, axis)


def repeat(count, body, step=8):
    def trip(k, carry):
        for j in range(step):
            body(k * step + j)
        return carry

    lax.fori_loop(0, count // step, trip, 0)


def tiles(value):
    return [value[:, k : k + LANES] for k in range(0, value.shape[1], LANES)]


def lane_neighbours(block, low, high):
    parts = tiles(block)
    lane = iota(parts[0].shape, 1)
    down = [pltpu.roll(part, 1, axis=1) for part in parts]
    up = [pltpu.roll(part, LANES - 1, axis=1) for part in parts]
    below = [jnp.where(lane == 0, a, b) for a, b in zip([low] + down[:-1], down)]
    above = [jnp.where(lane == LANES - 1, a, b) for a, b in zip(up[1:] + [high], up)]
    return jnp.concatenate([a + b for a, b in zip(below, above)], axis=1)


def interleave_matrix(count):
    row = iota((count, count), 0)
    col = iota((count, count), 1)
    half = count // 2
    source = jnp.where(col < half, 2 * col, 2 * (col - half) + 1)
    return (row == source).astype(jnp.float32)


def dot(a, b, contract):
    return lax.dot_general(
        a, b, (contract, ((), ())), precision=HIGHEST, preferred_element_type=jnp.float32
    )


def checker_pack(plane, parity):
    rows = plane.shape[0] // 2
    top = plane[:rows]
    bottom = plane[rows:]
    colour = (iota(top.shape, 0) + iota(top.shape, 1)) & 1
    return jnp.where(colour == parity, top, pltpu.roll(bottom, 1, axis=1))


def lane_column(column, cells, rows):
    kept = jnp.zeros((rows, LANES), jnp.float32)
    lane = iota((rows, LANES), 1)
    for i in range(cells):
        kept = jnp.where(lane == i, column(i), kept)
    return kept.T[:cells]


def pack_gx(plane, colour, gx, senda, sendb, dims):
    cells, rows, _, _, _, _ = dims
    half = rows // 2
    even = gx % 2 == 0
    for send, high in ((senda, even), (sendb, jnp.logical_not(even))):
        parity = jnp.where(high, (colour + cells - 1) % 2, colour)
        send[0:half, :] = checker_pack(plane(high), parity)


def pack_rest(fluid, fin, colour, grpa, grpb, gyx, place, dims):
    cells, rows, width, depth, fin_rows, fin_width = dims
    grp, _, gy = place
    even = grp % 2 == 0
    odd_row = (iota((rows, 1), 0) & 1) == 1
    inner = slice(PAD, PAD + rows)

    def face(lane, swap):
        column = slice(lane, lane + 1)
        return lane_column(
            lambda k: jnp.where(
                odd_row == swap, fluid[2 * k + 2, inner, column], fluid[2 * k + 1, inner, column]
            ),
            cells // 2, rows,
        )

    low, high = face(0, colour == 1), face(width - 1, colour == 0)
    grpa[0 : cells // 2, 0:LANES] = jnp.where(even, high, low)
    grpb[0 : cells // 2, 0:LANES] = jnp.where(even, low, high)
    up = jnp.where(even, depth, 1)
    grpa[cells : cells + fin_rows, :] = fin[up, PAD : PAD + fin_rows, :]
    grpb[cells : cells + fin_rows, :] = fin[depth + 1 - up, PAD : PAD + fin_rows, :]
    edge = PAD + (1 - gy) * (rows - 1)
    for i in range(cells):
        gyx[i : i + 1, :] = fluid[i + 1, pl.ds(edge, 1), :]
    lane = iota((fin_rows, LANES), 1)

    def columns(at, side):
        kept = jnp.zeros((fin_rows, LANES), jnp.float32)
        for d in range(depth):
            column = fin[d + 1, PAD : PAD + fin_rows, at : at + 1]
            kept = jnp.where(lane == 2 * d + side, column, kept)
        gyx[cells : cells + fin_rows, 0:LANES] = kept

    @pl.when(gy == 0)
    def _():
        columns(fin_width - 1, 1)

    @pl.when(gy != 0)
    def _():
        columns(0, 0)


def my_place():
    return [lax.axis_index(name) for name in ("grp", "gx", "gy")]


def sides_of(at, count):
    return at % 2 == 0, jnp.where((at == 0) | (at == count - 1), 0.0, 1.0)


def grp_halos(paira, pairb, grp, groups):
    even, inside = sides_of(grp, groups)
    a, b = paira[...], pairb[...] * inside
    return jnp.where(even, b, a), jnp.where(even, a, b)


def unpack_lines(fluid, side, gy, dims):
    cells, rows, _, _, _, _ = dims
    low_on = jnp.where(gy == 0, 0.0, 1.0)
    high_on = 1.0 - low_on
    for i in range(cells):
        line = side[i : i + 1, :]
        fluid[i + 1, PAD - 1 : PAD, :] = line * low_on
        fluid[i + 1, PAD + rows : PAD + rows + 1, :] = line * high_on


def unpack_fluid(fluid, zrows, zedge, paira, pairb, ghost, below, above, colour, place, count,
                 dims):
    cells, rows, width, _, _, _ = dims
    half = rows // 2
    grp, gx, _ = place
    even, inside = sides_of(gx, count)
    high_plane = jnp.where(even, cells + 1, 0)
    for plane, ref, on in ((high_plane, paira, 1.0), (cells + 1 - high_plane, pairb, inside)):
        packed = ref[0:half, :] * on
        fluid[plane, PAD : PAD + half, :] = packed
        fluid[plane, PAD + half : PAD + rows, :] = pltpu.roll(packed, width - 1, axis=1)
    odd_row = (iota((1, rows), 1) & 1) == 1
    for k in range(cells // 2):
        first, second = ghost[2 * k : 2 * k + 1, :], ghost[2 * k + 1 : 2 * k + 2, :]
        merged = jnp.where(odd_row == (colour == 0), second, first)
        zrows[2 * k : 2 * k + 1, :] = above[k : k + 1, 0:rows]
        zrows[2 * k + 1 : 2 * k + 2, :] = jnp.where(grp == 0, merged, below[k : k + 1, 0:rows])
    zrows[cells:, :] = jnp.zeros((LANES - cells, rows), jnp.float32)
    zedge[...] = zrows[...].T


def neighbour_sums(fluid, others, sums, colour, dims, pairs):
    _, rows, width, _, _, _ = dims
    updating = ((iota((ROWS, width), 0) + iota((ROWS, width), 1)) & 1) == colour
    end_parity = iota((1, width), 1) & 1
    first_pair, step, trips, group = pairs
    empty = jnp.zeros((ROWS, LANES), jnp.float32)

    def merge(k, other):
        a, b = 2 * k + 1, 2 * k + 2
        for at, swap in ((PAD - 1, 1 - colour), (PAD + rows, colour)):
            line = slice(at, at + 1)
            other[line, :] = jnp.where(end_parity == swap, fluid[b, line, :], fluid[a, line, :])
        for start in range(0, rows, ROWS):
            inner = slice(PAD + start, PAD + start + ROWS)
            other[inner, :] = jnp.where(updating, fluid[b, inner, :], fluid[a, inner, :])

    def add(other, total):
        for start in range(0, rows, ROWS):
            inner = slice(PAD + start, PAD + start + ROWS)
            total[start : start + ROWS, :] = (
                other[PAD + start - 1 : PAD + start + ROWS - 1, :]
                + other[PAD + start + 1 : PAD + start + ROWS + 1, :]
                + lane_neighbours(other[inner, :], empty, empty)
            )

    def trip(j, carry):
        ks = [first_pair + step * (group * j + u) for u in range(group)]
        for u, k in enumerate(ks):
            merge(k, others.at[u])
        for u, k in enumerate(ks):
            add(others.at[u], sums.at[k])
        return carry

    lax.fori_loop(0, trips, trip, 0)


def fluid_update(fluid, active, zedge, sums, colour, dims, pairs, done=None):
    _, rows, width, _, _, _ = dims
    off = ((iota((ROWS, width), 0) + iota((ROWS, width), 1)) & 1) ^ colour
    lane = iota((ROWS, LANES), 1)
    first_pair, step, trips, group = pairs

    def update(k, total):
        a, b = 2 * k + 1, 2 * k + 2
        for start in range(0, rows, ROWS):
            inner = slice(PAD + start, PAD + start + ROWS)
            edge = pltpu.roll(zedge[start : start + ROWS, :], LANES - 1 - 2 * k, axis=1)
            parts = tiles(total[start : start + ROWS, :])
            parts[0] = parts[0] + jnp.where(lane == 0, edge, 0.0)
            parts[-1] = parts[-1] + jnp.where(lane == LANES - 1, edge, 0.0)
            shared = jnp.concatenate(parts, axis=1)
            here_a = fluid[a, inner, :]
            here_b = fluid[b, inner, :]
            total_a = shared + fluid[a - 1, inner, :] + here_b
            total_b = shared + fluid[b + 1, inner, :] + here_a
            new_a = (here_a + FLUID_DIFFUSION * total_a) * FLUID_SCALE
            new_b = (here_b + FLUID_DIFFUSION * total_b) * FLUID_SCALE
            mask_a = active[a - 1, start : start + ROWS, :] > off
            mask_b = active[b - 1, start : start + ROWS, :] > 1 - off
            fluid[a, inner, :] = jnp.where(mask_a, new_a, here_a)
            fluid[b, inner, :] = jnp.where(mask_b, new_b, here_b)

    def trip(j, carry):
        for u in range(group):
            k = first_pair + step * (group * j + u)
            update(k, sums.at[k])
            if done is not None:
                done(k)
        return carry

    lax.fori_loop(0, trips, trip, 0)


def add_gx_rows(target, offset, rows_at, received, half, scales, depth, sends=None):
    def block(k, carry):
        part = pl.ds(half + 8 * k, 8)
        for n, (row, ref, scale) in enumerate(zip(rows_at, received, scales)):
            halo = ref[part, :] * scale
            new = [
                target[8 * k + j + offset, pl.ds(row, 1), :] + halo[j : j + 1, :] for j in range(8)
            ]
            for j in range(8):
                target[8 * k + j + offset, pl.ds(row, 1), :] = new[j]
            if sends is not None:
                sends[n][part, :] = jnp.concatenate(new, axis=0)
        return carry

    lax.fori_loop(0, depth // 8, block, 0)


def fin_neighbours(fin, d, hedge, fin_rows):
    inner = slice(PAD, PAD + fin_rows)
    here = fin[d + 1, inner, :]
    edge = pltpu.roll(hedge, LANES - 1 - 2 * d, axis=1)
    total = (
        fin[d, inner, :]
        + fin[d + 2, inner, :]
        + fin[d + 1, PAD - 1 : PAD + fin_rows - 1, :]
        + fin[d + 1, PAD + 1 : PAD + fin_rows + 1, :]
        + lane_neighbours(here, edge, edge)
    )
    return here, total


def solution(mesh):
    in_specs = (
        P("gx", "gy", "grp"),
        P("gx", "gy", "grp"),
        P("grp", "gx", "gy"),
        P("grp", "gx", "gy"),
        P("gx", "gy", None, None),
        P("gx", "gy", None),
    )
    out_specs = (P("gx", "gy", "grp"), P("grp", "gx", "gy"))
    count = mesh.shape["gx"]
    groups = mesh.shape["grp"]
    sides = mesh.shape["gy"]
    assert sides == 2 and groups % 2 == 0 and count % 2 == 0
    ring = count == 4
    vmem = pl.BlockSpec(memory_space=pltpu.VMEM)
    hbm = pl.BlockSpec(memory_space=pl.ANY)

    def local(fluid_temp, active, fin_temp, fin_source, wall_owner, wall_target):
        cells, rows, width = fluid_temp.shape
        depth, fin_rows, fin_width = fin_temp.shape
        assert rows == LANES and width == fin_width == 2 * rows and fin_rows == 2 * cells
        assert 2 * depth <= LANES and depth % 8 == 0 and depth >= 24 and cells % 2 == 0 and cells >= 4 and rows % ROWS == 0 and fin_rows % 8 == 0
        dims = (cells, rows, width, depth, fin_rows, fin_width)
        half = rows // 2
        pairs = cells // 2
        outer_group = max(g for g in (1, 2, 4) if pairs % g == 0)
        sum_group = max(g for g in (1, 2, 4, 8) if pairs % g == 0)
        inner_group = max(g for g in (1, 2, 3) if (pairs - 2) % g == 0)
        face_rows = half + depth
        wall_rows = fin_rows + cells
        gx_rows = face_rows + (wall_rows if ring else 0)
        small_rows = cells + fin_rows
        owners = wall_owner.reshape(cells, rows)
        targets = wall_target.reshape(cells, rows)
        f32 = lambda *shape: jax.ShapeDtypeStruct(shape, jnp.float32)
        params = pltpu.CompilerParams(vmem_limit_bytes=32 * 1024 * 1024)
        fluid_pad = f32(cells + 2, rows + 2 * PAD, width)
        fin_pad = f32(depth + 2, fin_rows + 2 * PAD, fin_width)
        faces = (f32(small_rows, width), f32(small_rows, width), f32(small_rows, width))

        def start_gx_kernel(fluid_hbm, fin_hbm, own_hbm, tgt_hbm, gxa, gxb, wall,
                            planes, bottom, low_rows, high_rows, root, own, tgt, sems):
            def copy(k, source, target):
                return pltpu.make_async_copy(source, target, sems.at[k])

            last = cells - 1
            copies = [
                copy(0, own_hbm, own),
                copy(1, tgt_hbm, tgt),
                copy(2, fluid_hbm.at[:, :, pl.ds(0, LANES)], bottom),
                copy(3, fin_hbm.at[0], root),
                copy(4, fluid_hbm.at[0], planes.at[0]),
                copy(5, fluid_hbm.at[last], planes.at[1]),
                copy(6, fin_hbm.at[:, pl.ds(0, PAD), :], low_rows),
                copy(7, fin_hbm.at[:, pl.ds(fin_rows - PAD, PAD), :], high_rows),
            ]
            for item in copies:
                item.start()
            for item in copies[:4]:
                item.wait()
            shape = (cells, rows)
            shift = tgt[...] - 2 * (iota(shape, 0) * fin_width + iota(shape, 1))
            row_shift = (shift >= fin_width).astype(jnp.int32)
            code = own[...] * 4 + row_shift * 2 + (shift - row_shift * fin_width)
            wall[fin_rows:, LANES:] = code.astype(jnp.float32)
            wall[fin_rows:, 0:LANES] = lane_column(lambda i: bottom[i, :, 0:1], cells, rows)
            even_rows = dot(interleave_matrix(fin_rows), root[...], ((0,), (0,)))
            wall[0:fin_rows, :] = dot(even_rows, interleave_matrix(fin_width), ((1,), (0,)))
            gx = lax.axis_index("gx")
            for item in copies[4:]:
                item.wait()
            pack_gx(lambda high: planes[jnp.where(high, 1, 0)], 1, gx, gxa, gxb, dims)
            even = gx % 2 == 0

            def lines(k, carry):
                part = pl.ds(half + 8 * k, 8)
                low = jnp.concatenate([low_rows[8 * k + j, 0:1, :] for j in range(8)], axis=0)
                high = jnp.concatenate(
                    [high_rows[8 * k + j, PAD - 1 : PAD, :] for j in range(8)], axis=0
                )
                gxa[part, :] = jnp.where(even, high, low)
                gxb[part, :] = jnp.where(even, low, high)
                return carry

            lax.fori_loop(0, depth // 8, lines, 0)
            if ring:
                gxa[face_rows:, :] = wall[...]
                gxb[face_rows:, :] = wall[...]

        fluid_hbm, fin_hbm, owners, targets = (
            pltpu.with_memory_space_constraint(v, pltpu.HBM)
            for v in (fluid_temp, fin_temp, owners, targets)
        )
        in_hbm = pl.BlockSpec(memory_space=pltpu.HBM)
        buffer = lambda *shape: pltpu.VMEM(shape, jnp.float32)
        gxa, gxb, wall = pl.pallas_call(
            start_gx_kernel,
            out_shape=(f32(gx_rows, width), f32(gx_rows, width), f32(wall_rows, width)),
            in_specs=[in_hbm] * 4,
            out_specs=(vmem,) * 3,
            scratch_shapes=[buffer(2, rows, width), buffer(cells, rows, LANES),
                            buffer(depth, PAD, fin_width), buffer(depth, PAD, fin_width),
                            buffer(fin_rows, fin_width), pltpu.VMEM((cells, rows), jnp.int32),
                            pltpu.VMEM((cells, rows), jnp.int32), pltpu.SemaphoreType.DMA((8,))],
            compiler_params=params,
            name="start_gx",
        )(fluid_hbm, fin_hbm, owners, targets)

        def start_rest_kernel(fluid_in, fin_in, fluid, fin, grpa, grpb, gyx):
            def fluid_plane(i):
                fluid[i + 1, PAD : PAD + rows, :] = fluid_in[i]

            def fin_plane(d):
                fin[d + 1, PAD : PAD + fin_rows, :] = fin_in[d]

            repeat(cells, fluid_plane, 2)
            repeat(depth, fin_plane, 8)
            clear_rows(fin)
            pack_rest(fluid, fin, 0, grpa, grpb, gyx, my_place(), dims)

        def clear_rows(fin):
            empty = jnp.zeros((depth, PAD, fin_width), jnp.float32)
            fin[1 : depth + 1, 0:PAD, :] = empty
            fin[1 : depth + 1, PAD + fin_rows :, :] = empty

        fluid0, fin0, grpa, grpb, gyx = pl.pallas_call(
            start_rest_kernel,
            out_shape=(fluid_pad, fin_pad) + faces,
            in_specs=[vmem, vmem],
            out_specs=(vmem,) * 5,
            compiler_params=params,
            name="start_rest",
        )(fluid_temp, fin_temp)

        def pairings(axis, size):
            cores = [(g, c) for g in range(size) for c in range(sides)]
            number = {core: k for k, core in enumerate(cores)}

            def partner(g, c):
                other = g - 1 if g % 2 == 0 else g + 1
                return (other, c) if 0 <= other < size else (g, 1 - c)

            first = [(number[g, c], number[g ^ 1, c]) for g, c in cores]
            second = [(number[g, c], number[partner(g, c)]) for g, c in cores]
            return (axis, "gy"), first, second

        def exchange(axis, size, paira, pairb):
            axes, first, second = pairings(axis, size)
            paira = lax.ppermute(paira, axes, first)
            pairb = lax.ppermute(pairb, axes, second)
            return paira, pairb

        def swap(side):
            return lax.ppermute(side, "gy", [(0, 1), (1, 0)])

        def mixed_with(k):
            return [(i, i ^ k) for i in range(count)]

        if ring:
            walls = [wall, lax.ppermute(wall, "gx", mixed_with(2))]
            gxa = lax.ppermute(gxa, "gx", mixed_with(1))
            gxb = lax.ppermute(gxb, "gx", mixed_with(3))
        else:
            gxa, gxb = exchange("gx", count, gxa, gxb)
            walls = [wall, lax.all_gather(wall, "gx")]
        side = swap(gyx)
        grpa, grpb = exchange("grp", groups, grpa, grpb)

        def fin_depth_halos(fin, paira, pairb):
            below, above = grp_halos(paira, pairb, lax.axis_index("grp"), groups)
            fin[0, PAD : PAD + fin_rows, :] = below[cells:, :]
            fin[depth + 1, PAD : PAD + fin_rows, :] = above[cells:, :]

        def fin_first(fin, src, first, rest, hedge, block):
            for j in range(8):
                d = block * 8 + j
                here, total = fin_neighbours(fin, d, hedge, fin_rows)
                rhs = here + src[d]
                first[d + 1, PAD : PAD + fin_rows, :] = (rhs + FIN_CONDUCTION * total) * (1.0 / DIAG)
                rest[d] = rhs * (OMEGA / DIAG) + here * (1.0 - OMEGA)

        def fin_second(first, rest, hedge, block):
            for j in range(8):
                d = block * 8 + j
                _, total = fin_neighbours(first, d, hedge, fin_rows)
                rest[d] = rest[d] + (OMEGA * FIN_CONDUCTION / DIAG) * total

        blocks = depth // 8

        def inner_blocks(body):
            group = 2 if blocks % 2 == 0 else 1

            def step(k, carry):
                for u in range(group):
                    body(1 + group * k + u)
                return carry

            lax.fori_loop(0, (blocks - 2) // group, step, 0)

        def middle_fin_kernel(fin, src, side, _, first, rest):
            hedge = side[cells : cells + fin_rows, 0:LANES]
            inner_blocks(lambda k: fin_first(fin, src, first, rest, hedge, k))
            clear_rows(first)

        first, rest = pl.pallas_call(
            middle_fin_kernel,
            out_shape=(fin_pad, f32(depth, fin_rows, fin_width)),
            in_specs=[vmem] * 4,
            out_specs=(vmem,) * 2,
            compiler_params=params,
            name="middle_fin",
        )(fin0, fin_source, side, active)

        def middle_grp_kernel(_0, _1, _2, _3, src, paira, pairb, side, fluid, fin, first, rest,
                              sums, others):
            fin_depth_halos(fin, paira, pairb)
            hedge = side[cells : cells + fin_rows, 0:LANES]
            for block in (0, blocks - 1):
                fin_first(fin, src, first, rest, hedge, block)
            unpack_lines(fluid, side, lax.axis_index("gy"), dims)
            neighbour_sums(fluid, others, sums, 0, dims, sum_pairs)

        fin_rest = f32(depth, fin_rows, fin_width)
        other_buffer = lambda planes: buffer(planes, rows + 2 * PAD, width)
        outer_pairs = (0, pairs - 1, 1, 2)
        all_pairs = (0, 1, pairs // outer_group, outer_group)
        sum_pairs = (0, 1, pairs // sum_group, sum_group)
        inner_pairs = (1, 1, (pairs - 2) // inner_group, inner_group)
        fluid0, _, first, rest, sums = pl.pallas_call(
            middle_grp_kernel,
            out_shape=(fluid_pad, fin_pad, fin_pad, fin_rest, f32(pairs, rows, width)),
            in_specs=[vmem] * 8,
            out_specs=(vmem,) * 5,
            scratch_shapes=[other_buffer(sum_group)],
            input_output_aliases={0: 0, 1: 1, 2: 2, 3: 3},
            compiler_params=params,
            name="middle_grp",
        )(fluid0, fin0, first, rest, fin_source, grpa, grpb, side)

        def middle_gx_kernel(*refs):
            (act, sums, gxa_in, gxb_in, paira, pairb, own), refs = refs[3:10], refs[10:]
            wall_refs, refs = refs[: len(walls) - 1], refs[len(walls) - 1 :]
            fluid, first, rest, ghost_out, zedge, gxa, gxb, zrows = refs
            place = my_place()
            grp, gx, _ = place
            on_wall = grp == 0
            own_code = own[fin_rows:, LANES:]
            if ring:
                slots = [(gx, own), (gx ^ 1, gxa_in.at[pl.ds(face_rows, wall_rows), :]),
                         (gx ^ 3, gxb_in.at[pl.ds(face_rows, wall_rows), :]), (gx ^ 2, wall_refs[0])]
            else:
                slots = [(s, wall_refs[0].at[s]) for s in range(count)]
            quadrants = [(a * cells, b * LANES) for a in range(2) for b in range(2)]
            ghost = jnp.zeros((cells, rows), jnp.float32)
            deposits = [jnp.zeros((cells, rows), jnp.float32) for _ in quadrants]
            mine = (4 * gx).astype(jnp.float32)
            for owner, ref in slots:
                theirs = own_code - (4 * jnp.asarray(owner, jnp.int32)).astype(jnp.float32)
                temps = ref[fin_rows:, 0:LANES]
                wanted = ref[fin_rows:, LANES:] - mine
                for q, (r, c) in enumerate(quadrants):
                    ghost = jnp.where(theirs == q, ref[r : r + cells, c : c + LANES], ghost)
                    flux = HEAT_COEF * (temps - own[r : r + cells, c : c + LANES])
                    deposits[q] = deposits[q] + jnp.where(wanted == q, flux, 0.0)
            ghost_out[...] = ghost

            @pl.when(on_wall)
            def _():
                split = jnp.concatenate(
                    [jnp.concatenate(deposits[0:2], axis=1), jnp.concatenate(deposits[2:4], axis=1)],
                    axis=0,
                )
                mixed = dot(split, interleave_matrix(fin_width), ((1,), (1,)))
                landed = dot(interleave_matrix(fin_rows), mixed, ((1,), (0,)))
                first[1, PAD : PAD + fin_rows, :] += landed * (1.0 / DIAG)
                rest[0] += landed * (OMEGA / DIAG)

            even, inside = sides_of(gx, count)
            high_row = PAD + fin_rows - 1
            row_a = jnp.where(even, high_row, PAD)
            row_b = PAD + high_row - row_a
            scale = FIN_CONDUCTION / DIAG
            add_gx_rows(first, 1, (row_a, row_b), (gxa_in, gxb_in), half, (scale, scale * inside),
                        depth, (gxa, gxb))
            below, above = grp_halos(paira, pairb, grp, groups)
            unpack_fluid(fluid, zrows, zedge, gxa_in, gxb_in, ghost, below, above, 0, place, count,
                         dims)
            fluid_update(fluid, act, zedge, sums, 0, dims, outer_pairs)
            pack_gx(
                lambda high: fluid[jnp.where(high, cells, 1), PAD : PAD + rows, :], 0, gx, gxa, gxb,
                dims,
            )

        zrows_buffer, zedge_buffer = buffer(LANES, rows), buffer(rows, LANES)
        fluid1, first, rest, ghost, zedge, gxa, gxb = pl.pallas_call(
            middle_gx_kernel,
            out_shape=(fluid_pad, fin_pad, fin_rest, f32(cells, rows),
                       f32(rows, LANES), f32(face_rows, width), f32(face_rows, width)),
            in_specs=[vmem] * (9 + len(walls)),
            out_specs=(vmem,) * 7,
            scratch_shapes=[zrows_buffer],
            input_output_aliases={0: 0, 1: 1, 2: 2},
            compiler_params=params,
            name="middle_gx",
        )(fluid0, first, rest, active, sums, gxa, gxb, grpa, grpb, *walls)
        gxa, gxb = exchange("gx", count, gxa, gxb)

        def middle_rest_kernel(_, act, zedge, first, sums, fluid, grpa, grpb, gyx):
            fluid_update(fluid, act, zedge, sums, 0, dims, inner_pairs)
            pack_rest(fluid, first, 1, grpa, grpb, gyx, my_place(), dims)

        fluid2, grpa, grpb, gyx = pl.pallas_call(
            middle_rest_kernel,
            out_shape=(fluid_pad,) + faces,
            in_specs=[vmem] * 5,
            out_specs=(vmem,) * 4,
            input_output_aliases={0: 0},
            compiler_params=params,
            name="middle_rest",
        )(fluid1, active, zedge, first, sums)
        side = swap(gyx)
        grpa, grpb = exchange("grp", groups, grpa, grpb)

        def end_fin_kernel(_0, _1, first, side, rest, fluid, sums, fin_new, others, sem):
            unpack_lines(fluid, side, lax.axis_index("gy"), dims)
            hedge = side[cells : cells + fin_rows, 0:LANES]
            inner_blocks(lambda k: fin_second(first, rest, hedge, k))
            copy = fin_copy(rest, fin_new, sem.at[0], inner_depths, inner_rows)
            copy.start()
            neighbour_sums(fluid, others, sums, 1, dims, sum_pairs)
            copy.wait()

        def fin_copy(rest, fin_new, sem, depths, lines):
            return pltpu.make_async_copy(rest.at[depths, lines], fin_new.at[depths, lines], sem)

        inner_depths, inner_rows = pl.ds(8, depth - 16), pl.ds(PAD, fin_rows - 2 * PAD)
        rest, fluid3, sums, fin_new = pl.pallas_call(
            end_fin_kernel,
            out_shape=(fin_rest, fluid_pad, f32(pairs, rows, width), fin_rest),
            in_specs=[vmem] * 4,
            out_specs=(vmem, vmem, vmem, hbm),
            scratch_shapes=[other_buffer(sum_group), pltpu.SemaphoreType.DMA((1,))],
            input_output_aliases={0: 0, 1: 1},
            compiler_params=params,
            name="end_fin",
        )(rest, fluid2, first, side)

        def end_kernel(_0, _1, _2, _3, act, ghost, gxa, gxb, paira, pairb, side, sums,
                       fluid, first, rest, fluid_new, fin_new,
                       zrows, zedge, fluid_sems, fin_sems):
            place = my_place()

            def fluid_copy(k):
                return pltpu.make_async_copy(
                    fluid.at[pl.ds(2 * k + 1, 2), pl.ds(PAD, rows), :],
                    fluid_new.at[pl.ds(2 * k, 2)], fluid_sems.at[k],
                )

            even, inside = sides_of(place[1], count)
            row_a = jnp.where(even, fin_rows - 1, 0)
            row_b = fin_rows - 1 - row_a
            scale = OMEGA * FIN_CONDUCTION / DIAG
            add_gx_rows(rest, 0, (row_a, row_b), (gxa, gxb), half, (scale, scale * inside), depth)
            whole = pl.ds(0, fin_rows)
            parts = ((inner_depths, pl.ds(0, PAD)), (inner_depths, pl.ds(fin_rows - PAD, PAD)),
                     (pl.ds(0, 8), whole), (pl.ds(depth - 8, 8), whole))
            fin_copies = [
                fin_copy(rest, fin_new, fin_sems.at[k], *part) for k, part in enumerate(parts)
            ]
            for item in fin_copies[:2]:
                item.start()
            fin_depth_halos(first, paira, pairb)
            hedge = side[cells : cells + fin_rows, 0:LANES]
            for block, item in ((0, fin_copies[2]), (blocks - 1, fin_copies[3])):
                fin_second(first, rest, hedge, block)
                item.start()
            below, above = grp_halos(paira, pairb, place[0], groups)
            unpack_fluid(fluid, zrows, zedge, gxa, gxb, ghost, below, above, 1, place, count, dims)
            fluid_update(fluid, act, zedge, sums, 1, dims, all_pairs,
                         lambda k: fluid_copy(k).start())

            def finish(k, carry):
                fluid_copy(k).wait()
                return carry

            for item in fin_copies:
                item.wait()
            lax.fori_loop(0, pairs, finish, 0)

        results = pl.pallas_call(
            end_kernel,
            out_shape=(fluid_pad, fin_pad, f32(depth, fin_rows, fin_width),
                       f32(cells, rows, width), f32(depth, fin_rows, fin_width)),
            in_specs=[vmem] * 3 + [hbm] + [vmem] * 8,
            out_specs=(vmem, vmem, vmem, hbm, hbm),
            scratch_shapes=[zrows_buffer, zedge_buffer,
                            pltpu.SemaphoreType.DMA((pairs,)), pltpu.SemaphoreType.DMA((4,))],
            input_output_aliases={0: 0, 1: 1, 2: 2, 3: 4},
            compiler_params=params,
            name="end",
        )(fluid3, first, rest, fin_new, active, ghost, gxa, gxb, grpa, grpb, side, sums)
        return results[3], results[4]

    return jax.shard_map(local, mesh=mesh, in_specs=in_specs, out_specs=out_specs, check_vma=False)
```
